32 devices in a mesh: seq: 8 (over z, y), inner: 4 (over x, core).
Axes of the slice: x: 2, y: 2, z: 4, core: 2. Of those that a mesh axis runs over, the one named last changes fastest.
Arguments:
- queries: bfloat16 [8, 16, 16384], P('inner', None, 'seq'), may hold values from -24 to 24
- key_states: bfloat16 [8, 16, 16384], P('inner', None, 'seq'), may hold values from -24 to 24
- value_states: bfloat16 [128, 25, 16384], P('inner', None, 'seq'), may hold values from -48 to 48
- fractional: float32 [3, 16384], P(None, 'seq'), may hold values from 0 to 1
- block_counts: int32 [64], replicated, may hold values from 64 to 256
- neighbors: int32 [64, 3], P('seq'), may hold values from 0 to 63, as said below
- integer_wave_vectors: int32 [3, 2048], replicated, may hold values from -7 to 7, as said below
- charge_weight: bfloat16 [128, 16], P('inner'), may hold values from -0.5 to 0.5
Outputs:
- attention: bfloat16 [128, 25, 16384], P('inner', None, 'seq')
- potential: float32 [16, 16384], P(None, 'seq')
- forces: float32 [3, 16384], P(None, 'seq')
The draws below stay inside these ranges and needn't reach their ends.
Inputs may be any that keep to these rules, and one draw needn't show every extreme that they name: `neighbors`: row g lists 3 different blocks from g - 2 to g + 2 that lie in the grid, g itself among them. `integer_wave_vectors`: no column is all zeros.
All inputs are finite; a program needn't handle non-finite values.
Results may differ from the reference program's by a relative error of at most 0.006.
Values may be sent and summed in bfloat16 or wider, within the bound.
No kernel may reach another device: no remote copies, remote signals or barrier semaphores. Data moves between devices by JAX's collectives and lax.ppermute only.
A program may use at most 64 MiB of HBM per device.

```python
import math
import jax
import jax.numpy as jnp
from jax import lax

CH = 128
NH = 8
HD = 16
COMP = 25
NQ = 16
NK = 2048
KMAX = 7
BS = 256
NNB = 3
NBLK = 64
ATOMS = 16384


def query_key_pair(key):
    first_key, second_key = jax.random.split(jax.random.fold_in(key, 7), 2)
    query_draw = jnp.clip(jax.random.normal(first_key, (NH, HD, ATOMS), jnp.float32), -6.0, 6.0)
    key_draw = jnp.clip(jax.random.normal(second_key, (NH, HD, ATOMS), jnp.float32), -6.0, 6.0)
    return (query_draw, key_draw)


def draw_queries(key, part):
    return query_key_pair(key)[0].astype(jnp.bfloat16)


def draw_key_states(key, part):
    return query_key_pair(key)[1].astype(jnp.bfloat16)


def draw_neighbors(key, part):
    inner_key = jax.random.fold_in(key, 11)
    block_ids = jnp.arange(NBLK)
    offsets = jnp.arange(5) - 2
    candidates = block_ids[:, None] + offsets[None, :]
    inside = (candidates >= 0) & (candidates < NBLK)
    random_bits = jax.random.randint(inner_key, (NBLK, 5), 0, 1 << 20) * 8 + jnp.arange(5)[None, :]
    ranking = jnp.where(offsets[None, :] == 0, -1, jnp.where(inside, random_bits, (1 << 24) + random_bits))
    order = jnp.argsort(ranking, axis=1)
    chosen = jnp.take_along_axis(candidates, order[:, :NNB], axis=1)
    return chosen.astype(jnp.int32)


def draw_integer_wave_vectors(key, part):
    inner_key = jax.random.fold_in(key, 13)
    numbers = jax.random.randint(inner_key, (3, NK), -KMAX, KMAX + 1)
    all_zero = jnp.all(numbers == 0, axis=0)
    numbers = jnp.where((jnp.arange(3)[:, None] == 0) & all_zero[None, :], 1, numbers)
    return numbers.astype(jnp.int32)


def plant(values, rng, low, top_value):
    longest = values.shape.index(max(values.shape))
    spots = []
    for shift in (0, 1):
        where = [jax.random.randint(jax.random.fold_in(rng, axis), (), 0, length) for axis, length in enumerate(values.shape)]
        where[longest] = (where[longest] + shift) % values.shape[longest]
        spots.append(tuple(where))
    return values.at[spots[0]].set(low).at[spots[1]].set(top_value)


def steps_of(stream_key, extent, shards, smallest, largest):
    loudness, own = 1.0, jax.random.fold_in(stream_key, 6)
    for dim, blocks in shards:
        draws = jnp.exp(jax.random.uniform(jax.random.fold_in(own, dim), (blocks,), jnp.float32, smallest / len(shards), largest / len(shards)))
        loudness = loudness * jnp.repeat(draws, extent[dim] // blocks).reshape([-1 if axis == dim else 1 for axis in range(len(extent))])
    return loudness


def noise(rng, dims, spread, most, cuts=(), dtype=jnp.bfloat16):
    result = jax.random.normal(rng, dims, jnp.float32) * spread
    if len(cuts) > 0:
        result = steps_of(rng, dims, cuts, -0.22, 0.18) * result
    return jnp.clip(result, min=-most, max=most).astype(dtype)


def setup_inputs(seed: int = 0) -> dict:
    splits = jax.random.split(jax.random.key(seed), 9)
    return {
        "queries": draw_queries(jax.random.fold_in(splits[8], 71), 0),
        "key_states": draw_key_states(jax.random.fold_in(splits[8], 71), 0),
        "value_states": noise(splits[2], (CH, COMP, ATOMS), 8.0, 48.0, ((0, 4), (2, 8))),
        "fractional": jnp.clip(1.0 * jax.random.uniform(splits[3], (3, ATOMS), jnp.float32) ** steps_of(splits[3], (3, ATOMS), ((1, 8),), -0.2, 0.2), 0.0, 1.0),
        "block_counts": plant(jax.random.randint(splits[4], (NBLK,), BS // 4, BS + 1), jax.random.fold_in(splits[4], 1), BS // 4, BS).astype(jnp.int32),
        "neighbors": draw_neighbors(jax.random.fold_in(splits[8], 71), 0),
        "integer_wave_vectors": draw_integer_wave_vectors(jax.random.fold_in(splits[8], 71), 0),
        "charge_weight": noise(splits[7], (CH, NQ), CH ** -0.5, 0.5, ((0, 4),)),
    }


ewald_scale = 40.0
ewald_damp = 0.02

def attend_block(query_block, gathered, valid_keys, own_count, head_dim):
    key_part = gathered[:, :head_dim].astype(jnp.float32)
    value_part = gathered[:, head_dim:].astype(jnp.float32)
    scores = jnp.einsum('hdq,hdk->hqk', query_block.astype(jnp.float32), key_part) * head_dim ** (-0.5)
    scores = jnp.where(valid_keys[None, None, :], scores, -jnp.inf)
    row_max = lax.optimization_barrier(jnp.max(scores, axis=2, keepdims=True))
    weights = jnp.exp(scores - row_max)
    denominator = lax.optimization_barrier(jnp.sum(weights, axis=2))
    rounded = weights.astype(jnp.bfloat16).astype(jnp.float32)
    mixture = jnp.einsum('hck,hqk->hcq', value_part, rounded) / denominator[:, None, :]
    live_rows = jnp.arange(query_block.shape[2]) < own_count
    return jnp.where(live_rows[None, None, :], mixture, 0.0).astype(jnp.bfloat16)

def plane_wave_terms(reciprocal_vectors, atom_positions):
    phase_angles = 2.0 * math.pi * (reciprocal_vectors[0][:, None] * atom_positions[0][None, :] + reciprocal_vectors[1][:, None] * atom_positions[1][None, :] + reciprocal_vectors[2][:, None] * atom_positions[2][None, :])
    return (jnp.cos(phase_angles), jnp.sin(phase_angles))

def contract(atom_charges, wave_table):
    return lax.dot_general(atom_charges, wave_table, (((1,), (1,)), ((), ())), precision=lax.Precision.HIGHEST, preferred_element_type=jnp.float32)

def potential_field_values(atom_charges, cosine_phase_values, sine_phase_values, reciprocal_vectors, reciprocal_weight, structure_real, structure_imaginary):
    query_block_count = structure_real.shape[0]
    wave_vector_count = structure_real.shape[1]
    weighted_real_part = structure_real * reciprocal_weight[None, :]
    weighted_imaginary = structure_imaginary * reciprocal_weight[None, :]
    cosine_product = jnp.concatenate([weighted_real_part, -(weighted_imaginary[None] * reciprocal_vectors[:, None, :]).reshape(3 * query_block_count, wave_vector_count)], axis=0)
    sine_product = jnp.concatenate([weighted_imaginary, (weighted_real_part[None] * reciprocal_vectors[:, None, :]).reshape(3 * query_block_count, wave_vector_count)], axis=0)
    combined = jnp.dot(cosine_product, cosine_phase_values, precision=lax.Precision.HIGHEST, preferred_element_type=jnp.float32) + jnp.dot(sine_product, sine_phase_values, precision=lax.Precision.HIGHEST, preferred_element_type=jnp.float32)
    potential = combined[:query_block_count]
    gradient = combined[query_block_count:].reshape(3, query_block_count, -1)
    forces = lax.optimization_barrier(jnp.sum(atom_charges[None] * gradient, axis=1))
    return (potential, forces)

def reference(queries, key_states, value_states, fractional, block_counts, neighbors, integer_wave_vectors, charge_weight):
    head_chan = CH // NH
    row_width = HD + head_chan * COMP
    stacked = jnp.concatenate([key_states, value_states.reshape(NH, head_chan * COMP, ATOMS)], axis=1).reshape(NH, row_width, NBLK, BS)
    slot_ids = jnp.arange(BS)
    valid_all = slot_ids[None, :] < block_counts[:, None]
    query_blocks = queries.reshape(NH, HD, NBLK, BS).transpose(2, 0, 1, 3)

    def one_block(inputs):
        query_block, listed, own_count = inputs
        gathered = jnp.take(stacked, listed, axis=2).reshape(NH, row_width, NNB * BS)
        valid_keys = jnp.take(valid_all, listed, axis=0).reshape(NNB * BS)
        return attend_block(query_block, gathered, valid_keys, own_count, HD)
    blocks_out = lax.map(one_block, (query_blocks, neighbors, block_counts))
    attention = blocks_out.transpose(1, 2, 0, 3).reshape(CH, COMP, ATOMS)
    atom_charges = jnp.dot(charge_weight.T, attention[:, 0, :], preferred_element_type=jnp.float32)
    reciprocal_vectors = integer_wave_vectors.astype(jnp.float32)
    squared_norm = lax.optimization_barrier(jnp.sum(reciprocal_vectors * reciprocal_vectors, axis=0))
    reciprocal_weight = ewald_scale * jnp.exp(-ewald_damp * squared_norm) / squared_norm
    inv_root = 1.0 / math.sqrt(ATOMS)
    charge_blocks = atom_charges.reshape(NQ, NBLK, BS).transpose(1, 0, 2)
    coord_blocks = fractional.reshape(3, NBLK, BS).transpose(1, 0, 2)

    def add_block(running, inputs):
        block_atom_charges, block_atom_positions = inputs
        cosine_phase_values, sine_phase_values = plane_wave_terms(reciprocal_vectors, block_atom_positions)
        return ((running[0] + contract(block_atom_charges, cosine_phase_values) * inv_root, running[1] + contract(block_atom_charges, sine_phase_values) * inv_root), None)
    start = (jnp.zeros((NQ, NK), jnp.float32), jnp.zeros((NQ, NK), jnp.float32))
    (structure_real, structure_imaginary), _ = lax.scan(add_block, start, (charge_blocks, coord_blocks))

    def field_block(inputs):
        block_atom_charges, block_atom_positions = inputs
        cosine_phase_values, sine_phase_values = plane_wave_terms(reciprocal_vectors, block_atom_positions)
        return potential_field_values(block_atom_charges, cosine_phase_values, sine_phase_values, reciprocal_vectors, reciprocal_weight, structure_real, structure_imaginary)
    potential_blocks, force_blocks = lax.map(field_block, (charge_blocks, coord_blocks))
    potential = potential_blocks.transpose(1, 0, 2).reshape(NQ, ATOMS)
    forces = force_blocks.transpose(1, 0, 2).reshape(3, ATOMS)
    return (attention, potential, forces)
```

```python
import functools
import math

import jax
import jax.numpy as jnp
from jax import lax
from jax.experimental import pallas as pl
from jax.experimental.pallas import tpu as pltpu
from jax.sharding import PartitionSpec as P

BS = 256
NNB = 3
REACH = 2
PAD = 32

ewald_scale = 40.0
ewald_damp = 0.02

BF = jnp.bfloat16
F32 = jnp.float32

SIN = (6.283185302511499, -41.34170040531678, 81.60513138577247, -76.70301535353673,
       42.02592698394968, -14.899846662448152, 3.2381375038938693)
COS = (0.9999999890590217, -19.73920449945376, 64.93911745989128, -85.45013953083522,
       60.167630950695504, -25.967599247822193, 6.5286581606558824)


def params(mib, sides=False):
    return pltpu.CompilerParams(vmem_limit_bytes=mib << 20, dimension_semantics=("arbitrary",))


def dot(a, b, dims):
    return lax.dot_general(a, b, (dims, ((), ())), preferred_element_type=F32)


def horner(coeffs, u):
    total = coeffs[-1]
    for c in coeffs[-2::-1]:
        total = total * u + c
    return total


def halves(x):
    high = x.astype(BF)
    return high, (x - high.astype(F32)).astype(BF)


def score_kernel(
    heads, head_dim, head_chan, blocks,
    lists, counts, place, q_ref, own_ref, left_ref, right_ref, cw_ref,
    p_ref, scale_ref, charge_ref, kaug, v0,
):
    g = pl.program_id(0)
    first = place[0] * blocks
    chans = heads * head_chan
    total = counts.shape[0]

    @pl.when(g == 0)
    def _():
        lane = lax.broadcasted_iota(jnp.int32, (16, BS), 1)
        row = lax.broadcasted_iota(jnp.int32, (16, BS), 0)
        for b in range(blocks + 2 * REACH):
            index = first + b - REACH
            inside = (index >= 0) & (index < total)
            live = jnp.where(inside, counts[jnp.clip(index, 0, total - 1)], 0)
            if b < REACH:
                src = left_ref[:, b * BS : (b + 1) * BS]
            elif b < REACH + blocks:
                src = own_ref[:, (b - REACH) * BS : (b - REACH + 1) * BS]
            else:
                src = right_ref[:, (b - REACH - blocks) * BS : (b - REACH - blocks + 1) * BS]
            bias = jnp.where((row == 0) & (lane >= live), -1e30, 0.0).astype(BF)
            for h in range(heads):
                kaug[b, h, 0:head_dim, :] = src[h * head_dim : (h + 1) * head_dim]
                kaug[b, h, head_dim : head_dim + 16, :] = bias
            v0[b] = src[heads * head_dim : heads * head_dim + chans]

    own_count = counts[first + g]
    live_q = lax.broadcasted_iota(jnp.int32, (1, BS), 1) < own_count
    ones = jnp.where(lax.broadcasted_iota(jnp.int32, (16, BS), 0) == 0, 1.0, 0.0).astype(BF)
    charge = None
    for h in range(heads):
        q = (q_ref[h * head_dim : (h + 1) * head_dim, :].astype(F32) * head_dim ** (-0.5)).astype(BF)
        qa = jnp.concatenate([q, ones], axis=0)
        listed = [lists[g, e] - (first - REACH) for e in range(NNB)]
        scores = [dot(kaug[b, h], qa, ((0,), (0,))) for b in listed]
        top = functools.reduce(jnp.maximum, [jnp.max(s, axis=0, keepdims=True) for s in scores])
        denominator = 0.0
        mixed = 0.0
        for e, b in enumerate(listed):
            w = jnp.exp(scores[e] - top)
            denominator = denominator + jnp.sum(w, axis=0, keepdims=True)
            w16 = w.astype(BF)
            p_ref[0, h, e * BS : (e + 1) * BS, :] = w16
            mixed = mixed + dot(v0[b, h * head_chan : (h + 1) * head_chan, :], w16, ((1,), (0,)))
        scale = jnp.where(live_q, 1.0 / denominator, 0.0)
        scale_ref[0, h : h + 1, :] = scale
        att0 = (mixed * scale).astype(BF)
        part = dot(cw_ref[h * head_chan : (h + 1) * head_chan, :], att0, ((0,), (0,)))
        charge = part if charge is None else charge + part
    charge_ref[...] = charge


def scores_call(lists, counts, place, q, own, left, right, cw, heads, head_dim, head_chan, blocks):
    rows = own.shape[0]
    nq = cw.shape[1]
    atoms = q.shape[1]
    band = blocks + 2 * REACH
    whole = lambda shape: pl.BlockSpec(shape, lambda g, *_: (0,) * len(shape))
    return pl.pallas_call(
        functools.partial(score_kernel, heads, head_dim, head_chan, blocks),
        grid_spec=pltpu.PrefetchScalarGridSpec(
            num_scalar_prefetch=3,
            grid=(blocks,),
            in_specs=[
                pl.BlockSpec((heads * head_dim, BS), lambda g, *_: (0, g)),
                whole(own.shape),
                whole(left.shape),
                whole(right.shape),
                whole(cw.shape),
            ],
            out_specs=[
                pl.BlockSpec((1, heads, NNB * BS, BS), lambda g, *_: (g, 0, 0, 0)),
                pl.BlockSpec((1, heads, BS), lambda g, *_: (g, 0, 0)),
                pl.BlockSpec((nq, BS), lambda g, *_: (0, g)),
            ],
            scratch_shapes=[
                pltpu.VMEM((band, heads, head_dim + 16, BS), BF),
                pltpu.VMEM((band, heads * head_chan, BS), BF),
            ],
        ),
        out_shape=[
            jax.ShapeDtypeStruct((blocks, heads, NNB * BS, BS), BF),
            jax.ShapeDtypeStruct((blocks, heads, BS), F32),
            jax.ShapeDtypeStruct((nq, atoms), F32),
        ],
        compiler_params=params(16),
        cost_estimate=pl.CostEstimate(
            flops=blocks * heads * NNB * BS * BS * 200, transcendentals=blocks * heads * NNB * BS * BS,
            bytes_accessed=blocks * heads * NNB * BS * BS * 2,
        ),
        name="scores",
    )(lists, counts, place, q, own, left, right, cw)


def inner_kernel(heads, head_chan, comps, lists, place, *refs):
    values, (p_ref, scale_ref, out_ref) = refs[:NNB], refs[NNB:]
    for h in range(heads):
        chans = slice(h * head_chan, (h + 1) * head_chan)
        acc = 0.0
        for e in range(NNB):
            v = values[e][chans].reshape(head_chan * PAD, BS)
            acc = acc + dot(v, p_ref[0, h, e * BS : (e + 1) * BS, :], ((1,), (0,)))
        acc = acc * scale_ref[0, h : h + 1, :]
        out_ref[chans] = acc.astype(BF).reshape(head_chan, PAD, BS)


def inner_call(lists, place, v, p, scale, heads, blocks):
    chans, comps, atoms = v.shape
    steps = blocks - 2 * REACH

    def value_map(e):
        return lambda i, lists, place: (0, 0, lists[i + REACH, e] - place[0] * blocks)

    return pl.pallas_call(
        functools.partial(inner_kernel, heads, chans // heads, comps),
        grid_spec=pltpu.PrefetchScalarGridSpec(
            num_scalar_prefetch=2,
            grid=(steps,),
            in_specs=[pl.BlockSpec((chans, PAD, BS), value_map(e)) for e in range(NNB)]
            + [
                pl.BlockSpec((1, heads, NNB * BS, BS), lambda i, *_: (i + REACH, 0, 0, 0)),
                pl.BlockSpec((1, heads, BS), lambda i, *_: (i + REACH, 0, 0)),
            ],
            out_specs=pl.BlockSpec((chans, PAD, BS), lambda i, *_: (0, 0, i + REACH)),
        ),
        out_shape=jax.ShapeDtypeStruct(v.shape, BF),
        compiler_params=params(24),
        cost_estimate=pl.CostEstimate(
            flops=steps * chans * PAD * NNB * BS * BS * 2, transcendentals=0,
            bytes_accessed=steps * chans * PAD * BS * 8,
        ),
        name="inner",
    )(lists, place, v, v, v, p, scale)


def edge_block(i, blocks):
    return jnp.where(i < REACH, i, i + blocks - 2 * REACH)


def edge_kernel(
    heads, head_chan, comps, blocks, row0,
    lists, place, own_ref, left_ref, right_ref, lsmall_ref, rsmall_ref, p_ref, scale_ref, prev_ref, out_ref, vb,
):
    i = pl.program_id(0)
    chans = heads * head_chan
    most = left_ref.shape[1]

    @pl.when(i == 0)
    def _():
        for b in range(blocks):
            vb[REACH + b] = own_ref[:, :, b * BS : (b + 1) * BS]
        for big, small, base in ((left_ref, lsmall_ref, 0), (right_ref, rsmall_ref, REACH + blocks)):
            for b in range(REACH):
                cols = slice(b * BS, (b + 1) * BS)
                vb[base + b, :, 0:most, :] = big[:, :, cols]
                tail = small[row0 : row0 + chans, cols].astype(F32)
                vb[base + b, :, most:PAD, :] = jnp.broadcast_to(
                    tail[:, None, :], (chans, PAD - most, BS)
                ).astype(BF)

    g = edge_block(i, blocks)
    offset = place[0] * blocks - REACH
    for h in range(heads):
        rows = slice(h * head_chan, (h + 1) * head_chan)
        acc = 0.0
        for e in range(NNB):
            v = vb[lists[g, e] - offset, rows].reshape(head_chan * PAD, BS)
            acc = acc + dot(v, p_ref[0, h, e * BS : (e + 1) * BS, :], ((1,), (0,)))
        acc = acc * scale_ref[0, h : h + 1, :]
        out_ref[rows] = acc.astype(BF).reshape(head_chan, PAD, BS)


def edge_call(lists, place, v, left, right, lsmall, rsmall, p, scale, prev, heads, head_dim, blocks):
    chans, comps, atoms = v.shape
    whole = lambda shape: pl.BlockSpec(shape, lambda g, *_: (0,) * len(shape), pipeline_mode=pl.Buffered(1))
    row0 = heads * head_dim + chans
    return pl.pallas_call(
        functools.partial(edge_kernel, heads, chans // heads, comps, blocks, row0),
        grid_spec=pltpu.PrefetchScalarGridSpec(
            num_scalar_prefetch=2,
            grid=(2 * REACH,),
            in_specs=[
                whole((chans, PAD, atoms)),
                whole(left.shape),
                whole(right.shape),
                whole(lsmall.shape),
                whole(rsmall.shape),
                pl.BlockSpec((1, heads, NNB * BS, BS), lambda i, *_: (edge_block(i, blocks), 0, 0, 0)),
                pl.BlockSpec((1, heads, BS), lambda i, *_: (edge_block(i, blocks), 0, 0)),
                pl.BlockSpec(memory_space=pl.ANY),
            ],
            out_specs=pl.BlockSpec((chans, PAD, BS), lambda i, *_: (0, 0, edge_block(i, blocks))),
            scratch_shapes=[pltpu.VMEM((blocks + 2 * REACH, chans, PAD, BS), BF)],
        ),
        out_shape=jax.ShapeDtypeStruct(v.shape, BF),
        input_output_aliases={9: 0},
        compiler_params=params(36),
        cost_estimate=pl.CostEstimate(
            flops=2 * REACH * chans * PAD * NNB * BS * BS * 2, transcendentals=0,
            bytes_accessed=2 * REACH * chans * PAD * BS * 8,
        ),
        name="edges",
    )(lists, place, v, left, right, lsmall, rsmall, p, scale, prev)


def table_kernel(place, n_ref, f_ref, out_ref, parts):
    @pl.when(pl.program_id(0) == 0)
    def _():
        f = f_ref[...]
        high, low = halves(f)
        rest = ((f - high.astype(F32)) - low.astype(F32)).astype(BF)
        parts[...] = jnp.concatenate([high, low, rest], axis=0)

    n = n_ref[...].astype(F32).astype(BF)
    turns = dot(jnp.concatenate([n, n, n], axis=0), parts[...], ((0,), (0,)))
    r = turns - jnp.round(turns)
    u = r * r
    out_ref[0] = horner(COS, u).astype(BF)
    out_ref[1] = (horner(SIN, u) * r).astype(BF)


def table_call(place, n, f, waves):
    step = 128
    atoms = f.shape[1]
    return pl.pallas_call(
        table_kernel,
        grid_spec=pltpu.PrefetchScalarGridSpec(
            num_scalar_prefetch=1,
            grid=(waves // step,),
            in_specs=[
                pl.BlockSpec((3, step), lambda i, place: (0, place[1] * (waves // step) + i)),
                pl.BlockSpec(f.shape, lambda i, place: (0, 0)),
            ],
            out_specs=pl.BlockSpec((2, step, atoms), lambda i, place: (0, i, 0)),
            scratch_shapes=[pltpu.VMEM((9, atoms), BF)],
        ),
        out_shape=jax.ShapeDtypeStruct((2, waves, atoms), BF),
        compiler_params=params(16),
        cost_estimate=pl.CostEstimate(
            flops=waves * atoms * 400, transcendentals=0, bytes_accessed=waves * atoms * 4
        ),
        name="table",
    )(place, n, f)


def structure_kernel(inv_root, c_ref, t_ref, out_ref):
    high, low = halves(c_ref[...])
    both = jnp.concatenate([high, low], axis=0)
    s = dot(t_ref[...], both, ((1,), (1,)))
    nq = c_ref.shape[0]
    out_ref[...] = (s[:, :nq] + s[:, nq:]).T * inv_root


def structure_call(c, table, inv_root):
    rows, atoms = table.shape
    step = min(256, rows)
    nq = c.shape[0]
    return pl.pallas_call(
        functools.partial(structure_kernel, inv_root),
        grid=(rows // step,),
        in_specs=[pl.BlockSpec((nq, atoms), lambda i: (0, 0)), pl.BlockSpec((step, atoms), lambda i: (i, 0))],
        out_specs=pl.BlockSpec((nq, step), lambda i: (0, i)),
        out_shape=jax.ShapeDtypeStruct((nq, rows), F32),
        compiler_params=params(12),
        cost_estimate=pl.CostEstimate(flops=rows * atoms * 512, transcendentals=0, bytes_accessed=rows * atoms * 2),
        name="structure",
    )(c, table)


def field_kernel(place, s_ref, n_ref, c_ref, t_ref, out_ref, coeff):
    nq = c_ref.shape[0]
    waves = n_ref.shape[1]

    @pl.when(pl.program_id(0) == 0)
    def _():
        n = n_ref[...].astype(F32)
        norm = n[0:1] * n[0:1] + n[1:2] * n[1:2] + n[2:3] * n[2:3]
        weight = ewald_scale * jnp.exp(-ewald_damp * norm) / norm
        real = s_ref[:, :waves] * weight
        imag = s_ref[:, waves:] * weight
        with_cos = jnp.concatenate([real] + [-imag * n[d : d + 1] for d in range(3)], axis=0)
        with_sin = jnp.concatenate([imag] + [real * n[d : d + 1] for d in range(3)], axis=0)
        for part, x in enumerate((with_cos, with_sin)):
            high, low = halves(x)
            cols = slice(part * waves, (part + 1) * waves)
            coeff[0 : 4 * nq, cols] = high
            coeff[4 * nq :, cols] = low

    both = dot(coeff[...], t_ref[...], ((1,), (0,)))
    sums = both[: 4 * nq] + both[4 * nq :]
    c = c_ref[...]
    out_ref[0:nq, :] = sums[:nq]
    forces = [
        jnp.sum(c * sums[(d + 1) * nq : (d + 2) * nq], axis=0, keepdims=True) for d in range(3)
    ]
    out_ref[nq : nq + 8, :] = jnp.concatenate(forces + [jnp.zeros((5, c.shape[1]), F32)], axis=0)


def field_call(place, s, n, c, table, waves):
    rows, atoms = table.shape
    step = 512
    nq = c.shape[0]
    return pl.pallas_call(
        field_kernel,
        grid_spec=pltpu.PrefetchScalarGridSpec(
            num_scalar_prefetch=1,
            grid=(atoms // step,),
            in_specs=[
                pl.BlockSpec((nq, rows), lambda i, place: (0, 0)),
                pl.BlockSpec((3, waves), lambda i, place: (0, place[1])),
                pl.BlockSpec((nq, step), lambda i, place: (0, i)),
                pl.BlockSpec((rows, step), lambda i, place: (0, i)),
            ],
            out_specs=pl.BlockSpec((nq + 8, step), lambda i, place: (0, i)),
            scratch_shapes=[pltpu.VMEM((8 * nq, rows), BF)],
        ),
        out_shape=jax.ShapeDtypeStruct((nq + 8, atoms), F32),
        compiler_params=params(12),
        cost_estimate=pl.CostEstimate(flops=rows * atoms * 512, transcendentals=0, bytes_accessed=rows * atoms * 2),
        name="fields",
    )(place, s, n, c, table)


def summed(x, axis):
    size = lax.axis_size(axis)
    if size & (size - 1):
        return lax.psum(x, axis)
    step = 1
    while step < size:
        x = x + lax.ppermute(x, axis, [(i, i ^ step) for i in range(size)])
        step *= 2
    return x


def local(
    queries,
    key_states,
    value_states,
    fractional,
    block_counts,
    neighbors,
    integer_wave_vectors,
    charge_weight,
):
    heads, head_dim, atoms = queries.shape
    chans, comps, _ = value_states.shape
    blocks = atoms // BS
    nq = charge_weight.shape[1]
    waves = integer_wave_vectors.shape[1] // lax.axis_size("inner")
    inv_root = 1.0 / math.sqrt(atoms * lax.axis_size("seq"))
    place = jnp.stack([lax.axis_index("seq"), lax.axis_index("inner")]).astype(jnp.int32)
    width = REACH * BS
    count = lax.axis_size("seq")
    up = [(i, i + 1) for i in range(count - 1)]
    down = [(i + 1, i) for i in range(count - 1)]

    small = jnp.concatenate(
        [
            key_states.reshape(heads * head_dim, atoms),
            value_states[:, 0, :],
            value_states[:, comps - 1, :],
        ],
        axis=0,
    )
    small_left = lax.ppermute(small[:, atoms - width :], "seq", up)
    small_right = lax.ppermute(small[:, :width], "seq", down)
    most = comps - 1
    big_left = lax.ppermute(value_states[:, :most, atoms - width :], "seq", up)
    big_right = lax.ppermute(value_states[:, :most, :width], "seq", down)

    table = table_call(place, integer_wave_vectors, fractional, waves).reshape(2 * waves, atoms)
    weights, scale, part = scores_call(
        neighbors, block_counts, place, queries.reshape(heads * head_dim, atoms),
        small, small_left, small_right, charge_weight, heads, head_dim, chans // heads, blocks,
    )
    charges = summed(part, "inner")
    structure = summed(structure_call(charges, table, inv_root), "seq")
    fields = summed(field_call(place, structure, integer_wave_vectors, charges, table, waves), "inner")

    attention = inner_call(neighbors, place, value_states, weights, scale, heads, blocks)
    attention = edge_call(
        neighbors, place, value_states, big_left, big_right, small_left, small_right,
        weights, scale, attention, heads, head_dim, blocks,
    )
    return (attention, fields[:nq], fields[nq : nq + 3])


def solution(mesh):
    placed = (
        P("inner", None, "seq"),
        P("inner", None, "seq"),
        P("inner", None, "seq"),
        P(None, "seq"),
        P(),
        P("seq", None),
        P(),
        P("inner", None),
    )
    return jax.shard_map(
        local,
        mesh=mesh,
        in_specs=placed,
        out_specs=(P("inner", None, "seq"), P(None, "seq"), P(None, "seq")),
        check_vma=False,
    )
```

```python
import functools
import math

import jax
import jax.numpy as jnp
from jax import lax
from jax.experimental import pallas as pl
from jax.experimental.pallas import tpu as pltpu
from jax.sharding import PartitionSpec as P


BS = 256
NNB = 3
REACH = 2

ewald_scale = 40.0
ewald_damp = 0.02

BF = jnp.bfloat16
F32 = jnp.float32

SIN = (6.283185302511499, -41.34170040531678, 81.60513138577247, -76.70301535353673,
       42.02592698394968, -14.899846662448152, 3.2381375038938693)
COS = (0.9999999890590217, -19.73920449945376, 64.93911745989128, -85.45013953083522,
       60.167630950695504, -25.967599247822193, 6.5286581606558824)


def params(mib):
    return pltpu.CompilerParams(vmem_limit_bytes=mib << 20, dimension_semantics=("arbitrary",))


def dot(a, b, dims):
    return lax.dot_general(a, b, (dims, ((), ())), preferred_element_type=F32)


def horner(coeffs, u):
    total = coeffs[-1]
    for c in coeffs[-2::-1]:
        total = total * u + c
    return total


def halves(x):
    high = x.astype(BF)
    return high, (x - high.astype(F32)).astype(BF)


def span(part, blocks):
    if part == "interior":
        return blocks - 2 * REACH, lambda i: i + REACH
    return 2 * REACH, lambda i: jnp.where(i < REACH, i, i + blocks - 2 * REACH)


def score_kernel(heads, head_dim, head_chan, blocks, part, lists, counts, place, *refs):
    q_ref, k_ref, v_ref, cw_ref = refs[:4]
    sides, (p_ref, scale_ref, charge_ref, kaug, v0) = refs[4:-5], refs[-5:]
    i = pl.program_id(0)
    first = place[0] * blocks
    total = counts.shape[0]

    @pl.when(i == 0)
    def _():
        lane = lax.broadcasted_iota(jnp.int32, (16, BS), 1)
        row = lax.broadcasted_iota(jnp.int32, (16, BS), 0)
        for b in range(blocks + 2 * REACH):
            own = REACH <= b < REACH + blocks
            if not own and part == "interior":
                continue
            index = first + b - REACH
            inside = (index >= 0) & (index < total)
            live = jnp.where(inside, counts[jnp.clip(index, 0, total - 1)], 0)
            if own:
                cols = slice((b - REACH) * BS, (b - REACH + 1) * BS)
                keys, v0[b] = k_ref[:, cols], v_ref[0, :, cols]
            else:
                side = sides[0] if b < REACH else sides[1]
                at = b if b < REACH else b - REACH - blocks
                cols = slice(at * BS, (at + 1) * BS)
                keys, v0[b] = side[0 : heads * head_dim, cols], side[heads * head_dim :, cols]
            bias = jnp.where((row == 0) & (lane >= live), -1e30, 0.0).astype(BF)
            for h in range(heads):
                kaug[b, h, 0:head_dim, :] = keys[h * head_dim : (h + 1) * head_dim]
                kaug[b, h, head_dim : head_dim + 16, :] = bias

    g = span(part, blocks)[1](i)
    own_count = counts[first + g]
    live_q = lax.broadcasted_iota(jnp.int32, (1, BS), 1) < own_count
    ones = jnp.where(lax.broadcasted_iota(jnp.int32, (16, BS), 0) == 0, 1.0, 0.0).astype(BF)
    listed = [lists[e, g] - (first - REACH) for e in range(NNB)]
    charge = None
    for h in range(heads):
        q = (q_ref[h * head_dim : (h + 1) * head_dim, :].astype(F32) * head_dim ** (-0.5)).astype(BF)
        qa = jnp.concatenate([q, ones], axis=0)
        scores = [dot(kaug[b, h], qa, ((0,), (0,))) for b in listed]
        top = functools.reduce(jnp.maximum, [jnp.max(s, axis=0, keepdims=True) for s in scores])
        denominator = 0.0
        mixed = 0.0
        for e, b in enumerate(listed):
            w = jnp.exp(scores[e] - top)
            denominator = denominator + jnp.sum(w, axis=0, keepdims=True)
            w16 = w.astype(BF)
            p_ref[0, h, e * BS : (e + 1) * BS, :] = w16
            mixed = mixed + dot(v0[b, h * head_chan : (h + 1) * head_chan, :], w16, ((1,), (0,)))
        scale = jnp.where(live_q, 1.0 / denominator, 0.0)
        scale_ref[0, h : h + 1, :] = scale
        att0 = (mixed * scale).astype(BF)
        term = dot(cw_ref[:, h * head_chan : (h + 1) * head_chan], att0, ((1,), (0,)))
        charge = term if charge is None else charge + term
    charge_ref[0] = charge


def scores_call(part, lists, counts, place, q, k, v, cw, sides, heads, head_dim):
    _, chans, atoms = v.shape
    blocks = atoms // BS
    nq = cw.shape[0]
    head_chan = chans // heads
    band = blocks + 2 * REACH
    steps, at = span(part, blocks)
    whole = lambda shape: pl.BlockSpec(shape, lambda g, *_: (0,) * len(shape))
    return pl.pallas_call(
        functools.partial(score_kernel, heads, head_dim, head_chan, blocks, part),
        grid_spec=pltpu.PrefetchScalarGridSpec(
            num_scalar_prefetch=3,
            grid=(steps,),
            in_specs=[
                pl.BlockSpec((heads * head_dim, BS), lambda i, *_: (0, at(i))),
                whole(k.shape),
                whole((1, chans, atoms)),
                whole(cw.shape),
            ]
            + [whole(s.shape) for s in sides],
            out_specs=[
                pl.BlockSpec((1, heads, NNB * BS, BS), lambda i, *_: (i, 0, 0, 0)),
                pl.BlockSpec((1, heads, BS), lambda i, *_: (i, 0, 0)),
                pl.BlockSpec((1, nq, BS), lambda i, *_: (i, 0, 0)),
            ],
            scratch_shapes=[
                pltpu.VMEM((band, heads, head_dim + 16, BS), BF),
                pltpu.VMEM((band, chans, BS), BF),
            ],
        ),
        out_shape=[
            jax.ShapeDtypeStruct((steps, heads, NNB * BS, BS), BF),
            jax.ShapeDtypeStruct((steps, heads, BS), F32),
            jax.ShapeDtypeStruct((steps, nq, BS), F32),
        ],
        compiler_params=params(12),
        cost_estimate=pl.CostEstimate(
            flops=steps * heads * NNB * BS * BS * 200, transcendentals=steps * heads * NNB * BS * BS,
            bytes_accessed=steps * heads * NNB * BS * BS * 2,
        ),
    )(lists, counts, place, q, k, v, cw, *sides)


def mix(heads, head_chan, listed, band_ref, p_ref, scale_ref, out_ref):
    comps = band_ref.shape[1]
    for h in range(heads):
        rows = slice(h * head_chan, (h + 1) * head_chan)
        acc = 0.0
        for e in range(NNB):
            v = band_ref[listed[e], :, rows, :].reshape(comps * head_chan, BS)
            acc = acc + dot(v, p_ref[0, h, e * BS : (e + 1) * BS, :], ((1,), (0,)))
        acc = acc * scale_ref[0, h : h + 1, :]
        out_ref[:, rows, :] = acc.astype(BF).reshape(comps, head_chan, BS)


def interior_kernel(heads, head_chan, blocks, lists, place, v_ref, p_ref, scale_ref, out_ref, band_ref):
    i = pl.program_id(0)

    @pl.when(i == 0)
    def _():
        for b in range(blocks):
            band_ref[REACH + b] = v_ref[:, :, b * BS : (b + 1) * BS]

    g = span("interior", blocks)[1](i)
    listed = [lists[e, g] - (place[0] * blocks - REACH) for e in range(NNB)]
    mix(heads, head_chan, listed, band_ref, p_ref, scale_ref, out_ref)


def interior_call(lists, place, v, p, scale, heads):
    comps, chans, atoms = v.shape
    blocks = atoms // BS
    steps, at = span("interior", blocks)
    band = (blocks + 2 * REACH, comps, chans, BS)
    return pl.pallas_call(
        functools.partial(interior_kernel, heads, chans // heads, blocks),
        grid_spec=pltpu.PrefetchScalarGridSpec(
            num_scalar_prefetch=2,
            grid=(steps,),
            in_specs=[
                pl.BlockSpec(v.shape, lambda i, *_: (0, 0, 0), pipeline_mode=pl.Buffered(1)),
                pl.BlockSpec((1, heads, NNB * BS, BS), lambda i, *_: (i, 0, 0, 0)),
                pl.BlockSpec((1, heads, BS), lambda i, *_: (i, 0, 0)),
            ],
            out_specs=[
                pl.BlockSpec((comps, chans, BS), lambda i, *_: (0, 0, at(i))),
                pl.BlockSpec(band, lambda i, *_: (0, 0, 0, 0), pipeline_mode=pl.Buffered(1)),
            ],
        ),
        out_shape=[jax.ShapeDtypeStruct(v.shape, BF), jax.ShapeDtypeStruct(band, BF)],
        compiler_params=params(20),
        cost_estimate=pl.CostEstimate(
            flops=steps * chans * comps * NNB * BS * BS * 2, transcendentals=0,
            bytes_accessed=steps * chans * comps * BS * 8,
        ),
        name="interior",
    )(lists, place, v, p, scale)


def edge_kernel(
    heads, head_dim, head_chan, blocks, lists, place, band_in, prev, p_ref, scale_ref, lsmall, rsmall, *refs
):
    halo, (out_ref, band_ref) = refs[:-2], refs[-2:]
    i = pl.program_id(0)

    @pl.when(i == 0)
    def _():
        for b in range(blocks):
            band_ref[REACH + b] = band_in[REACH + b]
        for side, (small, base) in enumerate(((lsmall, 0), (rsmall, REACH + blocks))):
            for b in range(REACH):
                cols = slice(b * BS, (b + 1) * BS)
                band_ref[base + b, 0] = small[heads * head_dim :, cols]
                at = 1
                for piece in halo[side::2]:
                    band_ref[base + b, at : at + piece.shape[0]] = piece[:, :, cols]
                    at += piece.shape[0]

    g = span("edges", blocks)[1](i)
    listed = [lists[e, g] - (place[0] * blocks - REACH) for e in range(NNB)]
    mix(heads, head_chan, listed, band_ref, p_ref, scale_ref, out_ref)


def edge_call(lists, place, v_shape, band, prev, p, scale, lsmall, rsmall, halo, heads, head_dim):
    comps, chans, atoms = v_shape
    blocks = atoms // BS
    steps, at = span("edges", blocks)
    whole = lambda shape: pl.BlockSpec(shape, lambda g, *_: (0,) * len(shape), pipeline_mode=pl.Buffered(1))
    return pl.pallas_call(
        functools.partial(edge_kernel, heads, head_dim, chans // heads, blocks),
        grid_spec=pltpu.PrefetchScalarGridSpec(
            num_scalar_prefetch=2,
            grid=(steps,),
            in_specs=[
                whole(band.shape),
                pl.BlockSpec(memory_space=pl.ANY),
                pl.BlockSpec((1, heads, NNB * BS, BS), lambda i, *_: (i, 0, 0, 0)),
                pl.BlockSpec((1, heads, BS), lambda i, *_: (i, 0, 0)),
                whole(lsmall.shape),
                whole(rsmall.shape),
            ]
            + [whole(x.shape) for x in halo],
            out_specs=pl.BlockSpec((comps, chans, BS), lambda i, *_: (0, 0, at(i))),
            scratch_shapes=[pltpu.VMEM(band.shape, BF)],
        ),
        out_shape=jax.ShapeDtypeStruct(v_shape, BF),
        input_output_aliases={3: 0},
        compiler_params=params(24),
        cost_estimate=pl.CostEstimate(
            flops=steps * chans * comps * NNB * BS * BS * 2, transcendentals=0,
            bytes_accessed=steps * chans * comps * BS * 8,
        ),
        name="edges",
    )(lists, place, band, prev, p, scale, lsmall, rsmall, *halo)


def table_kernel(place, n_ref, f_ref, out_ref, parts):
    @pl.when(pl.program_id(0) == 0)
    def _():
        f = f_ref[...]
        high, low = halves(f)
        rest = ((f - high.astype(F32)) - low.astype(F32)).astype(BF)
        parts[...] = jnp.concatenate([high, low, rest], axis=0)

    n = n_ref[...].astype(F32).astype(BF)
    turns = dot(jnp.concatenate([n, n, n], axis=0), parts[...], ((0,), (0,)))
    r = turns - jnp.round(turns)
    u = r * r
    out_ref[0] = horner(COS, u).astype(BF)
    out_ref[1] = (horner(SIN, u) * r).astype(BF)


def table_call(place, n, f, waves):
    step = 128
    atoms = f.shape[1]
    return pl.pallas_call(
        table_kernel,
        grid_spec=pltpu.PrefetchScalarGridSpec(
            num_scalar_prefetch=1,
            grid=(waves // step,),
            in_specs=[
                pl.BlockSpec((3, step), lambda i, place: (0, place[1] * (waves // step) + i)),
                pl.BlockSpec(f.shape, lambda i, place: (0, 0)),
            ],
            out_specs=pl.BlockSpec((2, step, atoms), lambda i, place: (0, i, 0)),
            scratch_shapes=[pltpu.VMEM((9, atoms), BF)],
        ),
        out_shape=jax.ShapeDtypeStruct((2, waves, atoms), BF),
        compiler_params=params(16),
        cost_estimate=pl.CostEstimate(
            flops=waves * atoms * 400, transcendentals=0, bytes_accessed=waves * atoms * 4
        ),
        name="table",
    )(place, n, f)


def structure_kernel(inv_root, c_ref, t_ref, out_ref):
    high, low = halves(c_ref[...])
    both = jnp.concatenate([high, low], axis=0)
    s = dot(t_ref[...], both, ((1,), (1,)))
    nq = c_ref.shape[0]
    out_ref[...] = (s[:, :nq] + s[:, nq:]).T * inv_root


def structure_call(c, table, inv_root):
    rows, atoms = table.shape
    step = min(256, rows)
    nq = c.shape[0]
    return pl.pallas_call(
        functools.partial(structure_kernel, inv_root),
        grid=(rows // step,),
        in_specs=[pl.BlockSpec((nq, atoms), lambda i: (0, 0)), pl.BlockSpec((step, atoms), lambda i: (i, 0))],
        out_specs=pl.BlockSpec((nq, step), lambda i: (0, i)),
        out_shape=jax.ShapeDtypeStruct((nq, rows), F32),
        compiler_params=params(12),
        cost_estimate=pl.CostEstimate(flops=rows * atoms * 512, transcendentals=0, bytes_accessed=rows * atoms * 2),
        name="structure",
    )(c, table)


def field_kernel(place, s_ref, n_ref, c_ref, t_ref, out_ref, coeff):
    nq = c_ref.shape[0]
    waves = n_ref.shape[1]

    @pl.when(pl.program_id(0) == 0)
    def _():
        n = n_ref[...].astype(F32)
        norm = n[0:1] * n[0:1] + n[1:2] * n[1:2] + n[2:3] * n[2:3]
        weight = ewald_scale * jnp.exp(-ewald_damp * norm) / norm
        real = s_ref[:, :waves] * weight
        imag = s_ref[:, waves:] * weight
        with_cos = jnp.concatenate([real] + [-imag * n[d : d + 1] for d in range(3)], axis=0)
        with_sin = jnp.concatenate([imag] + [real * n[d : d + 1] for d in range(3)], axis=0)
        for part, x in enumerate((with_cos, with_sin)):
            high, low = halves(x)
            cols = slice(part * waves, (part + 1) * waves)
            coeff[0 : 4 * nq, cols] = high
            coeff[4 * nq :, cols] = low

    both = dot(coeff[...], t_ref[...], ((1,), (0,)))
    sums = both[: 4 * nq] + both[4 * nq :]
    c = c_ref[...]
    out_ref[0:nq, :] = sums[:nq]
    forces = [
        jnp.sum(c * sums[(d + 1) * nq : (d + 2) * nq], axis=0, keepdims=True) for d in range(3)
    ]
    out_ref[nq : nq + 8, :] = jnp.concatenate(forces + [jnp.zeros((5, c.shape[1]), F32)], axis=0)


def field_call(place, s, n, c, table, waves):
    rows, atoms = table.shape
    step = 512
    nq = c.shape[0]
    return pl.pallas_call(
        field_kernel,
        grid_spec=pltpu.PrefetchScalarGridSpec(
            num_scalar_prefetch=1,
            grid=(atoms // step,),
            in_specs=[
                pl.BlockSpec((nq, rows), lambda i, place: (0, 0)),
                pl.BlockSpec((3, waves), lambda i, place: (0, place[1])),
                pl.BlockSpec((nq, step), lambda i, place: (0, i)),
                pl.BlockSpec((rows, step), lambda i, place: (0, i)),
            ],
            out_specs=pl.BlockSpec((nq + 8, step), lambda i, place: (0, i)),
            scratch_shapes=[pltpu.VMEM((8 * nq, rows), BF)],
        ),
        out_shape=jax.ShapeDtypeStruct((nq + 8, atoms), F32),
        compiler_params=params(12),
        cost_estimate=pl.CostEstimate(flops=rows * atoms * 512, transcendentals=0, bytes_accessed=rows * atoms * 2),
        name="fields",
    )(place, s, n, c, table)


def exchanged(x, axis, step):
    size = lax.axis_size(axis)
    if step >= size:
        return x
    return x + lax.ppermute(x, axis, [(i, i ^ step) for i in range(size)])


def summed(x, axis, step=1):
    size = lax.axis_size(axis)
    assert size & (size - 1) == 0
    while step < size:
        x = exchanged(x, axis, step)
        step *= 2
    return x


def whole_step(
    queries,
    key_states,
    value_states,
    fractional,
    block_counts,
    neighbors,
    integer_wave_vectors,
    charge_weight,
):
    heads, head_dim, atoms = queries.shape
    _, comps, _ = value_states.shape
    nq = charge_weight.shape[1]
    waves = integer_wave_vectors.shape[1] // lax.axis_size("inner")
    inv_root = 1.0 / math.sqrt(atoms * lax.axis_size("seq"))
    place = jnp.stack([lax.axis_index("seq"), lax.axis_index("inner")]).astype(jnp.int32)
    width = REACH * BS
    count = lax.axis_size("seq")
    up = [(i, i + 1) for i in range(count - 1)]
    down = [(i + 1, i) for i in range(count - 1)]

    keys = key_states.reshape(heads * head_dim, atoms)
    asked = queries.reshape(heads * head_dim, atoms)
    values = value_states.transpose(1, 0, 2)
    lists = neighbors.T
    weight = charge_weight.T
    tail, head = slice(atoms - width, atoms), slice(0, width)

    def shift(pick):
        left = lax.ppermute(pick(tail), "seq", up)
        right = lax.ppermute(pick(head), "seq", down)
        return left, right

    cut = 1 + (comps - 1) * 2 // 3
    sides = shift(lambda cols: jnp.concatenate([keys[:, cols], values[0, :, cols]], axis=0))
    halo_a = shift(lambda cols: values[1:cut, :, cols])

    p_in, scale_in, charge_in = scores_call(
        "interior", lists, block_counts, place, asked, keys, values, weight, (), heads, head_dim
    )
    p_out, scale_out, charge_out = scores_call(
        "edges", lists, block_counts, place, asked, keys, values, weight, sides, heads, head_dim
    )
    table = table_call(place, integer_wave_vectors, fractional, waves).reshape(2 * waves, atoms)
    part = jnp.concatenate([charge_out[:REACH], charge_in, charge_out[REACH:]], axis=0)
    part = part.transpose(1, 0, 2).reshape(nq, atoms)
    charges = summed(part, "inner")
    structure = structure_call(charges, table, inv_root)
    structure = exchanged(structure, "seq", 1)
    later, structure = lax.optimization_barrier((values, structure))
    halo_b = shift(lambda cols: later[cut:, :, cols])
    structure = summed(structure, "seq", 2)
    fields = summed(field_call(place, structure, integer_wave_vectors, charges, table, waves), "inner")

    attention, band = interior_call(lists, place, values, p_in, scale_in, heads)
    attention = edge_call(
        lists, place, values.shape, band, attention, p_out, scale_out, *sides, halo_a + halo_b, heads, head_dim
    )
    return (attention.transpose(1, 0, 2), fields[:nq], fields[nq : nq + 3])


def solution(mesh):
    placed = (
        P("inner", None, "seq"),
        P("inner", None, "seq"),
        P("inner", None, "seq"),
        P(None, "seq"),
        P(),
        P("seq", None),
        P(),
        P("inner", None),
    )
    return jax.shard_map(
        whole_step,
        mesh=mesh,
        in_specs=placed,
        out_specs=(P("inner", None, "seq"), P(None, "seq"), P(None, "seq")),
        check_vma=False,
    )
```

```python
import functools
import math

import jax
import jax.numpy as jnp
from jax import lax
from jax.experimental import pallas as pl
from jax.experimental.pallas import tpu as pltpu
from jax.sharding import PartitionSpec as P


BS = 256
NNB = 3
REACH = 2

ewald_scale = 40.0
ewald_damp = 0.02

BF = jnp.bfloat16
F32 = jnp.float32

SIN = (6.283185302511499, -41.34170040531678, 81.60513138577247, -76.70301535353673,
       42.02592698394968, -14.899846662448152, 3.2381375038938693)
COS = (0.9999999890590217, -19.73920449945376, 64.93911745989128, -85.45013953083522,
       60.167630950695504, -25.967599247822193, 6.5286581606558824)


def params(mib):
    return pltpu.CompilerParams(vmem_limit_bytes=mib << 20, dimension_semantics=("arbitrary",))


def dot(a, b, dims):
    return lax.dot_general(a, b, (dims, ((), ())), preferred_element_type=F32)


def horner(coeffs, u):
    total = coeffs[-1]
    for c in coeffs[-2::-1]:
        total = total * u + c
    return total


def halves(x):
    high = x.astype(BF)
    return high, (x - high.astype(F32)).astype(BF)


def load_kernel(chans, rows, width, place, *refs):
    (k, v, others), (near, far, near_big, far_big, v0, *copies) = (refs[0], refs[1], refs[2:7]), refs[7:-1]
    sems = refs[-1]
    atoms = v.shape[2]
    even = place[0] % 2 == 0
    last = atoms - width
    near_cols = pl.ds(pl.multiple_of(jnp.where(even, last, 0), 128), width)
    far_cols = pl.ds(pl.multiple_of(jnp.where(even, 0, last), 128), width)
    moves = []
    for piece, cols in ((far, far_cols), (near, near_cols)):
        moves.append((k.at[:, cols], piece.at[pl.ds(0, rows)]))
        moves.append((v.at[0, :, cols], piece.at[pl.ds(rows, chans)]))
    moves.append((k, copies[0]))
    moves.append((v.at[0], v0))
    moves += list(zip(others, copies[1:]))
    for piece, cols in ((far_big, far_cols), (near_big, near_cols)):
        moves.append((v.at[pl.ds(1, piece.shape[0]), :, cols], piece))
    started = [pltpu.make_async_copy(src, dst, sems.at[i]) for i, (src, dst) in enumerate(moves)]
    for copy in started:
        copy.start()
    for copy in started:
        copy.wait()


def load_call(place, k, v, others, width):
    comps, chans, atoms = v.shape
    rows = k.shape[0]
    shape = jax.ShapeDtypeStruct
    outs = [shape((rows + chans, width), BF)] * 2 + [shape((comps - 1, chans, width), BF)] * 2
    outs += [shape((chans, atoms), BF)] + [shape(x.shape, x.dtype) for x in (k, *others)]
    return pl.pallas_call(
        functools.partial(load_kernel, chans, rows, width),
        grid_spec=pltpu.PrefetchScalarGridSpec(
            num_scalar_prefetch=1,
            grid=(1,),
            in_specs=[pl.BlockSpec(memory_space=pltpu.HBM)] * (2 + len(others)),
            out_specs=[pl.BlockSpec(memory_space=pl.ANY)] * len(outs),
            scratch_shapes=[pltpu.SemaphoreType.DMA((8 + len(others),))],
        ),
        out_shape=outs,
        compiler_params=params(2),
        cost_estimate=pl.CostEstimate(flops=0, transcendentals=0, bytes_accessed=4 * comps * chans * width),
        name="load",
    )(place, *[pltpu.with_memory_space_constraint(x, pltpu.HBM) for x in (k, v, *others)])


def on_left(place, far):
    even = place[0] % 2 == 0
    return even if far else jnp.logical_not(even)


def edge_block(step, place, blocks):
    left = (step < REACH) == (place[0] % 2 == 0)
    return step % REACH + jnp.where(left, 0, blocks - REACH)


def score_kernel(heads, head_dim, head_chan, blocks, part, lists, counts, place, *refs):
    q_ref, k_ref, v_ref, cw_ref = refs[:4]
    sides, (p_ref, scale_ref, charge_ref, kaug, v0) = refs[4:-5], refs[-5:]
    i = pl.program_id(0)
    first = place[0] * blocks
    total = counts.shape[0]

    @pl.when(i == 0)
    def _():
        lane = lax.broadcasted_iota(jnp.int32, (16, BS), 1)
        row = lax.broadcasted_iota(jnp.int32, (16, BS), 0)

        def fill(b, keys, values):
            index = first + b - REACH
            inside = (index >= 0) & (index < total)
            live = jnp.where(inside, counts[jnp.clip(index, 0, total - 1)], 0)
            bias = jnp.where((row == 0) & (lane >= live), -1e30, 0.0).astype(BF)
            v0[b] = values
            for h in range(heads):
                kaug[b, h, 0:head_dim, :] = keys[h * head_dim : (h + 1) * head_dim]
                kaug[b, h, head_dim : head_dim + 16, :] = bias

        for b in range(blocks):
            cols = slice(b * BS, (b + 1) * BS)
            fill(b + REACH, k_ref[:, cols], v_ref[:, cols])
        for far, side in zip((True, False), sides[:2]):
            base = jnp.where(on_left(place, far), 0, blocks + REACH)
            for b in range(REACH):
                cols = slice(b * BS, (b + 1) * BS)
                fill(base + b, side[0 : heads * head_dim, cols], side[heads * head_dim :, cols])

    g = i + REACH if part == "interior" else edge_block(i, place, blocks)
    own_count = counts[first + g]
    live_q = lax.broadcasted_iota(jnp.int32, (1, BS), 1) < own_count
    ones = jnp.where(lax.broadcasted_iota(jnp.int32, (16, BS), 0) == 0, 1.0, 0.0).astype(BF)
    listed = [lists[e, g] - (first - REACH) for e in range(NNB)]
    charge = None
    for h in range(heads):
        q = (q_ref[h * head_dim : (h + 1) * head_dim, :].astype(F32) * head_dim ** (-0.5)).astype(BF)
        qa = jnp.concatenate([q, ones], axis=0)
        scores = [dot(kaug[b, h], qa, ((0,), (0,))) for b in listed]
        top = functools.reduce(jnp.maximum, [jnp.max(s, axis=0, keepdims=True) for s in scores])
        denominator = 0.0
        mixed = 0.0
        for e, b in enumerate(listed):
            w = jnp.exp(scores[e] - top)
            denominator = denominator + jnp.sum(w, axis=0, keepdims=True)
            w16 = w.astype(BF)
            p_ref[0, h, e * BS : (e + 1) * BS, :] = w16
            mixed = mixed + dot(v0[b, h * head_chan : (h + 1) * head_chan, :], w16, ((1,), (0,)))
        scale = jnp.where(live_q, 1.0 / denominator, 0.0)
        scale_ref[0, h : h + 1, :] = scale
        att0 = (mixed * scale).astype(BF)
        term = dot(cw_ref[:, h * head_chan : (h + 1) * head_chan], att0, ((1,), (0,)))
        charge = term if charge is None else charge + term
    charge_ref[...] = charge


def scores_call(part, lists, counts, place, q, k, v0, cw, sides, heads, head_dim):
    chans, atoms = v0.shape
    blocks = atoms // BS
    nq = cw.shape[0]
    head_chan = chans // heads
    band = blocks + 2 * REACH
    steps = blocks - 2 * REACH if part == "interior" else 2 * REACH

    def at(i, lists, counts, place):
        return i + REACH if part == "interior" else edge_block(i, place, blocks)

    whole = lambda shape: pl.BlockSpec(shape, lambda g, *_: (0,) * len(shape), pipeline_mode=pl.Buffered(1))
    any_space = pl.BlockSpec(memory_space=pl.ANY)
    return pl.pallas_call(
        functools.partial(score_kernel, heads, head_dim, head_chan, blocks, part),
        grid_spec=pltpu.PrefetchScalarGridSpec(
            num_scalar_prefetch=3,
            grid=(steps,),
            in_specs=[
                pl.BlockSpec((heads * head_dim, BS), lambda i, *s: (0, at(i, *s))),
                whole(k.shape),
                whole(v0.shape),
                whole(cw.shape),
            ]
            + [whole(s.shape) for s in sides[:2]] + [any_space] * len(sides[2:]),
            out_specs=[
                pl.BlockSpec((1, heads, NNB * BS, BS), lambda i, *_: (i, 0, 0, 0)),
                pl.BlockSpec((1, heads, BS), lambda i, *_: (i, 0, 0)),
                pl.BlockSpec((nq, BS), lambda i, *s: (0, at(i, *s))),
            ],
            scratch_shapes=[
                pltpu.VMEM((band, heads, head_dim + 16, BS), BF),
                pltpu.VMEM((band, chans, BS), BF),
            ],
        ),
        out_shape=[
            jax.ShapeDtypeStruct((steps, heads, NNB * BS, BS), BF),
            jax.ShapeDtypeStruct((steps, heads, BS), F32),
            jax.ShapeDtypeStruct((nq, atoms), F32),
        ],
        input_output_aliases={9: 2} if sides else {},
        compiler_params=params(10),
        cost_estimate=pl.CostEstimate(
            flops=steps * heads * NNB * BS * BS * 200, transcendentals=steps * heads * NNB * BS * BS,
            bytes_accessed=steps * heads * NNB * BS * BS * 2,
        ),
    )(lists, counts, place, q, k, v0, cw, *sides)


def mix_kernel(heads, head_dim, head_chan, blocks, part, lists, place, v_ref, p_ref, scale_ref, *refs):
    halo, out_ref = refs[: 2 if part in ("far", "near") else 0], refs[-2 if part in ("far", "near") else -1]
    comps = v_ref.shape[0]
    i = pl.program_id(0)
    offset = place[0] * blocks
    if halo:
        small, big = halo
        band = refs[-1]
        span = 3 * REACH
        left = on_left(place, part == "far")
        begin = jnp.where(left, 0, blocks + 2 * REACH - span)

        @pl.when(i == 0)
        def _():
            own = jnp.where(left, REACH, 0)
            first = jnp.where(left, 0, blocks - 2 * REACH)
            for b in range(2 * REACH):
                band[own + b] = v_ref[:, :, pl.ds(pl.multiple_of((first + b) * BS, BS), BS)]
            other = jnp.where(left, 0, 2 * REACH)
            for b in range(REACH):
                cols = slice(b * BS, (b + 1) * BS)
                band[other + b, 0] = small[heads * head_dim :, cols]
                band[other + b, 1:] = big[:, :, cols]

        g = edge_block(i if part == "far" else i + REACH, place, blocks)
        listed = [lists[e, g] - offset + REACH - begin for e in range(NNB)]
        pick = lambda b, rows: band[b, :, rows, :]
    else:
        g = i + (REACH if part == "low" else blocks // 2)
        listed = [lists[e, g] - offset for e in range(NNB)]
        pick = lambda b, rows: v_ref[:, rows, pl.ds(pl.multiple_of(b * BS, BS), BS)]
    for h in range(heads):
        rows = slice(h * head_chan, (h + 1) * head_chan)
        acc = 0.0
        for e in range(NNB):
            v = pick(listed[e], rows).reshape(comps * head_chan, BS)
            acc = acc + dot(v, p_ref[0, h, e * BS : (e + 1) * BS, :], ((1,), (0,)))
        acc = acc * scale_ref[0, h : h + 1, :]
        out_ref[:, rows, :] = acc.astype(BF).reshape(comps, head_chan, BS)


def mix_call(part, lists, place, v, p, scale, halo, prev, heads, head_dim):
    comps, chans, atoms = v.shape
    blocks = atoms // BS
    half = blocks // 2 - REACH
    steps = REACH if halo else half
    skip = {"low": 0, "high": half, "far": 0, "near": REACH}[part]

    def at(i, lists, place):
        if part in ("low", "high"):
            return i + REACH + skip
        return edge_block(i + skip, place, blocks)

    whole = lambda shape: pl.BlockSpec(shape, lambda g, *_: (0,) * len(shape), pipeline_mode=pl.Buffered(1))
    extra = list(halo) + ([] if prev is None else [prev])
    return pl.pallas_call(
        functools.partial(mix_kernel, heads, head_dim, chans // heads, blocks, part),
        grid_spec=pltpu.PrefetchScalarGridSpec(
            num_scalar_prefetch=2,
            grid=(steps,),
            in_specs=[
                whole(v.shape),
                pl.BlockSpec((1, heads, NNB * BS, BS), lambda i, *_: (i + skip, 0, 0, 0)),
                pl.BlockSpec((1, heads, BS), lambda i, *_: (i + skip, 0, 0)),
            ]
            + [whole(x.shape) for x in halo]
            + ([] if prev is None else [pl.BlockSpec(memory_space=pl.ANY)]),
            out_specs=pl.BlockSpec((comps, chans, BS), lambda i, *s: (0, 0, at(i, *s))),
            scratch_shapes=[pltpu.VMEM((3 * REACH, comps, chans, BS), BF)] if halo else [],
        ),
        out_shape=jax.ShapeDtypeStruct(v.shape, BF),
        input_output_aliases={} if prev is None else {4 + len(extra): 0},
        compiler_params=params(16),
        cost_estimate=pl.CostEstimate(
            flops=steps * chans * comps * NNB * BS * BS * 2, transcendentals=0,
            bytes_accessed=steps * chans * comps * BS * 8,
        ),
    )(lists, place, v, p, scale, *extra)


def table_kernel(place, n_ref, f_ref, out_ref, parts):
    @pl.when(pl.program_id(0) == 0)
    def _():
        f = f_ref[...]
        high, low = halves(f)
        rest = ((f - high.astype(F32)) - low.astype(F32)).astype(BF)
        parts[...] = jnp.concatenate([high, low, rest], axis=0)

    n = n_ref[...].astype(F32).astype(BF)
    turns = dot(jnp.concatenate([n, n, n], axis=0), parts[...], ((0,), (0,)))
    r = turns - jnp.round(turns)
    u = r * r
    out_ref[0] = horner(COS, u).astype(BF)
    out_ref[1] = (horner(SIN, u) * r).astype(BF)


def table_call(place, n, f, waves):
    step = 128
    atoms = f.shape[1]
    return pl.pallas_call(
        table_kernel,
        grid_spec=pltpu.PrefetchScalarGridSpec(
            num_scalar_prefetch=1,
            grid=(waves // step,),
            in_specs=[
                pl.BlockSpec((3, step), lambda i, place: (0, place[1] * (waves // step) + i)),
                pl.BlockSpec(f.shape, lambda i, place: (0, 0)),
            ],
            out_specs=pl.BlockSpec((2, step, atoms), lambda i, place: (0, i, 0)),
            scratch_shapes=[pltpu.VMEM((9, atoms), BF)],
        ),
        out_shape=jax.ShapeDtypeStruct((2, waves, atoms), BF),
        compiler_params=params(16),
        cost_estimate=pl.CostEstimate(
            flops=waves * atoms * 400, transcendentals=0, bytes_accessed=waves * atoms * 4
        ),
        name="table",
    )(place, n, f)


def structure_kernel(inv_root, c_ref, t_ref, out_ref):
    high, low = halves(c_ref[...])
    both = jnp.concatenate([high, low], axis=0)
    s = dot(t_ref[...], both, ((1,), (1,)))
    nq = c_ref.shape[0]
    out_ref[...] = (s[:, :nq] + s[:, nq:]).T * inv_root


def structure_call(c, table, inv_root):
    rows, atoms = table.shape
    step = min(256, rows)
    nq = c.shape[0]
    return pl.pallas_call(
        functools.partial(structure_kernel, inv_root),
        grid=(rows // step,),
        in_specs=[pl.BlockSpec((nq, atoms), lambda i: (0, 0)), pl.BlockSpec((step, atoms), lambda i: (i, 0))],
        out_specs=pl.BlockSpec((nq, step), lambda i: (0, i)),
        out_shape=jax.ShapeDtypeStruct((nq, rows), F32),
        compiler_params=params(12),
        cost_estimate=pl.CostEstimate(flops=rows * atoms * 512, transcendentals=0, bytes_accessed=rows * atoms * 2),
        name="structure",
    )(c, table)


def field_kernel(place, s_ref, n_ref, c_ref, t_ref, out_ref, coeff):
    nq = c_ref.shape[0]
    waves = n_ref.shape[1]

    @pl.when(pl.program_id(0) == 0)
    def _():
        n = n_ref[...].astype(F32)
        norm = n[0:1] * n[0:1] + n[1:2] * n[1:2] + n[2:3] * n[2:3]
        weight = ewald_scale * jnp.exp(-ewald_damp * norm) / norm
        real = s_ref[:, :waves] * weight
        imag = s_ref[:, waves:] * weight
        with_cos = jnp.concatenate([real] + [-imag * n[d : d + 1] for d in range(3)], axis=0)
        with_sin = jnp.concatenate([imag] + [real * n[d : d + 1] for d in range(3)], axis=0)
        for part, x in enumerate((with_cos, with_sin)):
            high, low = halves(x)
            cols = slice(part * waves, (part + 1) * waves)
            coeff[0 : 4 * nq, cols] = high
            coeff[4 * nq :, cols] = low

    both = dot(coeff[...], t_ref[...], ((1,), (0,)))
    sums = both[: 4 * nq] + both[4 * nq :]
    c = c_ref[...]
    out_ref[0:nq, :] = sums[:nq]
    forces = [
        jnp.sum(c * sums[(d + 1) * nq : (d + 2) * nq], axis=0, keepdims=True) for d in range(3)
    ]
    out_ref[nq : nq + 8, :] = jnp.concatenate(forces + [jnp.zeros((5, c.shape[1]), F32)], axis=0)


def field_call(place, s, n, c, table, waves):
    rows, atoms = table.shape
    step = 512
    nq = c.shape[0]
    return pl.pallas_call(
        field_kernel,
        grid_spec=pltpu.PrefetchScalarGridSpec(
            num_scalar_prefetch=1,
            grid=(atoms // step,),
            in_specs=[
                pl.BlockSpec((nq, rows), lambda i, place: (0, 0)),
                pl.BlockSpec((3, waves), lambda i, place: (0, place[1])),
                pl.BlockSpec((nq, step), lambda i, place: (0, i)),
                pl.BlockSpec((rows, step), lambda i, place: (0, i)),
            ],
            out_specs=pl.BlockSpec((nq + 8, step), lambda i, place: (0, i)),
            scratch_shapes=[pltpu.VMEM((8 * nq, rows), BF)],
        ),
        out_shape=jax.ShapeDtypeStruct((nq + 8, atoms), F32),
        compiler_params=params(12),
        cost_estimate=pl.CostEstimate(flops=rows * atoms * 512, transcendentals=0, bytes_accessed=rows * atoms * 2),
        name="fields",
    )(place, s, n, c, table)


def exchanged(x, axis, step):
    size = lax.axis_size(axis)
    if step >= size:
        return x
    return x + lax.ppermute(x, axis, [(i, i ^ step) for i in range(size)])


def summed(x, axis, step=1):
    size = lax.axis_size(axis)
    assert size & (size - 1) == 0
    while step < size:
        x = exchanged(x, axis, step)
        step *= 2
    return x


def whole_step(
    queries,
    key_states,
    value_states,
    fractional,
    block_counts,
    neighbors,
    integer_wave_vectors,
    charge_weight,
):
    heads, head_dim, atoms = queries.shape
    nq = charge_weight.shape[1]
    waves = integer_wave_vectors.shape[1] // lax.axis_size("inner")
    inv_root = 1.0 / math.sqrt(atoms * lax.axis_size("seq"))
    place = jnp.stack([lax.axis_index("seq"), lax.axis_index("inner")]).astype(jnp.int32)
    width = REACH * BS
    count = lax.axis_size("seq")
    near_pairs = [(i, i ^ 1) for i in range(count)]
    far_pairs = [(i, i + 1 if i % 2 else i - 1) for i in range(1, count - 1)]

    def swap(x, pairs):
        return lax.ppermute(x, "seq", pairs)

    values = value_states.transpose(1, 0, 2)
    near, far, near_big, far_big, v0, keys, asked, weight, counts, lists, vectors = load_call(
        place, key_states.reshape(heads * head_dim, atoms), values,
        (queries.reshape(heads * head_dim, atoms), charge_weight.T, block_counts, neighbors.T, integer_wave_vectors),
        width,
    )
    far = swap(far, far_pairs)
    near = swap(near, near_pairs)
    far_big = swap(far_big, far_pairs)
    near_big = swap(near_big, near_pairs)

    p_in, scale_in, part = scores_call(
        "interior", lists, counts, place, asked, keys, v0, weight, (), heads, head_dim
    )
    p_out, scale_out, part = scores_call(
        "edges", lists, counts, place, asked, keys, v0, weight, (far, near, part), heads, head_dim
    )
    table = table_call(place, vectors, fractional, waves).reshape(2 * waves, atoms)
    charges = summed(part, "inner")
    structure = structure_call(charges, table, inv_root)
    structure = exchanged(summed(structure, "seq", 2), "seq", 1)
    fields = field_call(place, structure, vectors, charges, table, waves)
    fields = summed(fields, "inner")

    mix = functools.partial(mix_call, heads=heads, head_dim=head_dim)
    attention = mix("low", lists, place, values, p_in, scale_in, (), None)
    attention = mix("high", lists, place, values, p_in, scale_in, (), attention)
    attention = mix("far", lists, place, values, p_out, scale_out, (far, far_big), attention)
    attention = mix("near", lists, place, values, p_out, scale_out, (near, near_big), attention)
    return (attention.transpose(1, 0, 2), fields[:nq], fields[nq : nq + 3])


def solution(mesh):
    placed = (
        P("inner", None, "seq"),
        P("inner", None, "seq"),
        P("inner", None, "seq"),
        P(None, "seq"),
        P(),
        P("seq", None),
        P(),
        P("inner", None),
    )
    return jax.shard_map(
        whole_step,
        mesh=mesh,
        in_specs=placed,
        out_specs=(P("inner", None, "seq"), P(None, "seq"), P(None, "seq")),
        check_vma=False,
    )
```

```python
import functools
import math

import jax
import jax.numpy as jnp
from jax import lax
from jax.experimental import pallas as pl
from jax.experimental.pallas import tpu as pltpu
from jax.sharding import PartitionSpec as P


BS = 256
NNB = 3
REACH = 2
KMAX = 7
LOG2E = 1.4426950408889634

ewald_scale = 40.0
ewald_damp = 0.02

BF = jnp.bfloat16
F32 = jnp.float32

SIN = (6.283185302511499, -41.34170040531678, 81.60513138577247, -76.70301535353673,
       42.02592698394968, -14.899846662448152, 3.2381375038938693)
COS = (0.9999999890590217, -19.73920449945376, 64.93911745989128, -85.45013953083522,
       60.167630950695504, -25.967599247822193, 6.5286581606558824)


def params(mib):
    return pltpu.CompilerParams(vmem_limit_bytes=mib << 20, dimension_semantics=("arbitrary",))


def dot(a, b, dims):
    return lax.dot_general(a, b, (dims, ((), ())), preferred_element_type=F32)


def horner(coeffs, u):
    total = coeffs[-1]
    for c in coeffs[-2::-1]:
        total = total * u + c
    return total


def halves(x):
    high = x.astype(BF)
    return high, (x - high.astype(F32)).astype(BF)


def thirds(x):
    high, low = halves(x)
    return high, low, ((x - high.astype(F32)) - low.astype(F32)).astype(BF)


def load_kernel(chans, rows, width, place, *refs):
    (k, v, others), (near, far, near_big, far_big, v0, *copies) = (refs[0], refs[1], refs[2:7]), refs[7:-1]
    sems = refs[-1]
    atoms = v.shape[2]
    even = place[0] % 2 == 0
    last = atoms - width
    near_cols = pl.ds(pl.multiple_of(jnp.where(even, last, 0), 128), width)
    far_cols = pl.ds(pl.multiple_of(jnp.where(even, 0, last), 128), width)
    moves = []
    for piece, cols in ((far, far_cols), (near, near_cols)):
        moves.append((k.at[:, cols], piece.at[pl.ds(0, rows)]))
        moves.append((v.at[0, :, cols], piece.at[pl.ds(rows, chans)]))
    moves.append((k, copies[0]))
    moves.append((v.at[0], v0))
    moves += list(zip(others, copies[1:]))
    for piece, cols in ((far_big, far_cols), (near_big, near_cols)):
        moves.append((v.at[pl.ds(1, piece.shape[0]), :, cols], piece))
    started = [pltpu.make_async_copy(src, dst, sems.at[i]) for i, (src, dst) in enumerate(moves)]
    for copy in started:
        copy.start()
    for copy in started:
        copy.wait()


def load_call(place, k, v, others, width):
    comps, chans, atoms = v.shape
    rows = k.shape[0]
    shape = jax.ShapeDtypeStruct
    outs = [shape((rows + chans, width), BF)] * 2 + [shape((comps - 1, chans, width), BF)] * 2
    outs += [shape((chans, atoms), BF)] + [shape(x.shape, x.dtype) for x in (k, *others)]
    return pl.pallas_call(
        functools.partial(load_kernel, chans, rows, width),
        grid_spec=pltpu.PrefetchScalarGridSpec(
            num_scalar_prefetch=1,
            grid=(1,),
            in_specs=[pl.BlockSpec(memory_space=pltpu.HBM)] * (2 + len(others)),
            out_specs=[pl.BlockSpec(memory_space=pl.ANY)] * len(outs),
            scratch_shapes=[pltpu.SemaphoreType.DMA((8 + len(others),))],
        ),
        out_shape=outs,
        compiler_params=params(2),
        cost_estimate=pl.CostEstimate(flops=0, transcendentals=0, bytes_accessed=4 * comps * chans * width),
        name="load",
    )(place, *[pltpu.with_memory_space_constraint(x, pltpu.HBM) for x in (k, v, *others)])


def on_left(place, far):
    even = place[0] % 2 == 0
    return even if far else jnp.logical_not(even)


def edge_block(step, place, blocks):
    left = (step < REACH) == (place[0] % 2 == 0)
    return step % REACH + jnp.where(left, 0, blocks - REACH)


def score_kernel(heads, head_dim, head_chan, blocks, part, lists, counts, place, *refs):
    q_ref, k_ref, v_ref, cw_ref = refs[:4]
    sides, (p_ref, scale_ref, charge_ref, kaug, v0) = refs[4:-5], refs[-5:]
    i = pl.program_id(0)
    first = place[0] * blocks
    total = counts.shape[0]

    @pl.when(i == 0)
    def _():
        lane = lax.broadcasted_iota(jnp.int32, (16, BS), 1)
        row = lax.broadcasted_iota(jnp.int32, (16, BS), 0)

        def fill(b, keys, values):
            index = first + b - REACH
            inside = (index >= 0) & (index < total)
            live = jnp.where(inside, counts[jnp.clip(index, 0, total - 1)], 0)
            bias = jnp.where((row == 0) & (lane >= live), -1e30, 0.0).astype(BF)
            v0[b] = values
            for h in range(heads):
                for copy in range(3):
                    kaug[b, h, copy * head_dim : (copy + 1) * head_dim, :] = keys[h * head_dim : (h + 1) * head_dim]
                kaug[b, h, 3 * head_dim : 3 * head_dim + 16, :] = bias

        for b in range(blocks):
            cols = slice(b * BS, (b + 1) * BS)
            fill(b + REACH, k_ref[:, cols], v_ref[:, cols])
        for far, side in zip((True, False), sides[:2]):
            base = jnp.where(on_left(place, far), 0, blocks + REACH)
            for b in range(REACH):
                cols = slice(b * BS, (b + 1) * BS)
                fill(base + b, side[0 : heads * head_dim, cols], side[heads * head_dim :, cols])

    g = i + REACH if part == "interior" else edge_block(i, place, blocks)
    own_count = counts[first + g]
    live_q = lax.broadcasted_iota(jnp.int32, (1, BS), 1) < own_count
    top_row = jnp.where(lax.broadcasted_iota(jnp.int32, (16, BS), 0) == 0, 1.0, 0.0).astype(BF)
    listed = [lists[e, g] - (first - REACH) for e in range(NNB)]
    scores = []
    for h in range(heads):
        q = q_ref[h * head_dim : (h + 1) * head_dim, :].astype(F32) * (head_dim ** (-0.5) * LOG2E)
        qa = jnp.concatenate([*thirds(q), top_row], axis=0)
        scores.append([dot(kaug[b, h], qa, ((0,), (0,))) for b in listed])
    charge = None
    for h in range(heads):
        top = functools.reduce(jnp.maximum, [jnp.max(s, axis=0, keepdims=True) for s in scores[h]])
        mixed = 0.0
        for e, b in enumerate(listed):
            w16 = jnp.exp2(scores[h][e] - top).astype(BF)
            p_ref[i, h, e * BS : (e + 1) * BS, :] = w16
            v = jnp.concatenate([v0[b, h * head_chan : (h + 1) * head_chan, :], top_row], axis=0)
            mixed = mixed + dot(v, w16, ((1,), (0,)))
        denominator = mixed[head_chan : head_chan + 1]
        scale = jnp.where(live_q, 1.0 / denominator, 0.0)
        scale_ref[i, h : h + 1, :] = scale
        att0 = (mixed[:head_chan] * scale).astype(BF)
        term = dot(cw_ref[:, h * head_chan : (h + 1) * head_chan], att0, ((1,), (0,)))
        charge = term if charge is None else charge + term
    charge_ref[...] = charge


def scores_call(part, lists, counts, place, q, k, v0, cw, sides, heads, head_dim):
    chans, atoms = v0.shape
    blocks = atoms // BS
    nq = cw.shape[0]
    head_chan = chans // heads
    band = blocks + 2 * REACH
    steps = blocks - 2 * REACH if part == "interior" else 2 * REACH

    def at(i, lists, counts, place):
        return i + REACH if part == "interior" else edge_block(i, place, blocks)

    whole = lambda shape: pl.BlockSpec(shape, lambda g, *_: (0,) * len(shape), pipeline_mode=pl.Buffered(1))
    any_space = pl.BlockSpec(memory_space=pl.ANY)
    return pl.pallas_call(
        functools.partial(score_kernel, heads, head_dim, head_chan, blocks, part),
        grid_spec=pltpu.PrefetchScalarGridSpec(
            num_scalar_prefetch=3,
            grid=(steps,),
            in_specs=[
                pl.BlockSpec((heads * head_dim, BS), lambda i, *s: (0, at(i, *s))),
                whole(k.shape),
                whole(v0.shape),
                whole(cw.shape),
            ]
            + [whole(s.shape) for s in sides[:2]] + [any_space] * len(sides[2:]),
            out_specs=[
                whole((steps, heads, NNB * BS, BS)),
                whole((steps, heads, BS)),
                pl.BlockSpec((nq, BS), lambda i, *s: (0, at(i, *s))),
            ],
            scratch_shapes=[
                pltpu.VMEM((band, heads, 3 * head_dim + 16, BS), BF),
                pltpu.VMEM((band, chans, BS), BF),
            ],
        ),
        out_shape=[
            jax.ShapeDtypeStruct((steps, heads, NNB * BS, BS), BF),
            jax.ShapeDtypeStruct((steps, heads, BS), F32),
            jax.ShapeDtypeStruct((nq, atoms), F32),
        ],
        input_output_aliases={9: 2} if sides else {},
        compiler_params=params(10),
        cost_estimate=pl.CostEstimate(
            flops=steps * heads * NNB * BS * BS * 200, transcendentals=steps * heads * NNB * BS * BS,
            bytes_accessed=steps * heads * NNB * BS * BS * 2,
        ),
    )(lists, counts, place, q, k, v0, cw, *sides)


def mix_kernel(heads, head_dim, head_chan, blocks, part, skip, lists, place, v_ref, p_ref, scale_ref, *refs):
    halo, out_ref = refs[: 2 if part in ("far", "near") else 0], refs[-2 if part in ("far", "near") else -1]
    comps = v_ref.shape[0]
    i = pl.program_id(0)
    offset = place[0] * blocks
    if halo:
        small, big = halo
        band = refs[-1]
        span = 3 * REACH
        left = on_left(place, part == "far")
        begin = jnp.where(left, 0, blocks + 2 * REACH - span)

        @pl.when(i == 0)
        def _():
            own = jnp.where(left, REACH, 0)
            first = jnp.where(left, 0, blocks - 2 * REACH)
            for b in range(2 * REACH):
                band[own + b] = v_ref[:, :, pl.ds(pl.multiple_of((first + b) * BS, BS), BS)]
            other = jnp.where(left, 0, 2 * REACH)
            for b in range(REACH):
                cols = slice(b * BS, (b + 1) * BS)
                band[other + b, 0] = small[heads * head_dim :, cols]
                band[other + b, 1:] = big[:, :, cols]

        g = edge_block(i if part == "far" else i + REACH, place, blocks)
        listed = [lists[e, g] - offset + REACH - begin for e in range(NNB)]
        pick = lambda b, rows: band[b, :, rows, :]
    else:
        g = i + (REACH if part == "low" else blocks // 2)
        listed = [lists[e, g] - offset for e in range(NNB)]
        pick = lambda b, rows: v_ref[:, rows, pl.ds(pl.multiple_of(b * BS, BS), BS)]
    for h in range(heads):
        rows = slice(h * head_chan, (h + 1) * head_chan)
        acc = 0.0
        for e in range(NNB):
            v = pick(listed[e], rows).reshape(comps * head_chan, BS)
            acc = acc + dot(v, p_ref[i + skip, h, e * BS : (e + 1) * BS, :], ((1,), (0,)))
        acc = acc * scale_ref[i + skip, h : h + 1, :]
        out_ref[:, rows, :] = acc.astype(BF).reshape(comps, head_chan, BS)


def mix_call(part, lists, place, v, p, scale, halo, prev, heads, head_dim):
    comps, chans, atoms = v.shape
    blocks = atoms // BS
    half = blocks // 2 - REACH
    steps = REACH if halo else half
    skip = {"low": 0, "high": half, "far": 0, "near": REACH}[part]

    def at(i, lists, place):
        if part in ("low", "high"):
            return i + REACH + skip
        return edge_block(i + skip, place, blocks)

    whole = lambda shape: pl.BlockSpec(shape, lambda g, *_: (0,) * len(shape), pipeline_mode=pl.Buffered(1))
    extra = list(halo) + ([] if prev is None else [prev])
    return pl.pallas_call(
        functools.partial(mix_kernel, heads, head_dim, chans // heads, blocks, part, skip),
        grid_spec=pltpu.PrefetchScalarGridSpec(
            num_scalar_prefetch=2,
            grid=(steps,),
            in_specs=[
                whole(v.shape),
                whole(p.shape),
                whole(scale.shape),
            ]
            + [whole(x.shape) for x in halo]
            + ([] if prev is None else [pl.BlockSpec(memory_space=pl.ANY)]),
            out_specs=pl.BlockSpec((comps, chans, BS), lambda i, *s: (0, 0, at(i, *s))),
            scratch_shapes=[pltpu.VMEM((3 * REACH, comps, chans, BS), BF)] if halo else [],
        ),
        out_shape=jax.ShapeDtypeStruct(v.shape, BF),
        input_output_aliases={} if prev is None else {4 + len(extra): 0},
        compiler_params=params(16),
        cost_estimate=pl.CostEstimate(
            flops=steps * chans * comps * NNB * BS * BS * 2, transcendentals=0,
            bytes_accessed=steps * chans * comps * BS * 8,
        ),
    )(lists, place, v, p, scale, *extra)


SPREAD = 2 * KMAX + 1
WIDE = 16


def wave(turns):
    r = turns - jnp.round(turns)
    u = r * r
    return horner(COS, u), horner(SIN, u) * r


def grid_points(base, planes):
    rows = planes * SPREAD * WIDE
    place = lax.broadcasted_iota(jnp.int32, (1, rows), 1).astype(F32)
    pair = jnp.floor((place + 0.5) * (1.0 / WIDE))
    n3 = place - pair * WIDE - KMAX
    plane = jnp.floor((pair + 0.5) * (1.0 / SPREAD))
    return plane + base.astype(F32), pair - plane * SPREAD - KMAX, n3


def grid_weights(n, base, planes):
    pairs = planes * SPREAD
    high = -(-pairs // 16) * 16
    flip = jnp.where(n[0:1] < 0, -1, 1)
    pair = (n[0:1] * flip - base) * SPREAD + n[1:2] * flip + KMAX
    mine = (n[0:1] * flip >= base) & (n[0:1] * flip < base + planes)
    third = n[2:3] * flip + KMAX
    count = n.shape[1]
    is_pair = (lax.broadcasted_iota(jnp.int32, (high, count), 0) == pair) & mine
    is_third = lax.broadcasted_iota(jnp.int32, (WIDE, count), 0) == third
    one_hot = lambda x: jnp.where(x, 1.0, 0.0).astype(BF)
    found = dot(one_hot(is_pair), one_hot(is_third), ((1,), (1,)))
    rows = pairs * WIDE
    row = lax.broadcasted_iota(jnp.int32, (WIDE, rows), 0)
    spread = one_hot((lax.broadcasted_iota(jnp.int32, (WIDE, rows), 1) & (WIDE - 1)) == row)
    wide = sum(dot(part, spread, ((1,), (0,))) for part in thirds(found))
    own = lax.broadcasted_iota(jnp.int32, (high, rows), 1) >> (WIDE.bit_length() - 1)
    times = jnp.sum(jnp.where(own == lax.broadcasted_iota(jnp.int32, (high, rows), 0), wide, 0.0), axis=0, keepdims=True)
    n1, n2, n3 = grid_points(base, planes)
    norm = n1 * n1 + n2 * n2 + n3 * n3
    safe = jnp.maximum(norm, 1.0)
    return jnp.where(norm > 0, times * (ewald_scale * jnp.exp(-ewald_damp * safe) / safe), 0.0)


def table_kernel(planes, place, n_ref, f_ref, out_ref, weight_ref, pairs):
    base = place[1] * planes

    @pl.when(pl.program_id(0) == 0)
    def _():
        weight_ref[...] = grid_weights(n_ref[...], base, planes)

    atoms = f_ref.shape[1]
    wide = lax.broadcasted_iota(jnp.int32, (WIDE, atoms), 0)
    steps = (wide - KMAX).astype(F32)
    second = wave(steps * f_ref[1:2, :])
    third = wave(steps * f_ref[2:3, :])
    for plane in range(planes):
        first = wave((base + plane).astype(F32) * f_ref[0:1, :])
        pairs[0, plane] = first[0] * second[0] - first[1] * second[1]
        pairs[1, plane] = first[1] * second[0] + first[0] * second[1]
        for m in range(SPREAD):
            real, imag = pairs[0, plane, m : m + 1, :], pairs[1, plane, m : m + 1, :]
            at = slice((plane * SPREAD + m) * WIDE, (plane * SPREAD + m + 1) * WIDE)
            out_ref[0, at, :] = (real * third[0] - imag * third[1]).astype(BF)
            out_ref[1, at, :] = (imag * third[0] + real * third[1]).astype(BF)


def table_call(place, n, f, planes):
    rows = planes * SPREAD * WIDE
    atoms = f.shape[1]
    step = 256
    return pl.pallas_call(
        functools.partial(table_kernel, planes),
        grid_spec=pltpu.PrefetchScalarGridSpec(
            num_scalar_prefetch=1,
            grid=(atoms // step,),
            in_specs=[
                pl.BlockSpec(n.shape, lambda i, place: (0, 0), pipeline_mode=pl.Buffered(1)),
                pl.BlockSpec((3, step), lambda i, place: (0, i)),
            ],
            out_specs=[
                pl.BlockSpec((2, rows, step), lambda i, place: (0, 0, i)),
                pl.BlockSpec((1, rows), lambda i, place: (0, 0)),
            ],
            scratch_shapes=[pltpu.VMEM((2, planes, WIDE, step), F32)],
        ),
        out_shape=[jax.ShapeDtypeStruct((2, rows, atoms), BF), jax.ShapeDtypeStruct((1, rows), F32)],
        compiler_params=params(12),
        cost_estimate=pl.CostEstimate(flops=rows * atoms * 40, transcendentals=0, bytes_accessed=rows * atoms * 4),
        name="table",
    )(place, n, f)


def structure_kernel(inv_root, c_ref, t_ref, out_ref):
    high, low = halves(c_ref[...])
    both = jnp.concatenate([high, low], axis=0)
    s = dot(t_ref[...], both, ((1,), (1,)))
    nq = c_ref.shape[0]
    out_ref[...] = (s[:, :nq] + s[:, nq:]).T * inv_root


def structure_call(c, table, inv_root):
    rows, atoms = table.shape
    step = rows
    nq = c.shape[0]
    return pl.pallas_call(
        functools.partial(structure_kernel, inv_root),
        grid=(rows // step,),
        in_specs=[pl.BlockSpec((nq, atoms), lambda i: (0, 0)), pl.BlockSpec((step, atoms), lambda i: (i, 0))],
        out_specs=pl.BlockSpec((nq, step), lambda i: (0, i)),
        out_shape=jax.ShapeDtypeStruct((nq, rows), F32),
        compiler_params=params(12),
        cost_estimate=pl.CostEstimate(flops=rows * atoms * 512, transcendentals=0, bytes_accessed=rows * atoms * 2),
        name="structure",
    )(c, table)


def field_kernel(planes, place, s_ref, weight_ref, c_ref, t_ref, out_ref, coeff):
    nq = c_ref.shape[0]
    waves = weight_ref.shape[1]

    @pl.when(pl.program_id(0) == 0)
    def _():
        n = grid_points(place[1] * planes, planes)
        real = s_ref[:, :waves] * weight_ref[...]
        imag = s_ref[:, waves:] * weight_ref[...]
        with_cos = jnp.concatenate([real] + [-imag * n[d] for d in range(3)], axis=0)
        with_sin = jnp.concatenate([imag] + [real * n[d] for d in range(3)], axis=0)
        for part, x in enumerate((with_cos, with_sin)):
            high, low = halves(x)
            coeff[part, 0 : 4 * nq] = high
            coeff[part, 4 * nq :] = low

    both = dot(coeff[0], t_ref[0], ((1,), (0,))) + dot(coeff[1], t_ref[1], ((1,), (0,)))
    sums = both[: 4 * nq] + both[4 * nq :]
    c = c_ref[...]
    out_ref[0:nq, :] = sums[:nq]
    forces = [
        jnp.sum(c * sums[(d + 1) * nq : (d + 2) * nq], axis=0, keepdims=True) for d in range(3)
    ]
    out_ref[nq : nq + 8, :] = jnp.concatenate(forces + [jnp.zeros((5, c.shape[1]), F32)], axis=0)


def field_call(place, s, weight, c, table, planes):
    _, rows, atoms = table.shape
    step = 512
    nq = c.shape[0]
    return pl.pallas_call(
        functools.partial(field_kernel, planes),
        grid_spec=pltpu.PrefetchScalarGridSpec(
            num_scalar_prefetch=1,
            grid=(atoms // step,),
            in_specs=[
                pl.BlockSpec(s.shape, lambda i, place: (0, 0)),
                pl.BlockSpec(weight.shape, lambda i, place: (0, 0)),
                pl.BlockSpec((nq, step), lambda i, place: (0, i)),
                pl.BlockSpec((2, rows, step), lambda i, place: (0, 0, i)),
            ],
            out_specs=pl.BlockSpec((nq + 8, step), lambda i, place: (0, i)),
            scratch_shapes=[pltpu.VMEM((2, 8 * nq, rows), BF)],
        ),
        out_shape=jax.ShapeDtypeStruct((nq + 8, atoms), F32),
        compiler_params=params(12),
        cost_estimate=pl.CostEstimate(flops=rows * atoms * 512, transcendentals=0, bytes_accessed=rows * atoms * 2),
        name="fields",
    )(place, s, weight, c, table)


def finish_kernel(mine_ref, theirs_ref, potential_ref, force_ref):
    nq = potential_ref.shape[0]
    potential_ref[...] = mine_ref[0:nq] + theirs_ref[0:nq]
    force_ref[...] = (mine_ref[nq : nq + 8] + theirs_ref[nq : nq + 8])[:3]


def finish_call(mine, theirs, nq):
    atoms = mine.shape[1]
    return pl.pallas_call(
        finish_kernel,
        out_shape=[jax.ShapeDtypeStruct((nq, atoms), F32), jax.ShapeDtypeStruct((3, atoms), F32)],
        compiler_params=pltpu.CompilerParams(vmem_limit_bytes=4 << 20),
        name="finish",
    )(mine, theirs)


def exchanged(x, axis, step):
    size = lax.axis_size(axis)
    if step >= size:
        return x
    return x + lax.ppermute(x, axis, [(i, i ^ step) for i in range(size)])


def summed(x, axis, step=1, stop=None):
    size = lax.axis_size(axis)
    assert size & (size - 1) == 0
    while step < (stop or size):
        x = exchanged(x, axis, step)
        step *= 2
    return x


def whole_step(
    queries,
    key_states,
    value_states,
    fractional,
    block_counts,
    neighbors,
    integer_wave_vectors,
    charge_weight,
):
    heads, head_dim, atoms = queries.shape
    nq = charge_weight.shape[1]
    planes = (KMAX + 1) // lax.axis_size("inner")
    assert planes * lax.axis_size("inner") == KMAX + 1
    inv_root = 1.0 / math.sqrt(atoms * lax.axis_size("seq"))
    place = jnp.stack([lax.axis_index("seq"), lax.axis_index("inner")]).astype(jnp.int32)
    width = REACH * BS
    count = lax.axis_size("seq")
    near_pairs = [(i, i ^ 1) for i in range(count)]
    far_pairs = [(i, i + 1 if i % 2 else i - 1) for i in range(1, count - 1)]

    def swap(x, pairs):
        return lax.ppermute(x, "seq", pairs)

    values = value_states.transpose(1, 0, 2)
    near, far, near_big, far_big, v0, keys, asked, weight, counts, lists, vectors = load_call(
        place, key_states.reshape(heads * head_dim, atoms), values,
        (queries.reshape(heads * head_dim, atoms), charge_weight.T, block_counts, neighbors.T, integer_wave_vectors),
        width,
    )
    far = swap(far, far_pairs)
    near = swap(near, near_pairs)
    far_big = swap(far_big, far_pairs)
    near_big = swap(near_big, near_pairs)

    p_in, scale_in, part = scores_call(
        "interior", lists, counts, place, asked, keys, v0, weight, (), heads, head_dim
    )
    p_out, scale_out, part = scores_call(
        "edges", lists, counts, place, asked, keys, v0, weight, (far, near, part), heads, head_dim
    )
    table, wave_weight = table_call(place, vectors, fractional, planes)
    charges = summed(part, "inner")
    structure = structure_call(charges, table.reshape(-1, atoms), inv_root)
    structure = summed(structure, "seq")
    fields = field_call(place, structure, wave_weight, charges, table, planes)
    last = lax.axis_size("inner") // 2
    fields = summed(fields, "inner", stop=last)
    others = lax.ppermute(fields, "inner", [(i, i ^ last) for i in range(2 * last)])
    potential, forces = finish_call(fields, others, nq)

    mix = functools.partial(mix_call, heads=heads, head_dim=head_dim)
    attention = mix("low", lists, place, values, p_in, scale_in, (), None)
    attention = mix("high", lists, place, values, p_in, scale_in, (), attention)
    attention = mix("far", lists, place, values, p_out, scale_out, (far, far_big), attention)
    attention = mix("near", lists, place, values, p_out, scale_out, (near, near_big), attention)
    return (attention.transpose(1, 0, 2), potential, forces)


def solution(mesh):
    placed = (
        P("inner", None, "seq"),
        P("inner", None, "seq"),
        P("inner", None, "seq"),
        P(None, "seq"),
        P(),
        P("seq", None),
        P(),
        P("inner", None),
    )
    return jax.shard_map(
        whole_step,
        mesh=mesh,
        in_specs=placed,
        out_specs=(P("inner", None, "seq"), P(None, "seq"), P(None, "seq")),
        check_vma=False,
    )
```

```python
import functools
import math

import jax
import jax.numpy as jnp
from jax import lax
from jax.experimental import pallas as pl
from jax.experimental.pallas import tpu as pltpu
from jax.sharding import PartitionSpec as P


BS = 256
NNB = 3
REACH = 2
KMAX = 7
LOG2E = 1.4426950408889634

ewald_scale = 40.0
ewald_damp = 0.02

BF = jnp.bfloat16
F32 = jnp.float32

SIN = (6.283185302511499, -41.34170040531678, 81.60513138577247, -76.70301535353673,
       42.02592698394968, -14.899846662448152, 3.2381375038938693)
COS = (0.9999999890590217, -19.73920449945376, 64.93911745989128, -85.45013953083522,
       60.167630950695504, -25.967599247822193, 6.5286581606558824)


def params(mib):
    return pltpu.CompilerParams(vmem_limit_bytes=mib << 20, dimension_semantics=("arbitrary",))


def dot(a, b, dims):
    return lax.dot_general(a, b, (dims, ((), ())), preferred_element_type=F32)


def horner(coeffs, u):
    total = coeffs[-1]
    for c in coeffs[-2::-1]:
        total = total * u + c
    return total


def halves(x):
    high = x.astype(BF)
    return high, (x - high.astype(F32)).astype(BF)


def thirds(x):
    high, low = halves(x)
    return high, low, ((x - high.astype(F32)) - low.astype(F32)).astype(BF)


def load_kernel(chans, rows, width, place, *refs):
    (k, v, others), (near, far, near_big, far_big, v0, *copies) = (refs[0], refs[1], refs[2:7]), refs[7:-1]
    sems = refs[-1]
    atoms = v.shape[2]
    even = place[0] % 2 == 0
    last = atoms - width
    near_cols = pl.ds(pl.multiple_of(jnp.where(even, last, 0), 128), width)
    far_cols = pl.ds(pl.multiple_of(jnp.where(even, 0, last), 128), width)
    moves = []
    for piece, cols in ((far, far_cols), (near, near_cols)):
        moves.append((k.at[:, cols], piece.at[pl.ds(0, rows)]))
        moves.append((v.at[0, :, cols], piece.at[pl.ds(rows, chans)]))
    moves.append((k, copies[0]))
    moves.append((v.at[0], v0))
    moves += list(zip(others, copies[1:]))
    for piece, cols in ((far_big, far_cols), (near_big, near_cols)):
        moves.append((v.at[pl.ds(1, piece.shape[0]), :, cols], piece))
    started = [pltpu.make_async_copy(src, dst, sems.at[i]) for i, (src, dst) in enumerate(moves)]
    for copy in started:
        copy.start()
    for copy in started:
        copy.wait()


def load_call(place, k, v, others, width):
    comps, chans, atoms = v.shape
    rows = k.shape[0]
    shape = jax.ShapeDtypeStruct
    outs = [shape((rows + chans, width), BF)] * 2 + [shape((comps - 1, chans, width), BF)] * 2
    outs += [shape((chans, atoms), BF)] + [shape(x.shape, x.dtype) for x in (k, *others)]
    return pl.pallas_call(
        functools.partial(load_kernel, chans, rows, width),
        grid_spec=pltpu.PrefetchScalarGridSpec(
            num_scalar_prefetch=1,
            grid=(1,),
            in_specs=[pl.BlockSpec(memory_space=pltpu.HBM)] * (2 + len(others)),
            out_specs=[pl.BlockSpec(memory_space=pl.ANY)] * len(outs),
            scratch_shapes=[pltpu.SemaphoreType.DMA((8 + len(others),))],
        ),
        out_shape=outs,
        compiler_params=params(2),
        cost_estimate=pl.CostEstimate(flops=0, transcendentals=0, bytes_accessed=4 * comps * chans * width),
        name="load",
    )(place, *[pltpu.with_memory_space_constraint(x, pltpu.HBM) for x in (k, v, *others)])


def on_left(place, far):
    even = place[0] % 2 == 0
    return even if far else jnp.logical_not(even)


def edge_block(step, place, blocks):
    left = (step < REACH) == (place[0] % 2 == 0)
    return step % REACH + jnp.where(left, 0, blocks - REACH)


def score_kernel(heads, head_dim, head_chan, blocks, part, lists, counts, place, *refs):
    q_ref, k_ref, v_ref, cw_ref = refs[:4]
    sides, (p_ref, scale_ref, charge_ref, kaug, v0) = refs[4:-5], refs[-5:]
    first = place[0] * blocks
    total = counts.shape[0]
    lane = lax.broadcasted_iota(jnp.int32, (16, BS), 1)
    row = lax.broadcasted_iota(jnp.int32, (16, BS), 0)
    top_row = jnp.where(row == 0, 1.0, 0.0).astype(BF)

    def fill(b, keys, values):
        index = first + b - REACH
        inside = (index >= 0) & (index < total)
        live = jnp.where(inside, counts[jnp.clip(index, 0, total - 1)], 0)
        bias = jnp.where((row == 0) & (lane >= live), -1e30, 0.0).astype(BF)
        for h in range(heads):
            for copy in range(3):
                kaug[b, h, copy * head_dim : (copy + 1) * head_dim, :] = keys[h * head_dim : (h + 1) * head_dim]
            kaug[b, h, 3 * head_dim : 3 * head_dim + 16, :] = bias
            v0[b, h, 0:head_chan] = values[h * head_chan : (h + 1) * head_chan]
            v0[b, h, head_chan : head_chan + 16] = top_row

    for b in range(blocks):
        cols = slice(b * BS, (b + 1) * BS)
        fill(b + REACH, k_ref[:, cols], v_ref[:, cols])
    if sides:
        for far, side in zip((True, False), sides[:2]):
            base = jnp.where(on_left(place, far), 0, blocks + REACH)
            for b in range(REACH):
                cols = slice(b * BS, (b + 1) * BS)
                fill(base + b, side[0 : heads * head_dim, cols], side[heads * head_dim :, cols])
        inner = slice(REACH * BS, (blocks - REACH) * BS)
        charge_ref[:, inner] = sides[2][:, inner]
    else:
        charge_ref[...] = jnp.zeros_like(charge_ref)

    def block_of(i):
        return i + REACH if part == "interior" else edge_block(i, place, blocks)

    def columns(g):
        return pl.ds(pl.multiple_of(g * BS, BS), BS)

    def scores_of(i, h):
        g = block_of(i)
        listed = [lists[e, g] - (first - REACH) for e in range(NNB)]
        q = q_ref[h * head_dim : (h + 1) * head_dim, columns(g)].astype(F32) * (head_dim ** (-0.5) * LOG2E)
        qa = jnp.concatenate([*thirds(q), top_row], axis=0)
        return listed, [dot(kaug[b, h], qa, ((0,), (0,))) for b in listed]

    steps = p_ref.shape[0]
    pairs = [(i, h) for i in range(steps) for h in range(heads)]
    coming = scores_of(*pairs[0])
    charge = None
    for at, (i, h) in enumerate(pairs):
        listed, scores = coming
        if at + 1 < len(pairs):
            coming = scores_of(*pairs[at + 1])
        g = block_of(i)
        top = functools.reduce(jnp.maximum, [jnp.max(s, axis=0, keepdims=True) for s in scores])
        mixed = 0.0
        for e, b in enumerate(listed):
            w16 = jnp.exp2(scores[e] - top).astype(BF)
            p_ref[i, h, e * BS : (e + 1) * BS, :] = w16
            mixed = mixed + dot(v0[b, h], w16, ((1,), (0,)))
        live_q = lane[0:1] < counts[first + g]
        scale = jnp.where(live_q, 1.0 / mixed[head_chan : head_chan + 1], 0.0)
        scale_ref[i, h : h + 1, :] = scale
        att0 = (mixed[:head_chan] * scale).astype(BF)
        term = dot(cw_ref[:, h * head_chan : (h + 1) * head_chan], att0, ((1,), (0,)))
        charge = term if h == 0 else charge + term
        if h == heads - 1:
            charge_ref[:, columns(g)] = charge


def scores_call(part, lists, counts, place, q, k, v0, cw, sides, heads, head_dim):
    chans, atoms = v0.shape
    blocks = atoms // BS
    nq = cw.shape[0]
    head_chan = chans // heads
    band = blocks + 2 * REACH
    steps = blocks - 2 * REACH if part == "interior" else 2 * REACH
    whole = lambda shape: pl.BlockSpec(shape, lambda g, *_: (0,) * len(shape), pipeline_mode=pl.Buffered(1))
    shapes = [((steps, heads, NNB * BS, BS), BF), ((steps, heads, BS), F32), ((nq, atoms), F32)]
    return pl.pallas_call(
        functools.partial(score_kernel, heads, head_dim, head_chan, blocks, part),
        grid_spec=pltpu.PrefetchScalarGridSpec(
            num_scalar_prefetch=3,
            grid=(1,),
            in_specs=[whole(x.shape) for x in (q, k, v0, cw, *sides)],
            out_specs=[whole(shape) for shape, _ in shapes],
            scratch_shapes=[
                pltpu.VMEM((band, heads, 3 * head_dim + 16, BS), BF),
                pltpu.VMEM((band, heads, head_chan + 16, BS), BF),
            ],
        ),
        out_shape=[jax.ShapeDtypeStruct(*x) for x in shapes],
        compiler_params=params(16),
        cost_estimate=pl.CostEstimate(
            flops=steps * heads * NNB * BS * BS * 200, transcendentals=steps * heads * NNB * BS * BS,
            bytes_accessed=steps * heads * NNB * BS * BS * 2,
        ),
    )(lists, counts, place, q, k, v0, cw, *sides)


def mix_kernel(heads, head_dim, head_chan, blocks, part, skip, lists, place, v_ref, p_ref, scale_ref, *refs):
    halo, out_ref = refs[: 2 if part in ("far", "near") else 0], refs[-2 if part in ("far", "near") else -1]
    comps = v_ref.shape[0]
    i = pl.program_id(0)
    offset = place[0] * blocks
    if halo:
        small, big = halo
        band = refs[-1]
        span = 3 * REACH
        left = on_left(place, part == "far")
        begin = jnp.where(left, 0, blocks + 2 * REACH - span)

        @pl.when(i == 0)
        def _():
            own = jnp.where(left, REACH, 0)
            first = jnp.where(left, 0, blocks - 2 * REACH)
            for b in range(2 * REACH):
                band[own + b] = v_ref[:, :, pl.ds(pl.multiple_of((first + b) * BS, BS), BS)]
            other = jnp.where(left, 0, 2 * REACH)
            for b in range(REACH):
                cols = slice(b * BS, (b + 1) * BS)
                band[other + b, 0] = small[heads * head_dim :, cols]
                band[other + b, 1:] = big[:, :, cols]

        g = edge_block(i if part == "far" else i + REACH, place, blocks)
        listed = [lists[e, g] - offset + REACH - begin for e in range(NNB)]
        pick = lambda b, rows: band[b, :, rows, :]
    else:
        g = i + (REACH if part == "low" else blocks // 2)
        listed = [lists[e, g] - offset for e in range(NNB)]
        pick = lambda b, rows: v_ref[:, rows, pl.ds(pl.multiple_of(b * BS, BS), BS)]
    for h in range(heads):
        rows = slice(h * head_chan, (h + 1) * head_chan)
        acc = 0.0
        for e in range(NNB):
            v = pick(listed[e], rows).reshape(comps * head_chan, BS)
            acc = acc + dot(v, p_ref[i + skip, h, e * BS : (e + 1) * BS, :], ((1,), (0,)))
        acc = acc * scale_ref[i + skip, h : h + 1, :]
        out_ref[:, rows, :] = acc.astype(BF).reshape(comps, head_chan, BS)


def mix_call(part, lists, place, v, p, scale, halo, prev, heads, head_dim):
    comps, chans, atoms = v.shape
    blocks = atoms // BS
    half = blocks // 2 - REACH
    steps = REACH if halo else half
    skip = {"low": 0, "high": half, "far": 0, "near": REACH}[part]

    def at(i, lists, place):
        if part in ("low", "high"):
            return i + REACH + skip
        return edge_block(i + skip, place, blocks)

    whole = lambda shape: pl.BlockSpec(shape, lambda g, *_: (0,) * len(shape), pipeline_mode=pl.Buffered(1))
    extra = list(halo) + ([] if prev is None else [prev])
    return pl.pallas_call(
        functools.partial(mix_kernel, heads, head_dim, chans // heads, blocks, part, skip),
        grid_spec=pltpu.PrefetchScalarGridSpec(
            num_scalar_prefetch=2,
            grid=(steps,),
            in_specs=[
                whole(v.shape),
                whole(p.shape),
                whole(scale.shape),
            ]
            + [whole(x.shape) for x in halo]
            + ([] if prev is None else [pl.BlockSpec(memory_space=pl.ANY)]),
            out_specs=pl.BlockSpec((comps, chans, BS), lambda i, *s: (0, 0, at(i, *s))),
            scratch_shapes=[pltpu.VMEM((3 * REACH, comps, chans, BS), BF)] if halo else [],
        ),
        out_shape=jax.ShapeDtypeStruct(v.shape, BF),
        input_output_aliases={} if prev is None else {4 + len(extra): 0},
        compiler_params=params(16),
        cost_estimate=pl.CostEstimate(
            flops=steps * chans * comps * NNB * BS * BS * 2, transcendentals=0,
            bytes_accessed=steps * chans * comps * BS * 8,
        ),
    )(lists, place, v, p, scale, *extra)


SPREAD = 2 * KMAX + 1
WIDE = 16


def wave(turns):
    r = turns - jnp.round(turns)
    u = r * r
    return horner(COS, u), horner(SIN, u) * r


def grid_points(base, planes):
    rows = planes * SPREAD * WIDE
    place = lax.broadcasted_iota(jnp.int32, (1, rows), 1).astype(F32)
    pair = jnp.floor((place + 0.5) * (1.0 / WIDE))
    n3 = place - pair * WIDE - KMAX
    plane = jnp.floor((pair + 0.5) * (1.0 / SPREAD))
    return plane + base.astype(F32), pair - plane * SPREAD - KMAX, n3


def grid_weights(n, base, planes):
    pairs = planes * SPREAD
    high = -(-pairs // 16) * 16
    flip = jnp.where(n[0:1] < 0, -1, 1)
    pair = (n[0:1] * flip - base) * SPREAD + n[1:2] * flip + KMAX
    mine = (n[0:1] * flip >= base) & (n[0:1] * flip < base + planes)
    third = n[2:3] * flip + KMAX
    count = n.shape[1]
    is_pair = (lax.broadcasted_iota(jnp.int32, (high, count), 0) == pair) & mine
    is_third = lax.broadcasted_iota(jnp.int32, (WIDE, count), 0) == third
    one_hot = lambda x: jnp.where(x, 1.0, 0.0).astype(BF)
    found = dot(one_hot(is_pair), one_hot(is_third), ((1,), (1,)))
    rows = pairs * WIDE
    row = lax.broadcasted_iota(jnp.int32, (WIDE, rows), 0)
    spread = one_hot((lax.broadcasted_iota(jnp.int32, (WIDE, rows), 1) & (WIDE - 1)) == row)
    wide = sum(dot(part, spread, ((1,), (0,))) for part in thirds(found))
    own = lax.broadcasted_iota(jnp.int32, (high, rows), 1) >> (WIDE.bit_length() - 1)
    times = jnp.sum(jnp.where(own == lax.broadcasted_iota(jnp.int32, (high, rows), 0), wide, 0.0), axis=0, keepdims=True)
    n1, n2, n3 = grid_points(base, planes)
    norm = n1 * n1 + n2 * n2 + n3 * n3
    safe = jnp.maximum(norm, 1.0)
    return jnp.where(norm > 0, times * (ewald_scale * jnp.exp(-ewald_damp * safe) / safe), 0.0)


def table_kernel(planes, place, n_ref, f_ref, out_ref, weight_ref, pairs):
    base = place[1] * planes

    @pl.when(pl.program_id(0) == 0)
    def _():
        weight_ref[...] = grid_weights(n_ref[...], base, planes)

    atoms = f_ref.shape[1]
    wide = lax.broadcasted_iota(jnp.int32, (WIDE, atoms), 0)
    steps = (wide - KMAX).astype(F32)
    second = wave(steps * f_ref[1:2, :])
    third = wave(steps * f_ref[2:3, :])
    for plane in range(planes):
        first = wave((base + plane).astype(F32) * f_ref[0:1, :])
        pairs[0, plane] = first[0] * second[0] - first[1] * second[1]
        pairs[1, plane] = first[1] * second[0] + first[0] * second[1]
        for m in range(SPREAD):
            real, imag = pairs[0, plane, m : m + 1, :], pairs[1, plane, m : m + 1, :]
            at = slice((plane * SPREAD + m) * WIDE, (plane * SPREAD + m + 1) * WIDE)
            out_ref[0, at, :] = (real * third[0] - imag * third[1]).astype(BF)
            out_ref[1, at, :] = (imag * third[0] + real * third[1]).astype(BF)


def table_call(place, n, f, planes):
    rows = planes * SPREAD * WIDE
    atoms = f.shape[1]
    step = 256
    return pl.pallas_call(
        functools.partial(table_kernel, planes),
        grid_spec=pltpu.PrefetchScalarGridSpec(
            num_scalar_prefetch=1,
            grid=(atoms // step,),
            in_specs=[
                pl.BlockSpec(n.shape, lambda i, place: (0, 0), pipeline_mode=pl.Buffered(1)),
                pl.BlockSpec((3, step), lambda i, place: (0, i)),
            ],
            out_specs=[
                pl.BlockSpec((2, rows, step), lambda i, place: (0, 0, i)),
                pl.BlockSpec((1, rows), lambda i, place: (0, 0)),
            ],
            scratch_shapes=[pltpu.VMEM((2, planes, WIDE, step), F32)],
        ),
        out_shape=[jax.ShapeDtypeStruct((2, rows, atoms), BF), jax.ShapeDtypeStruct((1, rows), F32)],
        compiler_params=params(12),
        cost_estimate=pl.CostEstimate(flops=rows * atoms * 40, transcendentals=0, bytes_accessed=rows * atoms * 4),
        name="table",
    )(place, n, f)


def structure_kernel(inv_root, c_ref, t_ref, out_ref):
    high, low = halves(c_ref[...])
    both = jnp.concatenate([high, low], axis=0)
    s = dot(t_ref[...], both, ((1,), (1,)))
    nq = c_ref.shape[0]
    out_ref[...] = (s[:, :nq] + s[:, nq:]).T * inv_root


def structure_call(c, table, inv_root):
    rows, atoms = table.shape
    step = rows
    nq = c.shape[0]
    return pl.pallas_call(
        functools.partial(structure_kernel, inv_root),
        grid=(rows // step,),
        in_specs=[pl.BlockSpec((nq, atoms), lambda i: (0, 0)), pl.BlockSpec((step, atoms), lambda i: (i, 0))],
        out_specs=pl.BlockSpec((nq, step), lambda i: (0, i)),
        out_shape=jax.ShapeDtypeStruct((nq, rows), F32),
        compiler_params=params(12),
        cost_estimate=pl.CostEstimate(flops=rows * atoms * 512, transcendentals=0, bytes_accessed=rows * atoms * 2),
        name="structure",
    )(c, table)


def field_kernel(planes, place, s_ref, weight_ref, c_ref, t_ref, out_ref, coeff):
    nq = c_ref.shape[0]
    waves = weight_ref.shape[1]

    @pl.when(pl.program_id(0) == 0)
    def _():
        n = grid_points(place[1] * planes, planes)
        real = s_ref[:, :waves] * weight_ref[...]
        imag = s_ref[:, waves:] * weight_ref[...]
        with_cos = jnp.concatenate([real] + [-imag * n[d] for d in range(3)], axis=0)
        with_sin = jnp.concatenate([imag] + [real * n[d] for d in range(3)], axis=0)
        for part, x in enumerate((with_cos, with_sin)):
            high, low = halves(x)
            coeff[part, 0 : 4 * nq] = high
            coeff[part, 4 * nq :] = low

    both = dot(coeff[0], t_ref[0], ((1,), (0,))) + dot(coeff[1], t_ref[1], ((1,), (0,)))
    sums = both[: 4 * nq] + both[4 * nq :]
    c = c_ref[...]
    out_ref[0:nq, :] = sums[:nq]
    forces = [
        jnp.sum(c * sums[(d + 1) * nq : (d + 2) * nq], axis=0, keepdims=True) for d in range(3)
    ]
    out_ref[nq : nq + 8, :] = jnp.concatenate(forces + [jnp.zeros((5, c.shape[1]), F32)], axis=0)


def field_call(place, s, weight, c, table, planes):
    _, rows, atoms = table.shape
    step = 512
    nq = c.shape[0]
    return pl.pallas_call(
        functools.partial(field_kernel, planes),
        grid_spec=pltpu.PrefetchScalarGridSpec(
            num_scalar_prefetch=1,
            grid=(atoms // step,),
            in_specs=[
                pl.BlockSpec(s.shape, lambda i, place: (0, 0)),
                pl.BlockSpec(weight.shape, lambda i, place: (0, 0)),
                pl.BlockSpec((nq, step), lambda i, place: (0, i)),
                pl.BlockSpec((2, rows, step), lambda i, place: (0, 0, i)),
            ],
            out_specs=pl.BlockSpec((nq + 8, step), lambda i, place: (0, i)),
            scratch_shapes=[pltpu.VMEM((2, 8 * nq, rows), BF)],
        ),
        out_shape=jax.ShapeDtypeStruct((nq + 8, atoms), F32),
        compiler_params=params(12),
        cost_estimate=pl.CostEstimate(flops=rows * atoms * 512, transcendentals=0, bytes_accessed=rows * atoms * 2),
        name="fields",
    )(place, s, weight, c, table)


def finish_kernel(mine_ref, theirs_ref, potential_ref, force_ref):
    nq = potential_ref.shape[0]
    potential_ref[...] = mine_ref[0:nq] + theirs_ref[0:nq]
    force_ref[...] = (mine_ref[nq : nq + 8] + theirs_ref[nq : nq + 8])[:3]


def finish_call(mine, theirs, nq):
    atoms = mine.shape[1]
    return pl.pallas_call(
        finish_kernel,
        out_shape=[jax.ShapeDtypeStruct((nq, atoms), F32), jax.ShapeDtypeStruct((3, atoms), F32)],
        compiler_params=pltpu.CompilerParams(vmem_limit_bytes=4 << 20),
        name="finish",
    )(mine, theirs)


def exchanged(x, axis, step):
    size = lax.axis_size(axis)
    if step >= size:
        return x
    return x + lax.ppermute(x, axis, [(i, i ^ step) for i in range(size)])


def summed(x, axis, step=1, stop=None):
    size = lax.axis_size(axis)
    assert size & (size - 1) == 0
    while step < (stop or size):
        x = exchanged(x, axis, step)
        step *= 2
    return x


def whole_step(
    queries,
    key_states,
    value_states,
    fractional,
    block_counts,
    neighbors,
    integer_wave_vectors,
    charge_weight,
):
    heads, head_dim, atoms = queries.shape
    nq = charge_weight.shape[1]
    planes = (KMAX + 1) // lax.axis_size("inner")
    assert planes * lax.axis_size("inner") == KMAX + 1
    inv_root = 1.0 / math.sqrt(atoms * lax.axis_size("seq"))
    place = jnp.stack([lax.axis_index("seq"), lax.axis_index("inner")]).astype(jnp.int32)
    width = REACH * BS
    count = lax.axis_size("seq")
    near_pairs = [(i, i ^ 1) for i in range(count)]
    far_pairs = [(i, i + 1 if i % 2 else i - 1) for i in range(1, count - 1)]

    def swap(x, pairs):
        return lax.ppermute(x, "seq", pairs)

    values = value_states.transpose(1, 0, 2)
    near, far, near_big, far_big, v0, keys, asked, weight, counts, lists, vectors = load_call(
        place, key_states.reshape(heads * head_dim, atoms), values,
        (queries.reshape(heads * head_dim, atoms), charge_weight.T, block_counts, neighbors.T, integer_wave_vectors),
        width,
    )
    far = swap(far, far_pairs)
    near = swap(near, near_pairs)
    far_big = swap(far_big, far_pairs)
    near_big = swap(near_big, near_pairs)

    p_in, scale_in, part = scores_call(
        "interior", lists, counts, place, asked, keys, v0, weight, (), heads, head_dim
    )
    p_out, scale_out, part = scores_call(
        "edges", lists, counts, place, asked, keys, v0, weight, (far, near, part), heads, head_dim
    )
    table, wave_weight = table_call(place, vectors, fractional, planes)
    charges = summed(part, "inner")
    structure = structure_call(charges, table.reshape(-1, atoms), inv_root)
    structure = summed(structure, "seq")
    fields = field_call(place, structure, wave_weight, charges, table, planes)
    last = lax.axis_size("inner") // 2
    fields = summed(fields, "inner", stop=last)
    others = lax.ppermute(fields, "inner", [(i, i ^ last) for i in range(2 * last)])
    potential, forces = finish_call(fields, others, nq)

    mix = functools.partial(mix_call, heads=heads, head_dim=head_dim)
    attention = mix("low", lists, place, values, p_in, scale_in, (), None)
    attention = mix("high", lists, place, values, p_in, scale_in, (), attention)
    attention = mix("far", lists, place, values, p_out, scale_out, (far, far_big), attention)
    attention = mix("near", lists, place, values, p_out, scale_out, (near, near_big), attention)
    return (attention.transpose(1, 0, 2), potential, forces)


def solution(mesh):
    placed = (
        P("inner", None, "seq"),
        P("inner", None, "seq"),
        P("inner", None, "seq"),
        P(None, "seq"),
        P(),
        P("seq", None),
        P(),
        P("inner", None),
    )
    return jax.shard_map(
        whole_step,
        mesh=mesh,
        in_specs=placed,
        out_specs=(P("inner", None, "seq"), P(None, "seq"), P(None, "seq")),
        check_vma=False,
    )
```

```python
import functools
import math

import jax
import jax.numpy as jnp
from jax import lax
from jax.experimental import pallas as pl
from jax.experimental.pallas import tpu as pltpu
from jax.sharding import PartitionSpec as P


BS = 256
NNB = 3
REACH = 2
KMAX = 7
LOG2E = 1.4426950408889634

ewald_scale = 40.0
ewald_damp = 0.02

BF = jnp.bfloat16
F32 = jnp.float32

SIN = (6.283185302511499, -41.34170040531678, 81.60513138577247, -76.70301535353673,
       42.02592698394968, -14.899846662448152, 3.2381375038938693)
COS = (0.9999999890590217, -19.73920449945376, 64.93911745989128, -85.45013953083522,
       60.167630950695504, -25.967599247822193, 6.5286581606558824)


def params(mib):
    return pltpu.CompilerParams(vmem_limit_bytes=mib << 20, dimension_semantics=("arbitrary",))


def dot(a, b, dims):
    return lax.dot_general(a, b, (dims, ((), ())), preferred_element_type=F32)


def horner(coeffs, u):
    total = coeffs[-1]
    for c in coeffs[-2::-1]:
        total = total * u + c
    return total


def halves(x):
    high = x.astype(BF)
    return high, (x - high.astype(F32)).astype(BF)


def thirds(x):
    high, low = halves(x)
    return high, low, ((x - high.astype(F32)) - low.astype(F32)).astype(BF)


def load_kernel(chans, rows, width, place, *refs):
    (k, v, others), (near, far, near_big, far_big, v0, *copies) = (refs[0], refs[1], refs[2:7]), refs[7:-1]
    sems = refs[-1]
    atoms = v.shape[2]
    even = place[0] % 2 == 0
    last = atoms - width
    near_cols = pl.ds(pl.multiple_of(jnp.where(even, last, 0), 128), width)
    far_cols = pl.ds(pl.multiple_of(jnp.where(even, 0, last), 128), width)
    moves = []
    for piece, cols in ((far, far_cols), (near, near_cols)):
        moves.append((k.at[:, cols], piece.at[pl.ds(0, rows)]))
        moves.append((v.at[0, :, cols], piece.at[pl.ds(rows, chans)]))
    moves.append((k, copies[0]))
    moves.append((v.at[0], v0))
    moves += list(zip(others, copies[1:]))
    for piece, cols in ((far_big, far_cols), (near_big, near_cols)):
        moves.append((v.at[pl.ds(1, piece.shape[0]), :, cols], piece))
    started = [pltpu.make_async_copy(src, dst, sems.at[i]) for i, (src, dst) in enumerate(moves)]
    for copy in started:
        copy.start()
    for copy in started:
        copy.wait()


def load_call(place, k, v, others, width):
    comps, chans, atoms = v.shape
    rows = k.shape[0]
    shape = jax.ShapeDtypeStruct
    outs = [shape((rows + chans, width), BF)] * 2 + [shape((comps - 1, chans, width), BF)] * 2
    outs += [shape((chans, atoms), BF)] + [shape(x.shape, x.dtype) for x in (k, *others)]
    return pl.pallas_call(
        functools.partial(load_kernel, chans, rows, width),
        grid_spec=pltpu.PrefetchScalarGridSpec(
            num_scalar_prefetch=1,
            grid=(1,),
            in_specs=[pl.BlockSpec(memory_space=pltpu.HBM)] * (2 + len(others)),
            out_specs=[pl.BlockSpec(memory_space=pl.ANY)] * len(outs),
            scratch_shapes=[pltpu.SemaphoreType.DMA((8 + len(others),))],
        ),
        out_shape=outs,
        compiler_params=params(2),
        cost_estimate=pl.CostEstimate(flops=0, transcendentals=0, bytes_accessed=4 * comps * chans * width),
        name="load",
    )(place, *[pltpu.with_memory_space_constraint(x, pltpu.HBM) for x in (k, v, *others)])


def on_left(place, far):
    even = place[0] % 2 == 0
    return even if far else jnp.logical_not(even)


def edge_block(step, place, blocks):
    left = (step < REACH) == (place[0] % 2 == 0)
    return step % REACH + jnp.where(left, 0, blocks - REACH)


def score_kernel(heads, head_dim, head_chan, blocks, part, lists, counts, place, *refs):
    q_ref, k_ref, v_ref, cw_ref = refs[:4]
    sides, (p_ref, scale_ref, charge_ref, kaug, v0) = refs[4:-5], refs[-5:]
    first = place[0] * blocks
    total = counts.shape[0]
    lane = lax.broadcasted_iota(jnp.int32, (16, BS), 1)
    row = lax.broadcasted_iota(jnp.int32, (16, BS), 0)
    top_row = jnp.where(row == 0, 1.0, 0.0).astype(BF)

    def fill(b, keys, values):
        index = first + b - REACH
        inside = (index >= 0) & (index < total)
        live = jnp.where(inside, counts[jnp.clip(index, 0, total - 1)], 0)
        bias = jnp.where((row == 0) & (lane >= live), -1e30, 0.0).astype(BF)
        for h in range(heads):
            for copy in range(3):
                kaug[b, h, copy * head_dim : (copy + 1) * head_dim, :] = keys[h * head_dim : (h + 1) * head_dim]
            kaug[b, h, 3 * head_dim : 3 * head_dim + 16, :] = bias
            v0[b, h, 0:head_chan] = values[h * head_chan : (h + 1) * head_chan]
            v0[b, h, head_chan : head_chan + 16] = top_row

    for b in range(blocks):
        cols = slice(b * BS, (b + 1) * BS)
        fill(b + REACH, k_ref[:, cols], v_ref[:, cols])
    if sides:
        for far, side in zip((True, False), sides[:2]):
            base = jnp.where(on_left(place, far), 0, blocks + REACH)
            for b in range(REACH):
                cols = slice(b * BS, (b + 1) * BS)
                fill(base + b, side[0 : heads * head_dim, cols], side[heads * head_dim :, cols])
        inner = slice(REACH * BS, (blocks - REACH) * BS)
        charge_ref[:, inner] = sides[2][:, inner]
    else:
        charge_ref[...] = jnp.zeros_like(charge_ref)

    def block_of(i):
        return i + REACH if part == "interior" else edge_block(i, place, blocks)

    def columns(g):
        return pl.ds(pl.multiple_of(g * BS, BS), BS)

    def scores_of(i, h):
        g = block_of(i)
        listed = [lists[e, g] - (first - REACH) for e in range(NNB)]
        q = q_ref[h * head_dim : (h + 1) * head_dim, columns(g)].astype(F32) * (head_dim ** (-0.5) * LOG2E)
        qa = jnp.concatenate([*thirds(q), top_row], axis=0)
        return listed, [dot(kaug[b, h], qa, ((0,), (0,))) for b in listed]

    steps = p_ref.shape[0]
    pairs = [(i, h) for i in range(steps) for h in range(heads)]
    coming = scores_of(*pairs[0])
    charge = None
    for at, (i, h) in enumerate(pairs):
        listed, scores = coming
        if at + 1 < len(pairs):
            coming = scores_of(*pairs[at + 1])
        g = block_of(i)
        top = functools.reduce(jnp.maximum, [jnp.max(s, axis=0, keepdims=True) for s in scores])
        mixed = 0.0
        for e, b in enumerate(listed):
            w16 = jnp.exp2(scores[e] - top).astype(BF)
            p_ref[i, h, e * BS : (e + 1) * BS, :] = w16
            mixed = mixed + dot(v0[b, h], w16, ((1,), (0,)))
        live_q = lane[0:1] < counts[first + g]
        scale = jnp.where(live_q, 1.0 / mixed[head_chan : head_chan + 1], 0.0)
        scale_ref[i, h : h + 1, :] = scale
        att0 = (mixed[:head_chan] * scale).astype(BF)
        term = dot(cw_ref[:, h * head_chan : (h + 1) * head_chan], att0, ((1,), (0,)))
        charge = term if h == 0 else charge + term
        if h == heads - 1:
            charge_ref[:, columns(g)] = charge


def scores_call(part, lists, counts, place, q, k, v0, cw, sides, heads, head_dim):
    chans, atoms = v0.shape
    blocks = atoms // BS
    nq = cw.shape[0]
    head_chan = chans // heads
    band = blocks + 2 * REACH
    steps = blocks - 2 * REACH if part == "interior" else 2 * REACH
    whole = lambda shape: pl.BlockSpec(shape, lambda g, *_: (0,) * len(shape), pipeline_mode=pl.Buffered(1))
    shapes = [((steps, heads, NNB * BS, BS), BF), ((steps, heads, BS), F32), ((nq, atoms), F32)]
    return pl.pallas_call(
        functools.partial(score_kernel, heads, head_dim, head_chan, blocks, part),
        grid_spec=pltpu.PrefetchScalarGridSpec(
            num_scalar_prefetch=3,
            grid=(1,),
            in_specs=[whole(x.shape) for x in (q, k, v0, cw, *sides)],
            out_specs=[whole(shape) for shape, _ in shapes],
            scratch_shapes=[
                pltpu.VMEM((band, heads, 3 * head_dim + 16, BS), BF),
                pltpu.VMEM((band, heads, head_chan + 16, BS), BF),
            ],
        ),
        out_shape=[jax.ShapeDtypeStruct(*x) for x in shapes],
        compiler_params=params(16),
        cost_estimate=pl.CostEstimate(
            flops=steps * heads * NNB * BS * BS * 200, transcendentals=steps * heads * NNB * BS * BS,
            bytes_accessed=steps * heads * NNB * BS * BS * 2,
        ),
    )(lists, counts, place, q, k, v0, cw, *sides)


def mix_kernel(heads, head_dim, head_chan, blocks, part, skip, lists, place, v_ref, p_ref, scale_ref, *refs):
    halo, out_ref = refs[: 2 if part in ("far", "near") else 0], refs[-2 if part in ("far", "near") else -1]
    comps = v_ref.shape[0]
    i = pl.program_id(0)
    offset = place[0] * blocks
    if halo:
        small, big = halo
        band = refs[-1]
        span = 3 * REACH
        left = on_left(place, part == "far")
        begin = jnp.where(left, 0, blocks + 2 * REACH - span)

        @pl.when(i == 0)
        def _():
            own = jnp.where(left, REACH, 0)
            first = jnp.where(left, 0, blocks - 2 * REACH)
            for b in range(2 * REACH):
                band[own + b] = v_ref[:, :, pl.ds(pl.multiple_of((first + b) * BS, BS), BS)]
            other = jnp.where(left, 0, 2 * REACH)
            for b in range(REACH):
                cols = slice(b * BS, (b + 1) * BS)
                band[other + b, 0] = small[heads * head_dim :, cols]
                band[other + b, 1:] = big[:, :, cols]

        g = edge_block(i if part == "far" else i + REACH, place, blocks)
        listed = [lists[e, g] - offset + REACH - begin for e in range(NNB)]
        pick = lambda b, rows: band[b, :, rows, :]
    else:
        g = i + (REACH if part == "low" else blocks // 2)
        listed = [lists[e, g] - offset for e in range(NNB)]
        pick = lambda b, rows: v_ref[:, rows, pl.ds(pl.multiple_of(b * BS, BS), BS)]
    for h in range(heads):
        rows = slice(h * head_chan, (h + 1) * head_chan)
        acc = 0.0
        for e in range(NNB):
            v = pick(listed[e], rows).reshape(comps * head_chan, BS)
            acc = acc + dot(v, p_ref[i + skip, h, e * BS : (e + 1) * BS, :], ((1,), (0,)))
        acc = acc * scale_ref[i + skip, h : h + 1, :]
        out_ref[:, rows, :] = acc.astype(BF).reshape(comps, head_chan, BS)


def mix_call(part, lists, place, v, p, scale, halo, prev, heads, head_dim):
    comps, chans, atoms = v.shape
    blocks = atoms // BS
    half = blocks // 2 - REACH
    steps = REACH if halo else half
    skip = {"low": 0, "high": half, "far": 0, "near": REACH}[part]

    def at(i, lists, place):
        if part in ("low", "high"):
            return i + REACH + skip
        return edge_block(i + skip, place, blocks)

    whole = lambda shape: pl.BlockSpec(shape, lambda g, *_: (0,) * len(shape), pipeline_mode=pl.Buffered(1))
    extra = list(halo) + ([] if prev is None else [prev])
    return pl.pallas_call(
        functools.partial(mix_kernel, heads, head_dim, chans // heads, blocks, part, skip),
        grid_spec=pltpu.PrefetchScalarGridSpec(
            num_scalar_prefetch=2,
            grid=(steps,),
            in_specs=[
                whole(v.shape),
                whole(p.shape),
                whole(scale.shape),
            ]
            + [whole(x.shape) for x in halo]
            + ([] if prev is None else [pl.BlockSpec(memory_space=pl.ANY)]),
            out_specs=pl.BlockSpec((comps, chans, BS), lambda i, *s: (0, 0, at(i, *s))),
            scratch_shapes=[pltpu.VMEM((3 * REACH, comps, chans, BS), BF)] if halo else [],
        ),
        out_shape=jax.ShapeDtypeStruct(v.shape, BF),
        input_output_aliases={} if prev is None else {4 + len(extra): 0},
        compiler_params=params(16),
        cost_estimate=pl.CostEstimate(
            flops=steps * chans * comps * NNB * BS * BS * 2, transcendentals=0,
            bytes_accessed=steps * chans * comps * BS * 8,
        ),
    )(lists, place, v, p, scale, *extra)


SPREAD = 2 * KMAX + 1
WIDE = 16


def wave(turns):
    r = turns - jnp.round(turns)
    u = r * r
    return horner(COS, u), horner(SIN, u) * r


def grid_points(base, planes):
    rows = planes * SPREAD * WIDE
    place = lax.broadcasted_iota(jnp.int32, (1, rows), 1).astype(F32)
    pair = jnp.floor((place + 0.5) * (1.0 / WIDE))
    n3 = place - pair * WIDE - KMAX
    plane = jnp.floor((pair + 0.5) * (1.0 / SPREAD))
    return plane + base.astype(F32), pair - plane * SPREAD - KMAX, n3


def grid_weights(n, base, planes):
    pairs = planes * SPREAD
    high = -(-pairs // 16) * 16
    flip = jnp.where(n[0:1] < 0, -1, 1)
    pair = (n[0:1] * flip - base) * SPREAD + n[1:2] * flip + KMAX
    mine = (n[0:1] * flip >= base) & (n[0:1] * flip < base + planes)
    third = n[2:3] * flip + KMAX
    count = n.shape[1]
    is_pair = (lax.broadcasted_iota(jnp.int32, (high, count), 0) == pair) & mine
    is_third = lax.broadcasted_iota(jnp.int32, (WIDE, count), 0) == third
    one_hot = lambda x: jnp.where(x, 1.0, 0.0).astype(BF)
    found = dot(one_hot(is_pair), one_hot(is_third), ((1,), (1,)))
    rows = pairs * WIDE
    row = lax.broadcasted_iota(jnp.int32, (WIDE, rows), 0)
    spread = one_hot((lax.broadcasted_iota(jnp.int32, (WIDE, rows), 1) & (WIDE - 1)) == row)
    wide = sum(dot(part, spread, ((1,), (0,))) for part in thirds(found))
    own = lax.broadcasted_iota(jnp.int32, (high, rows), 1) >> (WIDE.bit_length() - 1)
    times = jnp.sum(jnp.where(own == lax.broadcasted_iota(jnp.int32, (high, rows), 0), wide, 0.0), axis=0, keepdims=True)
    n1, n2, n3 = grid_points(base, planes)
    norm = n1 * n1 + n2 * n2 + n3 * n3
    safe = jnp.maximum(norm, 1.0)
    return jnp.where(norm > 0, times * (ewald_scale * jnp.exp(-ewald_damp * safe) / safe), 0.0)


def table_kernel(planes, step, place, n_ref, f_ref, out_ref, weight_ref, pairs):
    base = place[1] * planes
    weight_ref[...] = grid_weights(n_ref[...], base, planes)
    steps = (lax.broadcasted_iota(jnp.int32, (WIDE, step), 0) - KMAX).astype(F32)
    for start in range(0, f_ref.shape[1], step):
        cols = slice(start, start + step)
        second = wave(steps * f_ref[1:2, cols])
        third = wave(steps * f_ref[2:3, cols])
        for plane in range(planes):
            first = wave((base + plane).astype(F32) * f_ref[0:1, cols])
            pairs[0, plane] = first[0] * second[0] - first[1] * second[1]
            pairs[1, plane] = first[1] * second[0] + first[0] * second[1]
            for m in range(SPREAD):
                real, imag = pairs[0, plane, m : m + 1, :], pairs[1, plane, m : m + 1, :]
                at = slice((plane * SPREAD + m) * WIDE, (plane * SPREAD + m + 1) * WIDE)
                out_ref[0, at, cols] = (real * third[0] - imag * third[1]).astype(BF)
                out_ref[1, at, cols] = (imag * third[0] + real * third[1]).astype(BF)


def table_call(place, n, f, planes):
    rows = planes * SPREAD * WIDE
    atoms = f.shape[1]
    step = 256
    whole = lambda shape: pl.BlockSpec(shape, lambda g, *_: (0,) * len(shape), pipeline_mode=pl.Buffered(1))
    return pl.pallas_call(
        functools.partial(table_kernel, planes, step),
        grid_spec=pltpu.PrefetchScalarGridSpec(
            num_scalar_prefetch=1,
            grid=(1,),
            in_specs=[whole(n.shape), whole(f.shape)],
            out_specs=[whole((2, rows, atoms)), whole((1, rows))],
            scratch_shapes=[pltpu.VMEM((2, planes, WIDE, step), F32)],
        ),
        out_shape=[jax.ShapeDtypeStruct((2, rows, atoms), BF), jax.ShapeDtypeStruct((1, rows), F32)],
        compiler_params=params(12),
        cost_estimate=pl.CostEstimate(flops=rows * atoms * 40, transcendentals=0, bytes_accessed=rows * atoms * 4),
        name="table",
    )(place, n, f)


def structure_kernel(inv_root, c_ref, t_ref, out_ref):
    high, low = halves(c_ref[...])
    both = jnp.concatenate([high, low], axis=0)
    s = dot(t_ref[...], both, ((1,), (1,)))
    nq = c_ref.shape[0]
    out_ref[...] = (s[:, :nq] + s[:, nq:]).T * inv_root


def structure_call(c, table, inv_root):
    rows, atoms = table.shape
    step = rows
    nq = c.shape[0]
    return pl.pallas_call(
        functools.partial(structure_kernel, inv_root),
        grid=(rows // step,),
        in_specs=[pl.BlockSpec((nq, atoms), lambda i: (0, 0)), pl.BlockSpec((step, atoms), lambda i: (i, 0))],
        out_specs=pl.BlockSpec((nq, step), lambda i: (0, i)),
        out_shape=jax.ShapeDtypeStruct((nq, rows), F32),
        compiler_params=params(12),
        cost_estimate=pl.CostEstimate(flops=rows * atoms * 512, transcendentals=0, bytes_accessed=rows * atoms * 2),
        name="structure",
    )(c, table)


def field_kernel(planes, step, place, s_ref, weight_ref, c_ref, t_ref, out_ref):
    nq = c_ref.shape[0]
    waves = weight_ref.shape[1]
    n = grid_points(place[1] * planes, planes)
    real = s_ref[:, :waves] * weight_ref[...]
    imag = s_ref[:, waves:] * weight_ref[...]
    with_cos = jnp.concatenate([real] + [-imag * n[d] for d in range(3)], axis=0)
    with_sin = jnp.concatenate([imag] + [real * n[d] for d in range(3)], axis=0)
    with_cos, with_sin = [jnp.concatenate(halves(x), axis=0) for x in (with_cos, with_sin)]
    for start in range(0, c_ref.shape[1], step):
        cols = slice(start, start + step)
        both = dot(with_cos, t_ref[0, :, cols], ((1,), (0,))) + dot(with_sin, t_ref[1, :, cols], ((1,), (0,)))
        sums = both[: 4 * nq] + both[4 * nq :]
        c = c_ref[:, cols]
        out_ref[0:nq, cols] = sums[:nq]
        forces = [
            jnp.sum(c * sums[(d + 1) * nq : (d + 2) * nq], axis=0, keepdims=True) for d in range(3)
        ]
        out_ref[nq : nq + 8, cols] = jnp.concatenate(forces + [jnp.zeros((5, step), F32)], axis=0)


def field_call(place, s, weight, c, table, planes):
    _, rows, atoms = table.shape
    nq = c.shape[0]
    whole = lambda shape: pl.BlockSpec(shape, lambda g, *_: (0,) * len(shape), pipeline_mode=pl.Buffered(1))
    return pl.pallas_call(
        functools.partial(field_kernel, planes, 512),
        grid_spec=pltpu.PrefetchScalarGridSpec(
            num_scalar_prefetch=1,
            grid=(1,),
            in_specs=[whole(x.shape) for x in (s, weight, c, table)],
            out_specs=whole((nq + 8, atoms)),
        ),
        out_shape=jax.ShapeDtypeStruct((nq + 8, atoms), F32),
        compiler_params=params(12),
        cost_estimate=pl.CostEstimate(flops=rows * atoms * 512, transcendentals=0, bytes_accessed=rows * atoms * 2),
        name="fields",
    )(place, s, weight, c, table)


def finish_kernel(mine_ref, theirs_ref, potential_ref, force_ref):
    nq = potential_ref.shape[0]
    total = mine_ref[...].astype(F32) + theirs_ref[...].astype(F32)
    potential_ref[...] = total[:nq]
    force_ref[...] = total[nq : nq + 3]


def finish_call(mine, theirs, nq):
    atoms = mine.shape[1]
    return pl.pallas_call(
        finish_kernel,
        out_shape=[jax.ShapeDtypeStruct((nq, atoms), F32), jax.ShapeDtypeStruct((3, atoms), F32)],
        compiler_params=pltpu.CompilerParams(vmem_limit_bytes=4 << 20),
        name="finish",
    )(mine, theirs)


def exchanged(x, axis, step):
    size = lax.axis_size(axis)
    if step >= size:
        return x
    return x + lax.ppermute(x, axis, [(i, i ^ step) for i in range(size)])


def summed(x, axis, step=1, stop=None):
    size = lax.axis_size(axis)
    assert size & (size - 1) == 0
    while step < (stop or size):
        x = exchanged(x, axis, step)
        step *= 2
    return x


def whole_step(
    queries,
    key_states,
    value_states,
    fractional,
    block_counts,
    neighbors,
    integer_wave_vectors,
    charge_weight,
):
    heads, head_dim, atoms = queries.shape
    nq = charge_weight.shape[1]
    planes = (KMAX + 1) // lax.axis_size("inner")
    assert planes * lax.axis_size("inner") == KMAX + 1
    inv_root = 1.0 / math.sqrt(atoms * lax.axis_size("seq"))
    place = jnp.stack([lax.axis_index("seq"), lax.axis_index("inner")]).astype(jnp.int32)
    width = REACH * BS
    count = lax.axis_size("seq")
    near_pairs = [(i, i ^ 1) for i in range(count)]
    far_pairs = [(i, i + 1 if i % 2 else i - 1) for i in range(1, count - 1)]

    def swap(x, pairs):
        return lax.ppermute(x, "seq", pairs)

    values = value_states.transpose(1, 0, 2)
    near, far, near_big, far_big, v0, keys, asked, weight, counts, lists, vectors = load_call(
        place, key_states.reshape(heads * head_dim, atoms), values,
        (queries.reshape(heads * head_dim, atoms), charge_weight.T, block_counts, neighbors.T, integer_wave_vectors),
        width,
    )
    far = swap(far, far_pairs)
    near = swap(near, near_pairs)
    far_big = swap(far_big, far_pairs)
    near_big = swap(near_big, near_pairs)

    p_in, scale_in, part = scores_call(
        "interior", lists, counts, place, asked, keys, v0, weight, (), heads, head_dim
    )
    p_out, scale_out, part = scores_call(
        "edges", lists, counts, place, asked, keys, v0, weight, (far, near, part), heads, head_dim
    )
    table, wave_weight = table_call(place, vectors, fractional, planes)
    charges = summed(part, "inner")
    structure = structure_call(charges, table.reshape(-1, atoms), inv_root)
    structure = summed(structure, "seq")
    fields = field_call(place, structure, wave_weight, charges, table, planes)
    last = lax.axis_size("inner") // 2
    fields = summed(fields, "inner", stop=last).astype(BF)
    others = lax.ppermute(fields, "inner", [(i, i ^ last) for i in range(2 * last)])
    potential, forces = finish_call(fields, others, nq)

    mix = functools.partial(mix_call, heads=heads, head_dim=head_dim)
    attention = mix("far", lists, place, values, p_out, scale_out, (far, far_big), None)
    attention = mix("low", lists, place, values, p_in, scale_in, (), attention)
    attention = mix("high", lists, place, values, p_in, scale_in, (), attention)
    attention = mix("near", lists, place, values, p_out, scale_out, (near, near_big), attention)
    return (attention.transpose(1, 0, 2), potential, forces)


def solution(mesh):
    placed = (
        P("inner", None, "seq"),
        P("inner", None, "seq"),
        P("inner", None, "seq"),
        P(None, "seq"),
        P(),
        P("seq", None),
        P(),
        P("inner", None),
    )
    return jax.shard_map(
        whole_step,
        mesh=mesh,
        in_specs=placed,
        out_specs=(P("inner", None, "seq"), P(None, "seq"), P(None, "seq")),
        check_vma=False,
    )
```

```python
import functools
import math

import jax
import jax.numpy as jnp
from jax import lax
from jax.experimental import pallas as pl
from jax.experimental.pallas import tpu as pltpu
from jax.sharding import PartitionSpec as P


BS = 256
NNB = 3
REACH = 2
KMAX = 7
LOG2E = 1.4426950408889634

ewald_scale = 40.0
ewald_damp = 0.02

BF = jnp.bfloat16
F32 = jnp.float32

SIN = (6.283185302511499, -41.34170040531678, 81.60513138577247, -76.70301535353673,
       42.02592698394968, -14.899846662448152, 3.2381375038938693)
COS = (0.9999999890590217, -19.73920449945376, 64.93911745989128, -85.45013953083522,
       60.167630950695504, -25.967599247822193, 6.5286581606558824)


def params(mib):
    return pltpu.CompilerParams(vmem_limit_bytes=mib << 20, dimension_semantics=("arbitrary",))


def dot(a, b, dims):
    return lax.dot_general(a, b, (dims, ((), ())), preferred_element_type=F32)


def horner(coeffs, u):
    total = coeffs[-1]
    for c in coeffs[-2::-1]:
        total = total * u + c
    return total


def halves(x):
    high = x.astype(BF)
    return high, (x - high.astype(F32)).astype(BF)


def thirds(x):
    high, low = halves(x)
    return high, low, ((x - high.astype(F32)) - low.astype(F32)).astype(BF)


def load_kernel(chans, rows, width, place, *refs):
    (k, v, others), (near, far, near_big, far_big, v0, *copies) = (refs[0], refs[1], refs[2:7]), refs[7:-1]
    sems = refs[-1]
    atoms = v.shape[2]
    even = place[0] % 2 == 0
    last = atoms - width
    near_cols = pl.ds(pl.multiple_of(jnp.where(even, last, 0), 128), width)
    far_cols = pl.ds(pl.multiple_of(jnp.where(even, 0, last), 128), width)
    moves = []
    for piece, cols in ((far, far_cols), (near, near_cols)):
        moves.append((k.at[:, cols], piece.at[pl.ds(0, rows)]))
        moves.append((v.at[0, :, cols], piece.at[pl.ds(rows, chans)]))
    moves.append((k, copies[0]))
    moves.append((v.at[0], v0))
    moves += list(zip(others, copies[1:]))
    for piece, cols in ((far_big, far_cols), (near_big, near_cols)):
        moves.append((v.at[pl.ds(1, piece.shape[0]), :, cols], piece))
    started = [pltpu.make_async_copy(src, dst, sems.at[i]) for i, (src, dst) in enumerate(moves)]
    for copy in started:
        copy.start()
    for copy in started:
        copy.wait()


def load_call(place, k, v, others, width):
    comps, chans, atoms = v.shape
    rows = k.shape[0]
    shape = jax.ShapeDtypeStruct
    outs = [shape((rows + chans, width), BF)] * 2 + [shape((comps - 1, chans, width), BF)] * 2
    outs += [shape((chans, atoms), BF)] + [shape(x.shape, x.dtype) for x in (k, *others)]
    return pl.pallas_call(
        functools.partial(load_kernel, chans, rows, width),
        grid_spec=pltpu.PrefetchScalarGridSpec(
            num_scalar_prefetch=1,
            grid=(1,),
            in_specs=[pl.BlockSpec(memory_space=pltpu.HBM)] * (2 + len(others)),
            out_specs=[pl.BlockSpec(memory_space=pl.ANY)] * len(outs),
            scratch_shapes=[pltpu.SemaphoreType.DMA((8 + len(others),))],
        ),
        out_shape=outs,
        compiler_params=params(2),
        cost_estimate=pl.CostEstimate(flops=0, transcendentals=0, bytes_accessed=4 * comps * chans * width),
        name="load",
    )(place, *[pltpu.with_memory_space_constraint(x, pltpu.HBM) for x in (k, v, *others)])


def on_left(place, far):
    even = place[0] % 2 == 0
    return even if far else jnp.logical_not(even)


def edge_block(step, place, blocks):
    left = (step < REACH) == (place[0] % 2 == 0)
    return step % REACH + jnp.where(left, 0, blocks - REACH)


def score_kernel(heads, head_dim, head_chan, blocks, part, lists, counts, place, *refs):
    q_ref, k_ref, v_ref, cw_ref = refs[:4]
    sides, (p_ref, scale_ref, charge_ref, kaug, v0) = refs[4:-5], refs[-5:]
    first = place[0] * blocks
    total = counts.shape[0]
    lane = lax.broadcasted_iota(jnp.int32, (16, BS), 1)
    row = lax.broadcasted_iota(jnp.int32, (16, BS), 0)
    top_row = jnp.where(row == 0, 1.0, 0.0).astype(BF)

    def fill(b, keys, values):
        index = first + b - REACH
        inside = (index >= 0) & (index < total)
        live = jnp.where(inside, counts[jnp.clip(index, 0, total - 1)], 0)
        bias = jnp.where((row == 0) & (lane >= live), -1e30, 0.0).astype(BF)
        for h in range(heads):
            for copy in range(3):
                kaug[b, h, copy * head_dim : (copy + 1) * head_dim, :] = keys[h * head_dim : (h + 1) * head_dim]
            kaug[b, h, 3 * head_dim : 3 * head_dim + 16, :] = bias
            v0[b, h, 0:head_chan] = values[h * head_chan : (h + 1) * head_chan]
            v0[b, h, head_chan : head_chan + 16] = top_row

    for b in range(blocks):
        cols = slice(b * BS, (b + 1) * BS)
        fill(b + REACH, k_ref[:, cols], v_ref[:, cols])
    if sides:
        for far, side in zip((True, False), sides[:2]):
            base = jnp.where(on_left(place, far), 0, blocks + REACH)
            for b in range(REACH):
                cols = slice(b * BS, (b + 1) * BS)
                fill(base + b, side[0 : heads * head_dim, cols], side[heads * head_dim :, cols])
        inner = slice(REACH * BS, (blocks - REACH) * BS)
        charge_ref[:, inner] = sides[2][:, inner]
    else:
        charge_ref[...] = jnp.zeros_like(charge_ref)

    def block_of(i):
        return i + REACH if part == "interior" else edge_block(i, place, blocks)

    def columns(g):
        return pl.ds(pl.multiple_of(g * BS, BS), BS)

    def scores_of(i, h):
        g = block_of(i)
        listed = [lists[e, g] - (first - REACH) for e in range(NNB)]
        q = q_ref[h * head_dim : (h + 1) * head_dim, columns(g)].astype(F32) * (head_dim ** (-0.5) * LOG2E)
        qa = jnp.concatenate([*thirds(q), top_row], axis=0)
        return listed, [dot(kaug[b, h], qa, ((0,), (0,))) for b in listed]

    steps = p_ref.shape[0]
    pairs = [(i, h) for i in range(steps) for h in range(heads)]
    coming = scores_of(*pairs[0])
    charge = None
    for at, (i, h) in enumerate(pairs):
        listed, scores = coming
        if at + 1 < len(pairs):
            coming = scores_of(*pairs[at + 1])
        g = block_of(i)
        top = functools.reduce(jnp.maximum, [jnp.max(s, axis=0, keepdims=True) for s in scores])
        mixed = 0.0
        for e, b in enumerate(listed):
            w16 = jnp.exp2(scores[e] - top).astype(BF)
            p_ref[i, h, e * BS : (e + 1) * BS, :] = w16
            mixed = mixed + dot(v0[b, h], w16, ((1,), (0,)))
        live_q = lane[0:1] < counts[first + g]
        scale = jnp.where(live_q, 1.0 / mixed[head_chan : head_chan + 1], 0.0)
        scale_ref[i, h : h + 1, :] = scale
        att0 = (mixed[:head_chan] * scale).astype(BF)
        term = dot(cw_ref[:, h * head_chan : (h + 1) * head_chan], att0, ((1,), (0,)))
        charge = term if h == 0 else charge + term
        if h == heads - 1:
            charge_ref[:, columns(g)] = charge


def scores_call(part, lists, counts, place, q, k, v0, cw, sides, heads, head_dim):
    chans, atoms = v0.shape
    blocks = atoms // BS
    nq = cw.shape[0]
    head_chan = chans // heads
    band = blocks + 2 * REACH
    steps = blocks - 2 * REACH if part == "interior" else 2 * REACH
    whole = lambda shape: pl.BlockSpec(shape, lambda g, *_: (0,) * len(shape), pipeline_mode=pl.Buffered(1))
    shapes = [((steps, heads, NNB * BS, BS), BF), ((steps, heads, BS), F32), ((nq, atoms), F32)]
    return pl.pallas_call(
        functools.partial(score_kernel, heads, head_dim, head_chan, blocks, part),
        grid_spec=pltpu.PrefetchScalarGridSpec(
            num_scalar_prefetch=3,
            grid=(1,),
            in_specs=[whole(x.shape) for x in (q, k, v0, cw, *sides)],
            out_specs=[whole(shape) for shape, _ in shapes],
            scratch_shapes=[
                pltpu.VMEM((band, heads, 3 * head_dim + 16, BS), BF),
                pltpu.VMEM((band, heads, head_chan + 16, BS), BF),
            ],
        ),
        out_shape=[jax.ShapeDtypeStruct(*x) for x in shapes],
        compiler_params=params(16),
        cost_estimate=pl.CostEstimate(
            flops=steps * heads * NNB * BS * BS * 200, transcendentals=steps * heads * NNB * BS * BS,
            bytes_accessed=steps * heads * NNB * BS * BS * 2,
        ),
    )(lists, counts, place, q, k, v0, cw, *sides)


def mix_kernel(heads, head_dim, head_chan, blocks, part, skip, lists, place, v_ref, p_ref, scale_ref, *refs):
    halo, out_ref = refs[: 2 if part in ("far", "near") else 0], refs[-2 if part in ("far", "near") else -1]
    comps = v_ref.shape[0]
    i = pl.program_id(0)
    offset = place[0] * blocks
    if halo:
        small, big = halo
        band = refs[-1]
        span = 3 * REACH
        left = on_left(place, part == "far")
        begin = jnp.where(left, 0, blocks + 2 * REACH - span)

        @pl.when(i == 0)
        def _():
            own = jnp.where(left, REACH, 0)
            first = jnp.where(left, 0, blocks - 2 * REACH)
            for b in range(2 * REACH):
                band[own + b] = v_ref[:, :, pl.ds(pl.multiple_of((first + b) * BS, BS), BS)]
            other = jnp.where(left, 0, 2 * REACH)
            for b in range(REACH):
                cols = slice(b * BS, (b + 1) * BS)
                band[other + b, 0] = small[heads * head_dim :, cols]
                band[other + b, 1:] = big[:, :, cols]

        g = edge_block(i if part == "far" else i + REACH, place, blocks)
        listed = [lists[e, g] - offset + REACH - begin for e in range(NNB)]
        pick = lambda b, rows: band[b, :, rows, :]
    else:
        g = i + (REACH if part == "low" else blocks // 2)
        listed = [lists[e, g] - offset for e in range(NNB)]
        pick = lambda b, rows: v_ref[:, rows, pl.ds(pl.multiple_of(b * BS, BS), BS)]
    for h in range(heads):
        rows = slice(h * head_chan, (h + 1) * head_chan)
        acc = 0.0
        for e in range(NNB):
            v = pick(listed[e], rows).reshape(comps * head_chan, BS)
            acc = acc + dot(v, p_ref[i + skip, h, e * BS : (e + 1) * BS, :], ((1,), (0,)))
        acc = acc * scale_ref[i + skip, h : h + 1, :]
        out_ref[:, rows, :] = acc.astype(BF).reshape(comps, head_chan, BS)


def mix_call(part, lists, place, v, p, scale, halo, prev, heads, head_dim):
    comps, chans, atoms = v.shape
    blocks = atoms // BS
    half = blocks // 2 - REACH
    steps = REACH if halo else half
    skip = {"low": 0, "high": half, "far": 0, "near": REACH}[part]

    def at(i, lists, place):
        if part in ("low", "high"):
            return i + REACH + skip
        return edge_block(i + skip, place, blocks)

    whole = lambda shape: pl.BlockSpec(shape, lambda g, *_: (0,) * len(shape), pipeline_mode=pl.Buffered(1))
    extra = list(halo) + ([] if prev is None else [prev])
    return pl.pallas_call(
        functools.partial(mix_kernel, heads, head_dim, chans // heads, blocks, part, skip),
        grid_spec=pltpu.PrefetchScalarGridSpec(
            num_scalar_prefetch=2,
            grid=(steps,),
            in_specs=[
                whole(v.shape),
                whole(p.shape),
                whole(scale.shape),
            ]
            + [whole(x.shape) for x in halo]
            + ([] if prev is None else [pl.BlockSpec(memory_space=pl.ANY)]),
            out_specs=pl.BlockSpec((comps, chans, BS), lambda i, *s: (0, 0, at(i, *s))),
            scratch_shapes=[pltpu.VMEM((3 * REACH, comps, chans, BS), BF)] if halo else [],
        ),
        out_shape=jax.ShapeDtypeStruct(v.shape, BF),
        input_output_aliases={} if prev is None else {4 + len(extra): 0},
        compiler_params=params(16),
        cost_estimate=pl.CostEstimate(
            flops=steps * chans * comps * NNB * BS * BS * 2, transcendentals=0,
            bytes_accessed=steps * chans * comps * BS * 8,
        ),
    )(lists, place, v, p, scale, *extra)


SPREAD = 2 * KMAX + 1
WIDE = 16


def wave(turns):
    r = turns - jnp.round(turns)
    u = r * r
    return horner(COS, u), horner(SIN, u) * r


def grid_points(base, planes):
    rows = planes * SPREAD * WIDE
    place = lax.broadcasted_iota(jnp.int32, (1, rows), 1).astype(F32)
    pair = jnp.floor((place + 0.5) * (1.0 / WIDE))
    n3 = place - pair * WIDE - KMAX
    plane = jnp.floor((pair + 0.5) * (1.0 / SPREAD))
    return plane + base.astype(F32), pair - plane * SPREAD - KMAX, n3


def grid_weights(n, base, planes):
    pairs = planes * SPREAD
    high = -(-pairs // 16) * 16
    flip = jnp.where(n[0:1] < 0, -1, 1)
    pair = (n[0:1] * flip - base) * SPREAD + n[1:2] * flip + KMAX
    mine = (n[0:1] * flip >= base) & (n[0:1] * flip < base + planes)
    third = n[2:3] * flip + KMAX
    count = n.shape[1]
    is_pair = (lax.broadcasted_iota(jnp.int32, (high, count), 0) == pair) & mine
    is_third = lax.broadcasted_iota(jnp.int32, (WIDE, count), 0) == third
    one_hot = lambda x: jnp.where(x, 1.0, 0.0).astype(BF)
    found = dot(one_hot(is_pair), one_hot(is_third), ((1,), (1,)))
    rows = pairs * WIDE
    row = lax.broadcasted_iota(jnp.int32, (WIDE, rows), 0)
    spread = one_hot((lax.broadcasted_iota(jnp.int32, (WIDE, rows), 1) & (WIDE - 1)) == row)
    wide = sum(dot(part, spread, ((1,), (0,))) for part in thirds(found))
    own = lax.broadcasted_iota(jnp.int32, (high, rows), 1) >> (WIDE.bit_length() - 1)
    times = jnp.sum(jnp.where(own == lax.broadcasted_iota(jnp.int32, (high, rows), 0), wide, 0.0), axis=0, keepdims=True)
    n1, n2, n3 = grid_points(base, planes)
    norm = n1 * n1 + n2 * n2 + n3 * n3
    safe = jnp.maximum(norm, 1.0)
    return jnp.where(norm > 0, times * (ewald_scale * jnp.exp(-ewald_damp * safe) / safe), 0.0)


def table_kernel(planes, step, place, n_ref, f_ref, out_ref, weight_ref, pairs):
    base = place[1] * planes
    weight_ref[...] = grid_weights(n_ref[...], base, planes)
    steps = (lax.broadcasted_iota(jnp.int32, (WIDE, step), 0) - KMAX).astype(F32)
    for start in range(0, f_ref.shape[1], step):
        cols = slice(start, start + step)
        second = wave(steps * f_ref[1:2, cols])
        third = wave(steps * f_ref[2:3, cols])
        for plane in range(planes):
            first = wave((base + plane).astype(F32) * f_ref[0:1, cols])
            pairs[0, plane] = first[0] * second[0] - first[1] * second[1]
            pairs[1, plane] = first[1] * second[0] + first[0] * second[1]
            for m in range(SPREAD):
                real, imag = pairs[0, plane, m : m + 1, :], pairs[1, plane, m : m + 1, :]
                at = slice((plane * SPREAD + m) * WIDE, (plane * SPREAD + m + 1) * WIDE)
                out_ref[0, at, cols] = (real * third[0] - imag * third[1]).astype(BF)
                out_ref[1, at, cols] = (imag * third[0] + real * third[1]).astype(BF)


def table_call(place, n, f, planes):
    rows = planes * SPREAD * WIDE
    atoms = f.shape[1]
    step = 256
    whole = lambda shape: pl.BlockSpec(shape, lambda g, *_: (0,) * len(shape), pipeline_mode=pl.Buffered(1))
    return pl.pallas_call(
        functools.partial(table_kernel, planes, step),
        grid_spec=pltpu.PrefetchScalarGridSpec(
            num_scalar_prefetch=1,
            grid=(1,),
            in_specs=[whole(n.shape), whole(f.shape)],
            out_specs=[whole((2, rows, atoms)), whole((1, rows))],
            scratch_shapes=[pltpu.VMEM((2, planes, WIDE, step), F32)],
        ),
        out_shape=[jax.ShapeDtypeStruct((2, rows, atoms), BF), jax.ShapeDtypeStruct((1, rows), F32)],
        compiler_params=params(12),
        cost_estimate=pl.CostEstimate(flops=rows * atoms * 40, transcendentals=0, bytes_accessed=rows * atoms * 4),
        name="table",
    )(place, n, f)


def structure_kernel(inv_root, c_ref, t_ref, out_ref):
    high, low = halves(c_ref[...])
    both = jnp.concatenate([high, low], axis=0)
    s = dot(t_ref[...], both, ((1,), (1,)))
    nq = c_ref.shape[0]
    out_ref[...] = (s[:, :nq] + s[:, nq:]).T * inv_root


def structure_call(c, table, inv_root):
    rows, atoms = table.shape
    step = rows
    nq = c.shape[0]
    return pl.pallas_call(
        functools.partial(structure_kernel, inv_root),
        grid=(rows // step,),
        in_specs=[pl.BlockSpec((nq, atoms), lambda i: (0, 0)), pl.BlockSpec((step, atoms), lambda i: (i, 0))],
        out_specs=pl.BlockSpec((nq, step), lambda i: (0, i)),
        out_shape=jax.ShapeDtypeStruct((nq, rows), F32),
        compiler_params=params(12),
        cost_estimate=pl.CostEstimate(flops=rows * atoms * 512, transcendentals=0, bytes_accessed=rows * atoms * 2),
        name="structure",
    )(c, table)


def field_kernel(planes, step, place, s_ref, weight_ref, c_ref, t_ref, out_ref):
    nq = c_ref.shape[0]
    waves = weight_ref.shape[1]
    n = grid_points(place[1] * planes, planes)
    real = s_ref[:, :waves] * weight_ref[...]
    imag = s_ref[:, waves:] * weight_ref[...]
    with_cos = jnp.concatenate([real] + [-imag * n[d] for d in range(3)], axis=0)
    with_sin = jnp.concatenate([imag] + [real * n[d] for d in range(3)], axis=0)
    with_cos, with_sin = [jnp.concatenate(halves(x), axis=0) for x in (with_cos, with_sin)]
    for start in range(0, c_ref.shape[1], step):
        cols = slice(start, start + step)
        both = dot(with_cos, t_ref[0, :, cols], ((1,), (0,))) + dot(with_sin, t_ref[1, :, cols], ((1,), (0,)))
        sums = both[: 4 * nq] + both[4 * nq :]
        c = c_ref[:, cols]
        out_ref[0:nq, cols] = sums[:nq]
        forces = [
            jnp.sum(c * sums[(d + 1) * nq : (d + 2) * nq], axis=0, keepdims=True) for d in range(3)
        ]
        out_ref[nq : nq + 8, cols] = jnp.concatenate(forces + [jnp.zeros((5, step), F32)], axis=0)


def field_call(place, s, weight, c, table, planes):
    _, rows, atoms = table.shape
    nq = c.shape[0]
    whole = lambda shape: pl.BlockSpec(shape, lambda g, *_: (0,) * len(shape), pipeline_mode=pl.Buffered(1))
    return pl.pallas_call(
        functools.partial(field_kernel, planes, 512),
        grid_spec=pltpu.PrefetchScalarGridSpec(
            num_scalar_prefetch=1,
            grid=(1,),
            in_specs=[whole(x.shape) for x in (s, weight, c, table)],
            out_specs=whole((nq + 8, atoms)),
        ),
        out_shape=jax.ShapeDtypeStruct((nq + 8, atoms), F32),
        compiler_params=params(12),
        cost_estimate=pl.CostEstimate(flops=rows * atoms * 512, transcendentals=0, bytes_accessed=rows * atoms * 2),
        name="fields",
    )(place, s, weight, c, table)


def finish_kernel(mine_ref, theirs_ref, potential_ref, force_ref):
    nq = potential_ref.shape[0]
    total = mine_ref[...].astype(F32) + theirs_ref[...].astype(F32)
    potential_ref[...] = total[:nq]
    force_ref[...] = total[nq : nq + 3]


def finish_call(mine, theirs, nq):
    atoms = mine.shape[1]
    return pl.pallas_call(
        finish_kernel,
        out_shape=[jax.ShapeDtypeStruct((nq, atoms), F32), jax.ShapeDtypeStruct((3, atoms), F32)],
        compiler_params=pltpu.CompilerParams(vmem_limit_bytes=4 << 20),
        name="finish",
    )(mine, theirs)


def exchanged(x, axis, step):
    size = lax.axis_size(axis)
    if step >= size:
        return x
    return x + lax.ppermute(x, axis, [(i, i ^ step) for i in range(size)])


def summed(x, axis, step=1, stop=None):
    size = lax.axis_size(axis)
    assert size & (size - 1) == 0
    while step < (stop or size):
        x = exchanged(x, axis, step)
        step *= 2
    return x


def whole_step(
    queries,
    key_states,
    value_states,
    fractional,
    block_counts,
    neighbors,
    integer_wave_vectors,
    charge_weight,
):
    heads, head_dim, atoms = queries.shape
    nq = charge_weight.shape[1]
    planes = (KMAX + 1) // lax.axis_size("inner")
    assert planes * lax.axis_size("inner") == KMAX + 1
    inv_root = 1.0 / math.sqrt(atoms * lax.axis_size("seq"))
    place = jnp.stack([lax.axis_index("seq"), lax.axis_index("inner")]).astype(jnp.int32)
    width = REACH * BS
    count = lax.axis_size("seq")
    near_pairs = [(i, i ^ 1) for i in range(count)]
    far_pairs = [(i, i + 1 if i % 2 else i - 1) for i in range(1, count - 1)]

    def swap(x, pairs):
        return lax.ppermute(x, "seq", pairs)

    values = value_states.transpose(1, 0, 2)
    near, far, near_big, far_big, v0, keys, asked, weight, counts, lists, vectors = load_call(
        place, key_states.reshape(heads * head_dim, atoms), values,
        (queries.reshape(heads * head_dim, atoms), charge_weight.T, block_counts, neighbors.T, integer_wave_vectors),
        width,
    )
    far = swap(far, far_pairs)
    near = swap(near, near_pairs)
    far_big = swap(far_big, far_pairs)
    near_big = swap(near_big, near_pairs)

    p_in, scale_in, part = scores_call(
        "interior", lists, counts, place, asked, keys, v0, weight, (), heads, head_dim
    )
    p_out, scale_out, part = scores_call(
        "edges", lists, counts, place, asked, keys, v0, weight, (far, near, part), heads, head_dim
    )
    table, wave_weight = table_call(place, vectors, fractional, planes)
    last = lax.axis_size("inner") // 2

    def halfway(x, name):
        x = summed(x, "inner", stop=last)
        x = x.astype(BF) if name == "charge" else x
        return x, lax.ppermute(x, "inner", [(i, i ^ last) for i in range(2 * last)])

    mine, theirs = halfway(part, "charge")
    charges = mine.astype(F32) + theirs.astype(F32)
    structure = structure_call(charges, table.reshape(-1, atoms), inv_root)
    for step in (2, 1):
        structure = exchanged(structure, "seq", step)
    structure = summed(structure, "seq", 4)
    fields = field_call(place, structure, wave_weight, charges, table, planes)
    fields, others = halfway(fields, "field")
    potential, forces = finish_call(fields, others, nq)

    mix = functools.partial(mix_call, heads=heads, head_dim=head_dim)
    attention = mix("low", lists, place, values, p_in, scale_in, (), None)
    attention = mix("high", lists, place, values, p_in, scale_in, (), attention)
    attention = mix("far", lists, place, values, p_out, scale_out, (far, far_big), attention)
    attention = mix("near", lists, place, values, p_out, scale_out, (near, near_big), attention)
    return (attention.transpose(1, 0, 2), potential, forces)


def solution(mesh):
    placed = (
        P("inner", None, "seq"),
        P("inner", None, "seq"),
        P("inner", None, "seq"),
        P(None, "seq"),
        P(),
        P("seq", None),
        P(),
        P("inner", None),
    )
    return jax.shard_map(
        whole_step,
        mesh=mesh,
        in_specs=placed,
        out_specs=(P("inner", None, "seq"), P(None, "seq"), P(None, "seq")),
        check_vma=False,
    )
```

```python
import functools
import math

import jax
import jax.numpy as jnp
from jax import lax
from jax.experimental import pallas as pl
from jax.experimental.pallas import tpu as pltpu
from jax.sharding import PartitionSpec as P


BS = 256
NNB = 3
REACH = 2
KMAX = 7
LOG2E = 1.4426950408889634

ewald_scale = 40.0
ewald_damp = 0.02

BF = jnp.bfloat16
F32 = jnp.float32

SIN = (6.283185302511499, -41.34170040531678, 81.60513138577247, -76.70301535353673,
       42.02592698394968, -14.899846662448152, 3.2381375038938693)
COS = (0.9999999890590217, -19.73920449945376, 64.93911745989128, -85.45013953083522,
       60.167630950695504, -25.967599247822193, 6.5286581606558824)


def params(mib):
    return pltpu.CompilerParams(vmem_limit_bytes=mib << 20, dimension_semantics=("arbitrary",))


def dot(a, b, dims):
    return lax.dot_general(a, b, (dims, ((), ())), preferred_element_type=F32)


def horner(coeffs, u):
    total = coeffs[-1]
    for c in coeffs[-2::-1]:
        total = total * u + c
    return total


def halves(x):
    high = x.astype(BF)
    return high, (x - high.astype(F32)).astype(BF)


def thirds(x):
    high, low = halves(x)
    return high, low, ((x - high.astype(F32)) - low.astype(F32)).astype(BF)


def columns_of(place, width, atoms, far):
    first = on_left(place, far)
    return pl.ds(pl.multiple_of(jnp.where(first, 0, atoms - width), 128), width)


def run(moves, sems):
    started = [pltpu.make_async_copy(src, dst, sems.at[i]) for i, (src, dst) in enumerate(moves)]
    for copy in started:
        copy.start()
    for copy in started:
        copy.wait()


def piece_kernel(place, k, v, near, far, far_big, sems):
    rows, atoms = k.shape
    chans, width = v.shape[1], near.shape[1]
    moves = []
    for piece, is_far in ((far, True), (near, False)):
        cols = columns_of(place, width, atoms, is_far)
        moves.append((k.at[:, cols], piece.at[pl.ds(0, rows)]))
        moves.append((v.at[0, :, cols], piece.at[pl.ds(rows, chans)]))
    moves.append((v.at[pl.ds(1, far_big.shape[0]), :, columns_of(place, width, atoms, True)], far_big))
    run(moves, sems)


def load_kernel(place, v, *refs):
    others, (near_big, v0, *copies), sems = refs[: (len(refs) - 3) // 2], refs[(len(refs) - 3) // 2 : -1], refs[-1]
    cols = columns_of(place, near_big.shape[2], v.shape[2], False)
    run(
        list(zip(others, copies)) + [(v.at[0], v0), (v.at[pl.ds(1, near_big.shape[0]), :, cols], near_big)],
        sems,
    )


def copying_call(kernel, place, operands, outs):
    return pl.pallas_call(
        kernel,
        grid_spec=pltpu.PrefetchScalarGridSpec(
            num_scalar_prefetch=1,
            grid=(1,),
            in_specs=[pl.BlockSpec(memory_space=pltpu.HBM)] * len(operands),
            out_specs=[pl.BlockSpec(memory_space=pl.ANY)] * len(outs),
            scratch_shapes=[pltpu.SemaphoreType.DMA((8,))],
        ),
        out_shape=outs,
        compiler_params=params(2),
        cost_estimate=pl.CostEstimate(flops=0, transcendentals=0, bytes_accessed=1 << 20),
    )(place, *[pltpu.with_memory_space_constraint(x, pltpu.HBM) for x in operands])


def piece_call(place, k, v, width):
    comps, chans, _ = v.shape
    small = jax.ShapeDtypeStruct((k.shape[0] + chans, width), BF)
    return copying_call(
        piece_kernel, place, (k, v), [small, small, jax.ShapeDtypeStruct((comps - 1, chans, width), BF)]
    )


def load_call(place, v, others, width):
    comps, chans, atoms = v.shape
    shape = jax.ShapeDtypeStruct
    outs = [shape((comps - 1, chans, width), BF), shape((chans, atoms), BF)] + [shape(x.shape, x.dtype) for x in others]
    return copying_call(load_kernel, place, (v, *others), outs)


def on_left(place, far):
    even = place[0] % 2 == 0
    return even if far else jnp.logical_not(even)


def edge_block(step, place, blocks):
    left = (step < REACH) == (place[0] % 2 == 0)
    return step % REACH + jnp.where(left, 0, blocks - REACH)


def score_kernel(heads, head_dim, head_chan, blocks, part, lists, counts, place, *refs):
    q_ref, k_ref, v_ref, cw_ref = refs[:4]
    sides, (p_ref, scale_ref, charge_ref, kaug, v0) = refs[4:-5], refs[-5:]
    first = place[0] * blocks
    total = counts.shape[0]
    lane = lax.broadcasted_iota(jnp.int32, (16, BS), 1)
    row = lax.broadcasted_iota(jnp.int32, (16, BS), 0)
    top_row = jnp.where(row == 0, 1.0, 0.0).astype(BF)

    def fill(b, keys, values):
        index = first + b - REACH
        inside = (index >= 0) & (index < total)
        live = jnp.where(inside, counts[jnp.clip(index, 0, total - 1)], 0)
        bias = jnp.where((row == 0) & (lane >= live), -1e30, 0.0).astype(BF)
        for h in range(heads):
            for copy in range(3):
                kaug[b, h, copy * head_dim : (copy + 1) * head_dim, :] = keys[h * head_dim : (h + 1) * head_dim]
            kaug[b, h, 3 * head_dim : 3 * head_dim + 16, :] = bias
            v0[b, h, 0:head_chan] = values[h * head_chan : (h + 1) * head_chan]
            v0[b, h, head_chan : head_chan + 16] = top_row

    for b in range(blocks):
        cols = slice(b * BS, (b + 1) * BS)
        fill(b + REACH, k_ref[:, cols], v_ref[:, cols])
    if sides:
        for far, side in zip((True, False), sides[:2]):
            base = jnp.where(on_left(place, far), 0, blocks + REACH)
            for b in range(REACH):
                cols = slice(b * BS, (b + 1) * BS)
                fill(base + b, side[0 : heads * head_dim, cols], side[heads * head_dim :, cols])
        inner = slice(REACH * BS, (blocks - REACH) * BS)
        charge_ref[:, inner] = sides[2][:, inner]
    else:
        charge_ref[...] = jnp.zeros_like(charge_ref)

    def block_of(i):
        return i + REACH if part == "interior" else edge_block(i, place, blocks)

    def columns(g):
        return pl.ds(pl.multiple_of(g * BS, BS), BS)

    def scores_of(i, h):
        g = block_of(i)
        listed = [lists[e, g] - (first - REACH) for e in range(NNB)]
        q = q_ref[h * head_dim : (h + 1) * head_dim, columns(g)].astype(F32) * (head_dim ** (-0.5) * LOG2E)
        qa = jnp.concatenate([*thirds(q), top_row], axis=0)
        return listed, [dot(kaug[b, h], qa, ((0,), (0,))) for b in listed]

    steps = p_ref.shape[0]
    pairs = [(i, h) for i in range(steps) for h in range(heads)]
    coming = scores_of(*pairs[0])
    charge = None
    for at, (i, h) in enumerate(pairs):
        listed, scores = coming
        if at + 1 < len(pairs):
            coming = scores_of(*pairs[at + 1])
        g = block_of(i)
        top = functools.reduce(jnp.maximum, [jnp.max(s, axis=0, keepdims=True) for s in scores])
        mixed = 0.0
        for e, b in enumerate(listed):
            w16 = jnp.exp2(scores[e] - top).astype(BF)
            p_ref[i, h, e * BS : (e + 1) * BS, :] = w16
            mixed = mixed + dot(v0[b, h], w16, ((1,), (0,)))
        live_q = lane[0:1] < counts[first + g]
        scale = jnp.where(live_q, 1.0 / mixed[head_chan : head_chan + 1], 0.0)
        scale_ref[i, h : h + 1, :] = scale
        att0 = (mixed[:head_chan] * scale).astype(BF)
        term = dot(cw_ref[:, h * head_chan : (h + 1) * head_chan], att0, ((1,), (0,)))
        charge = term if h == 0 else charge + term
        if h == heads - 1:
            charge_ref[:, columns(g)] = charge


def scores_call(part, lists, counts, place, q, k, v0, cw, sides, heads, head_dim):
    chans, atoms = v0.shape
    blocks = atoms // BS
    nq = cw.shape[0]
    head_chan = chans // heads
    band = blocks + 2 * REACH
    steps = blocks - 2 * REACH if part == "interior" else 2 * REACH
    whole = lambda shape: pl.BlockSpec(shape, lambda g, *_: (0,) * len(shape), pipeline_mode=pl.Buffered(1))
    shapes = [((steps, heads, NNB * BS, BS), BF), ((steps, heads, BS), F32), ((nq, atoms), F32)]
    return pl.pallas_call(
        functools.partial(score_kernel, heads, head_dim, head_chan, blocks, part),
        grid_spec=pltpu.PrefetchScalarGridSpec(
            num_scalar_prefetch=3,
            grid=(1,),
            in_specs=[whole(x.shape) for x in (q, k, v0, cw, *sides)],
            out_specs=[whole(shape) for shape, _ in shapes],
            scratch_shapes=[
                pltpu.VMEM((band, heads, 3 * head_dim + 16, BS), BF),
                pltpu.VMEM((band, heads, head_chan + 16, BS), BF),
            ],
        ),
        out_shape=[jax.ShapeDtypeStruct(*x) for x in shapes],
        compiler_params=params(16),
        cost_estimate=pl.CostEstimate(
            flops=steps * heads * NNB * BS * BS * 200, transcendentals=steps * heads * NNB * BS * BS,
            bytes_accessed=steps * heads * NNB * BS * BS * 2,
        ),
    )(lists, counts, place, q, k, v0, cw, *sides)


def mix_kernel(heads, head_dim, head_chan, blocks, part, skip, lists, place, v_ref, p_ref, scale_ref, *refs):
    halo, out_ref = refs[: 2 if part in ("far", "near") else 0], refs[-2 if part in ("far", "near") else -1]
    comps = v_ref.shape[0]
    i = pl.program_id(0)
    offset = place[0] * blocks
    if halo:
        small, big = halo
        band = refs[-1]
        span = 3 * REACH
        left = on_left(place, part == "far")
        begin = jnp.where(left, 0, blocks + 2 * REACH - span)

        @pl.when(i == 0)
        def _():
            own = jnp.where(left, REACH, 0)
            first = jnp.where(left, 0, blocks - 2 * REACH)
            for b in range(2 * REACH):
                band[own + b] = v_ref[:, :, pl.ds(pl.multiple_of((first + b) * BS, BS), BS)]
            other = jnp.where(left, 0, 2 * REACH)
            for b in range(REACH):
                cols = slice(b * BS, (b + 1) * BS)
                band[other + b, 0] = small[heads * head_dim :, cols]
                band[other + b, 1:] = big[:, :, cols]

        g = edge_block(i if part == "far" else i + REACH, place, blocks)
        listed = [lists[e, g] - offset + REACH - begin for e in range(NNB)]
        pick = lambda b, rows: band[b, :, rows, :]
    else:
        g = i + (REACH if part == "low" else blocks // 2)
        listed = [lists[e, g] - offset for e in range(NNB)]
        pick = lambda b, rows: v_ref[:, rows, pl.ds(pl.multiple_of(b * BS, BS), BS)]
    for h in range(heads):
        rows = slice(h * head_chan, (h + 1) * head_chan)
        acc = 0.0
        for e in range(NNB):
            v = pick(listed[e], rows).reshape(comps * head_chan, BS)
            acc = acc + dot(v, p_ref[i + skip, h, e * BS : (e + 1) * BS, :], ((1,), (0,)))
        acc = acc * scale_ref[i + skip, h : h + 1, :]
        out_ref[:, rows, :] = acc.astype(BF).reshape(comps, head_chan, BS)


def mix_call(part, lists, place, v, p, scale, halo, prev, heads, head_dim):
    comps, chans, atoms = v.shape
    blocks = atoms // BS
    half = blocks // 2 - REACH
    steps = REACH if halo else half
    skip = {"low": 0, "high": half, "far": 0, "near": REACH}[part]

    def at(i, lists, place):
        if part in ("low", "high"):
            return i + REACH + skip
        return edge_block(i + skip, place, blocks)

    whole = lambda shape: pl.BlockSpec(shape, lambda g, *_: (0,) * len(shape), pipeline_mode=pl.Buffered(1))
    extra = list(halo) + ([] if prev is None else [prev])
    return pl.pallas_call(
        functools.partial(mix_kernel, heads, head_dim, chans // heads, blocks, part, skip),
        grid_spec=pltpu.PrefetchScalarGridSpec(
            num_scalar_prefetch=2,
            grid=(steps,),
            in_specs=[
                whole(v.shape),
                whole(p.shape),
                whole(scale.shape),
            ]
            + [whole(x.shape) for x in halo]
            + ([] if prev is None else [pl.BlockSpec(memory_space=pl.ANY)]),
            out_specs=pl.BlockSpec((comps, chans, BS), lambda i, *s: (0, 0, at(i, *s))),
            scratch_shapes=[pltpu.VMEM((3 * REACH, comps, chans, BS), BF)] if halo else [],
        ),
        out_shape=jax.ShapeDtypeStruct(v.shape, BF),
        input_output_aliases={} if prev is None else {4 + len(extra): 0},
        compiler_params=params(16),
        cost_estimate=pl.CostEstimate(
            flops=steps * chans * comps * NNB * BS * BS * 2, transcendentals=0,
            bytes_accessed=steps * chans * comps * BS * 8,
        ),
    )(lists, place, v, p, scale, *extra)


SPREAD = 2 * KMAX + 1
WIDE = 16


def wave(turns):
    r = turns - jnp.round(turns)
    u = r * r
    return horner(COS, u), horner(SIN, u) * r


def grid_points(base, planes):
    rows = planes * SPREAD * WIDE
    place = lax.broadcasted_iota(jnp.int32, (1, rows), 1).astype(F32)
    pair = jnp.floor((place + 0.5) * (1.0 / WIDE))
    n3 = place - pair * WIDE - KMAX
    plane = jnp.floor((pair + 0.5) * (1.0 / SPREAD))
    return plane + base.astype(F32), pair - plane * SPREAD - KMAX, n3


def grid_weights(n, base, planes):
    pairs = planes * SPREAD
    high = -(-pairs // 16) * 16
    flip = jnp.where(n[0:1] < 0, -1, 1)
    pair = (n[0:1] * flip - base) * SPREAD + n[1:2] * flip + KMAX
    mine = (n[0:1] * flip >= base) & (n[0:1] * flip < base + planes)
    third = n[2:3] * flip + KMAX
    count = n.shape[1]
    is_pair = (lax.broadcasted_iota(jnp.int32, (high, count), 0) == pair) & mine
    is_third = lax.broadcasted_iota(jnp.int32, (WIDE, count), 0) == third
    one_hot = lambda x: jnp.where(x, 1.0, 0.0).astype(BF)
    found = dot(one_hot(is_pair), one_hot(is_third), ((1,), (1,)))
    rows = pairs * WIDE
    row = lax.broadcasted_iota(jnp.int32, (WIDE, rows), 0)
    spread = one_hot((lax.broadcasted_iota(jnp.int32, (WIDE, rows), 1) & (WIDE - 1)) == row)
    wide = sum(dot(part, spread, ((1,), (0,))) for part in thirds(found))
    own = lax.broadcasted_iota(jnp.int32, (high, rows), 1) >> (WIDE.bit_length() - 1)
    times = jnp.sum(jnp.where(own == lax.broadcasted_iota(jnp.int32, (high, rows), 0), wide, 0.0), axis=0, keepdims=True)
    n1, n2, n3 = grid_points(base, planes)
    norm = n1 * n1 + n2 * n2 + n3 * n3
    safe = jnp.maximum(norm, 1.0)
    return jnp.where(norm > 0, times * (ewald_scale * jnp.exp(-ewald_damp * safe) / safe), 0.0)


def table_kernel(planes, step, place, n_ref, f_ref, out_ref, weight_ref, pairs):
    base = place[1] * planes
    weight_ref[...] = grid_weights(n_ref[...], base, planes)
    steps = (lax.broadcasted_iota(jnp.int32, (WIDE, step), 0) - KMAX).astype(F32)
    for start in range(0, f_ref.shape[1], step):
        cols = slice(start, start + step)
        second = wave(steps * f_ref[1:2, cols])
        third = wave(steps * f_ref[2:3, cols])
        for plane in range(planes):
            first = wave((base + plane).astype(F32) * f_ref[0:1, cols])
            pairs[0, plane] = first[0] * second[0] - first[1] * second[1]
            pairs[1, plane] = first[1] * second[0] + first[0] * second[1]
            for m in range(SPREAD):
                real, imag = pairs[0, plane, m : m + 1, :], pairs[1, plane, m : m + 1, :]
                at = slice((plane * SPREAD + m) * WIDE, (plane * SPREAD + m + 1) * WIDE)
                out_ref[0, at, cols] = (real * third[0] - imag * third[1]).astype(BF)
                out_ref[1, at, cols] = (imag * third[0] + real * third[1]).astype(BF)


def table_call(place, n, f, planes):
    rows = planes * SPREAD * WIDE
    atoms = f.shape[1]
    step = 256
    whole = lambda shape: pl.BlockSpec(shape, lambda g, *_: (0,) * len(shape), pipeline_mode=pl.Buffered(1))
    return pl.pallas_call(
        functools.partial(table_kernel, planes, step),
        grid_spec=pltpu.PrefetchScalarGridSpec(
            num_scalar_prefetch=1,
            grid=(1,),
            in_specs=[whole(n.shape), whole(f.shape)],
            out_specs=[whole((2, rows, atoms)), whole((1, rows))],
            scratch_shapes=[pltpu.VMEM((2, planes, WIDE, step), F32)],
        ),
        out_shape=[jax.ShapeDtypeStruct((2, rows, atoms), BF), jax.ShapeDtypeStruct((1, rows), F32)],
        compiler_params=params(12),
        cost_estimate=pl.CostEstimate(flops=rows * atoms * 40, transcendentals=0, bytes_accessed=rows * atoms * 4),
        name="table",
    )(place, n, f)


def structure_kernel(inv_root, c_ref, t_ref, out_ref):
    high, low = halves(c_ref[...])
    both = jnp.concatenate([high, low], axis=0)
    s = dot(t_ref[...], both, ((1,), (1,)))
    nq = c_ref.shape[0]
    out_ref[...] = (s[:, :nq] + s[:, nq:]).T * inv_root


def structure_call(c, table, inv_root):
    rows, atoms = table.shape
    step = rows
    nq = c.shape[0]
    return pl.pallas_call(
        functools.partial(structure_kernel, inv_root),
        grid=(rows // step,),
        in_specs=[pl.BlockSpec((nq, atoms), lambda i: (0, 0)), pl.BlockSpec((step, atoms), lambda i: (i, 0))],
        out_specs=pl.BlockSpec((nq, step), lambda i: (0, i)),
        out_shape=jax.ShapeDtypeStruct((nq, rows), F32),
        compiler_params=params(12),
        cost_estimate=pl.CostEstimate(flops=rows * atoms * 512, transcendentals=0, bytes_accessed=rows * atoms * 2),
        name="structure",
    )(c, table)


def field_kernel(planes, step, place, s_ref, weight_ref, c_ref, t_ref, out_ref):
    nq = c_ref.shape[0]
    waves = weight_ref.shape[1]
    n = grid_points(place[1] * planes, planes)
    real = s_ref[:, :waves] * weight_ref[...]
    imag = s_ref[:, waves:] * weight_ref[...]
    with_cos = jnp.concatenate([real] + [-imag * n[d] for d in range(3)], axis=0)
    with_sin = jnp.concatenate([imag] + [real * n[d] for d in range(3)], axis=0)
    with_cos, with_sin = [jnp.concatenate(halves(x), axis=0) for x in (with_cos, with_sin)]
    for start in range(0, c_ref.shape[1], step):
        cols = slice(start, start + step)
        both = dot(with_cos, t_ref[0, :, cols], ((1,), (0,))) + dot(with_sin, t_ref[1, :, cols], ((1,), (0,)))
        sums = both[: 4 * nq] + both[4 * nq :]
        c = c_ref[:, cols]
        out_ref[0:nq, cols] = sums[:nq]
        forces = [
            jnp.sum(c * sums[(d + 1) * nq : (d + 2) * nq], axis=0, keepdims=True) for d in range(3)
        ]
        out_ref[nq : nq + 8, cols] = jnp.concatenate(forces + [jnp.zeros((5, step), F32)], axis=0)


def field_call(place, s, weight, c, table, planes):
    _, rows, atoms = table.shape
    nq = c.shape[0]
    whole = lambda shape: pl.BlockSpec(shape, lambda g, *_: (0,) * len(shape), pipeline_mode=pl.Buffered(1))
    return pl.pallas_call(
        functools.partial(field_kernel, planes, 512),
        grid_spec=pltpu.PrefetchScalarGridSpec(
            num_scalar_prefetch=1,
            grid=(1,),
            in_specs=[whole(x.shape) for x in (s, weight, c, table)],
            out_specs=whole((nq + 8, atoms)),
        ),
        out_shape=jax.ShapeDtypeStruct((nq + 8, atoms), F32),
        compiler_params=params(12),
        cost_estimate=pl.CostEstimate(flops=rows * atoms * 512, transcendentals=0, bytes_accessed=rows * atoms * 2),
        name="fields",
    )(place, s, weight, c, table)


def finish_kernel(mine_ref, theirs_ref, potential_ref, force_ref):
    nq = potential_ref.shape[0]
    total = mine_ref[...].astype(F32) + theirs_ref[...].astype(F32)
    potential_ref[...] = total[:nq]
    force_ref[...] = total[nq : nq + 3]


def finish_call(mine, theirs, nq):
    atoms = mine.shape[1]
    return pl.pallas_call(
        finish_kernel,
        out_shape=[jax.ShapeDtypeStruct((nq, atoms), F32), jax.ShapeDtypeStruct((3, atoms), F32)],
        compiler_params=pltpu.CompilerParams(vmem_limit_bytes=4 << 20),
        name="finish",
    )(mine, theirs)


def exchanged(x, axis, step):
    size = lax.axis_size(axis)
    if step >= size:
        return x
    return x + lax.ppermute(x, axis, [(i, i ^ step) for i in range(size)])


def summed(x, axis, step=1, stop=None):
    size = lax.axis_size(axis)
    assert size & (size - 1) == 0
    while step < (stop or size):
        x = exchanged(x, axis, step)
        step *= 2
    return x


def whole_step(
    queries,
    key_states,
    value_states,
    fractional,
    block_counts,
    neighbors,
    integer_wave_vectors,
    charge_weight,
):
    heads, head_dim, atoms = queries.shape
    nq = charge_weight.shape[1]
    planes = (KMAX + 1) // lax.axis_size("inner")
    assert planes * lax.axis_size("inner") == KMAX + 1
    inv_root = 1.0 / math.sqrt(atoms * lax.axis_size("seq"))
    place = jnp.stack([lax.axis_index("seq"), lax.axis_index("inner")]).astype(jnp.int32)
    width = REACH * BS
    count = lax.axis_size("seq")
    near_pairs = [(i, i ^ 1) for i in range(count)]
    far_pairs = [(i, i + 1 if i % 2 else i - 1) for i in range(1, count - 1)]

    def swap(x, pairs):
        return lax.ppermute(x, "seq", pairs)

    values = value_states.transpose(1, 0, 2)
    keys = key_states.reshape(heads * head_dim, atoms)
    near, far, far_big = piece_call(place, keys, values, width)
    near_big, v0, keys, asked, weight, counts, lists = load_call(
        place, values, (keys, queries.reshape(heads * head_dim, atoms), charge_weight.T, block_counts, neighbors.T), width
    )
    vectors = integer_wave_vectors
    far = swap(far, far_pairs)
    near = swap(near, near_pairs)
    far_big = swap(far_big, far_pairs)
    near_big = swap(near_big, near_pairs)

    p_in, scale_in, part = scores_call(
        "interior", lists, counts, place, asked, keys, v0, weight, (), heads, head_dim
    )
    p_out, scale_out, part = scores_call(
        "edges", lists, counts, place, asked, keys, v0, weight, (far, near, part), heads, head_dim
    )
    table, wave_weight = table_call(place, vectors, fractional, planes)
    last = lax.axis_size("inner") // 2

    def halfway(x):
        x = summed(x, "inner", stop=last).astype(BF)
        return x, lax.ppermute(x, "inner", [(i, i ^ last) for i in range(2 * last)])

    mine, theirs = halfway(part)
    charges = mine.astype(F32) + theirs.astype(F32)
    structure = structure_call(charges, table.reshape(-1, atoms), inv_root)
    structure = summed(structure, "seq")
    fields = field_call(place, structure, wave_weight, charges, table, planes)
    fields, others = halfway(fields)
    potential, forces = finish_call(fields, others, nq)

    mix = functools.partial(mix_call, heads=heads, head_dim=head_dim)
    attention = mix("low", lists, place, values, p_in, scale_in, (), None)
    attention = mix("far", lists, place, values, p_out, scale_out, (far, far_big), attention)
    attention = mix("high", lists, place, values, p_in, scale_in, (), attention)
    attention = mix("near", lists, place, values, p_out, scale_out, (near, near_big), attention)
    return (attention.transpose(1, 0, 2), potential, forces)


def solution(mesh):
    placed = (
        P("inner", None, "seq"),
        P("inner", None, "seq"),
        P("inner", None, "seq"),
        P(None, "seq"),
        P(),
        P("seq", None),
        P(),
        P("inner", None),
    )
    return jax.shard_map(
        whole_step,
        mesh=mesh,
        in_specs=placed,
        out_specs=(P("inner", None, "seq"), P(None, "seq"), P(None, "seq")),
        check_vma=False,
    )
```

```python
import functools
import math

import jax
import jax.numpy as jnp
from jax import lax
from jax.experimental import pallas as pl
from jax.experimental.pallas import tpu as pltpu
from jax.sharding import PartitionSpec as P


BS = 256
NNB = 3
REACH = 2
KMAX = 7
LOG2E = 1.4426950408889634

ewald_scale = 40.0
ewald_damp = 0.02

BF = jnp.bfloat16
F32 = jnp.float32

SIN = (6.283185302511499, -41.34170040531678, 81.60513138577247, -76.70301535353673,
       42.02592698394968, -14.899846662448152, 3.2381375038938693)
COS = (0.9999999890590217, -19.73920449945376, 64.93911745989128, -85.45013953083522,
       60.167630950695504, -25.967599247822193, 6.5286581606558824)


def params(mib):
    return pltpu.CompilerParams(vmem_limit_bytes=mib << 20, dimension_semantics=("arbitrary",))


def dot(a, b, dims):
    return lax.dot_general(a, b, (dims, ((), ())), preferred_element_type=F32)


def horner(coeffs, u):
    total = coeffs[-1]
    for c in coeffs[-2::-1]:
        total = total * u + c
    return total


def halves(x):
    high = x.astype(BF)
    return high, (x - high.astype(F32)).astype(BF)


def thirds(x):
    high, low = halves(x)
    return high, low, ((x - high.astype(F32)) - low.astype(F32)).astype(BF)


def columns_of(place, width, atoms, far):
    first = on_left(place, far)
    return pl.ds(pl.multiple_of(jnp.where(first, 0, atoms - width), 128), width)


def run(moves, sems):
    started = [pltpu.make_async_copy(src, dst, sems.at[i]) for i, (src, dst) in enumerate(moves)]
    for copy in started:
        copy.start()
    for copy in started:
        copy.wait()


def load_kernel(place, k, v, *refs):
    others, (near, far, far_big, v0, *copies), sems = refs[: (len(refs) - 6) // 2], refs[(len(refs) - 6) // 2 : -1], refs[-1]
    rows, atoms = k.shape
    chans, width = v.shape[1], near.shape[1]
    moves = []
    for piece, is_far in ((far, True), (near, False)):
        cols = columns_of(place, width, atoms, is_far)
        moves.append((k.at[:, cols], piece.at[pl.ds(0, rows)]))
        moves.append((v.at[0, :, cols], piece.at[pl.ds(rows, chans)]))
    moves += list(zip((k, *others), copies)) + [(v.at[0], v0)]
    moves.append((v.at[pl.ds(1, far_big.shape[0]), :, columns_of(place, width, atoms, True)], far_big))
    run(moves, sems)


def load_call(place, k, v, others, width):
    comps, chans, atoms = v.shape
    shape = jax.ShapeDtypeStruct
    outs = [shape((k.shape[0] + chans, width), BF)] * 2 + [shape((comps - 1, chans, width), BF)]
    outs += [shape((chans, atoms), BF)] + [shape(x.shape, x.dtype) for x in (k, *others)]
    operands = (k, v, *others)
    return pl.pallas_call(
        load_kernel,
        grid_spec=pltpu.PrefetchScalarGridSpec(
            num_scalar_prefetch=1,
            grid=(1,),
            in_specs=[pl.BlockSpec(memory_space=pltpu.HBM)] * len(operands),
            out_specs=[pl.BlockSpec(memory_space=pl.ANY)] * len(outs),
            scratch_shapes=[pltpu.SemaphoreType.DMA((7 + len(others),))],
        ),
        out_shape=outs,
        compiler_params=params(2),
        cost_estimate=pl.CostEstimate(flops=0, transcendentals=0, bytes_accessed=1 << 20),
        name="load",
    )(place, *[pltpu.with_memory_space_constraint(x, pltpu.HBM) for x in operands])


def on_left(place, far):
    even = place[0] % 2 == 0
    return even if far else jnp.logical_not(even)


def edge_block(step, place, blocks):
    left = (step < REACH) == (place[0] % 2 == 0)
    return step % REACH + jnp.where(left, 0, blocks - REACH)


def score_kernel(heads, head_dim, head_chan, blocks, part, lists, counts, place, *refs):
    q_ref, k_ref, v_ref, cw_ref = refs[:4]
    if part == "interior":
        sides = ()
        values, p_ref, scale_ref, charge_ref, near_big, kaug, v0, sems = refs[4:]
        atoms, width = values.shape[2], near_big.shape[2]
        cut = values.at[pl.ds(1, near_big.shape[0]), :, columns_of(place, width, atoms, False)]
        cutting = pltpu.make_async_copy(cut, near_big, sems.at[0])
        cutting.start()
    else:
        sides, (p_ref, scale_ref, charge_ref, kaug, v0) = refs[4:7], refs[7:]
    first = place[0] * blocks
    total = counts.shape[0]
    lane = lax.broadcasted_iota(jnp.int32, (16, BS), 1)
    row = lax.broadcasted_iota(jnp.int32, (16, BS), 0)
    top_row = jnp.where(row == 0, 1.0, 0.0).astype(BF)

    def fill(b, keys, values):
        index = first + b - REACH
        inside = (index >= 0) & (index < total)
        live = jnp.where(inside, counts[jnp.clip(index, 0, total - 1)], 0)
        bias = jnp.where((row == 0) & (lane >= live), -1e30, 0.0).astype(BF)
        for h in range(heads):
            for copy in range(3):
                kaug[b, h, copy * head_dim : (copy + 1) * head_dim, :] = keys[h * head_dim : (h + 1) * head_dim]
            kaug[b, h, 3 * head_dim : 3 * head_dim + 16, :] = bias
            v0[b, h, 0:head_chan] = values[h * head_chan : (h + 1) * head_chan]
            v0[b, h, head_chan : head_chan + 16] = top_row

    for b in range(blocks):
        cols = slice(b * BS, (b + 1) * BS)
        fill(b + REACH, k_ref[:, cols], v_ref[:, cols])
    if sides:
        for far, side in zip((True, False), sides[:2]):
            base = jnp.where(on_left(place, far), 0, blocks + REACH)
            for b in range(REACH):
                cols = slice(b * BS, (b + 1) * BS)
                fill(base + b, side[0 : heads * head_dim, cols], side[heads * head_dim :, cols])
        inner = slice(REACH * BS, (blocks - REACH) * BS)
        charge_ref[:, inner] = sides[2][:, inner]
    else:
        charge_ref[...] = jnp.zeros_like(charge_ref)

    def block_of(i):
        return i + REACH if part == "interior" else edge_block(i, place, blocks)

    def columns(g):
        return pl.ds(pl.multiple_of(g * BS, BS), BS)

    def scores_of(i, h):
        g = block_of(i)
        listed = [lists[e, g] - (first - REACH) for e in range(NNB)]
        q = q_ref[h * head_dim : (h + 1) * head_dim, columns(g)].astype(F32) * (head_dim ** (-0.5) * LOG2E)
        qa = jnp.concatenate([*thirds(q), top_row], axis=0)
        return listed, [dot(kaug[b, h], qa, ((0,), (0,))) for b in listed]

    steps = p_ref.shape[0]
    pairs = [(i, h) for i in range(steps) for h in range(heads)]
    coming = scores_of(*pairs[0])
    charge = None
    for at, (i, h) in enumerate(pairs):
        listed, scores = coming
        if at + 1 < len(pairs):
            coming = scores_of(*pairs[at + 1])
        g = block_of(i)
        top = functools.reduce(jnp.maximum, [jnp.max(s, axis=0, keepdims=True) for s in scores])
        mixed = 0.0
        for e, b in enumerate(listed):
            w16 = jnp.exp2(scores[e] - top).astype(BF)
            p_ref[i, h, e * BS : (e + 1) * BS, :] = w16
            mixed = mixed + dot(v0[b, h], w16, ((1,), (0,)))
        live_q = lane[0:1] < counts[first + g]
        scale = jnp.where(live_q, 1.0 / mixed[head_chan : head_chan + 1], 0.0)
        scale_ref[i, h : h + 1, :] = scale
        att0 = (mixed[:head_chan] * scale).astype(BF)
        term = dot(cw_ref[:, h * head_chan : (h + 1) * head_chan], att0, ((1,), (0,)))
        charge = term if h == 0 else charge + term
        if h == heads - 1:
            charge_ref[:, columns(g)] = charge
    if part == "interior":
        cutting.wait()


def scores_call(part, lists, counts, place, q, k, v0, cw, sides, heads, head_dim):
    chans, atoms = v0.shape
    blocks = atoms // BS
    nq = cw.shape[0]
    head_chan = chans // heads
    band = blocks + 2 * REACH
    steps = blocks - 2 * REACH if part == "interior" else 2 * REACH
    whole = lambda shape: pl.BlockSpec(shape, lambda g, *_: (0,) * len(shape), pipeline_mode=pl.Buffered(1))
    shapes = [((steps, heads, NNB * BS, BS), BF), ((steps, heads, BS), F32), ((nq, atoms), F32)]
    interior = part == "interior"
    cuts = [((sides[0].shape[0] - 1, chans, REACH * BS), BF)] if interior else []
    if interior:
        sides = [pltpu.with_memory_space_constraint(x, pltpu.HBM) for x in sides]
    return pl.pallas_call(
        functools.partial(score_kernel, heads, head_dim, head_chan, blocks, part),
        grid_spec=pltpu.PrefetchScalarGridSpec(
            num_scalar_prefetch=3,
            grid=(1,),
            in_specs=[whole(x.shape) for x in (q, k, v0, cw)]
            + [pl.BlockSpec(memory_space=pltpu.HBM) if interior else whole(x.shape) for x in sides],
            out_specs=[whole(shape) for shape, _ in shapes] + [pl.BlockSpec(memory_space=pl.ANY)] * len(cuts),
            scratch_shapes=[
                pltpu.VMEM((band, heads, 3 * head_dim + 16, BS), BF),
                pltpu.VMEM((band, heads, head_chan + 16, BS), BF),
            ]
            + [pltpu.SemaphoreType.DMA((1,))] * len(cuts),
        ),
        out_shape=[jax.ShapeDtypeStruct(*x) for x in shapes + cuts],
        compiler_params=params(16),
        cost_estimate=pl.CostEstimate(
            flops=steps * heads * NNB * BS * BS * 200, transcendentals=steps * heads * NNB * BS * BS,
            bytes_accessed=steps * heads * NNB * BS * BS * 2,
        ),
    )(lists, counts, place, q, k, v0, cw, *sides)


def mix_kernel(heads, head_dim, head_chan, blocks, part, skip, lists, place, v_ref, p_ref, scale_ref, *refs):
    halo, out_ref = refs[: 2 if part in ("far", "near") else 0], refs[-2 if part in ("far", "near") else -1]
    comps = v_ref.shape[0]
    i = pl.program_id(0)
    offset = place[0] * blocks
    if halo:
        small, big = halo
        band = refs[-1]
        span = 3 * REACH
        left = on_left(place, part == "far")
        begin = jnp.where(left, 0, blocks + 2 * REACH - span)

        @pl.when(i == 0)
        def _():
            own = jnp.where(left, REACH, 0)
            first = jnp.where(left, 0, blocks - 2 * REACH)
            for b in range(2 * REACH):
                band[own + b] = v_ref[:, :, pl.ds(pl.multiple_of((first + b) * BS, BS), BS)]
            other = jnp.where(left, 0, 2 * REACH)
            for b in range(REACH):
                cols = slice(b * BS, (b + 1) * BS)
                band[other + b, 0] = small[heads * head_dim :, cols]
                band[other + b, 1:] = big[:, :, cols]

        g = edge_block(i if part == "far" else i + REACH, place, blocks)
        listed = [lists[e, g] - offset + REACH - begin for e in range(NNB)]
        pick = lambda b, rows: band[b, :, rows, :]
    else:
        g = i + (REACH if part == "low" else blocks // 2)
        listed = [lists[e, g] - offset for e in range(NNB)]
        pick = lambda b, rows: v_ref[:, rows, pl.ds(pl.multiple_of(b * BS, BS), BS)]
    for h in range(heads):
        rows = slice(h * head_chan, (h + 1) * head_chan)
        acc = 0.0
        for e in range(NNB):
            v = pick(listed[e], rows).reshape(comps * head_chan, BS)
            acc = acc + dot(v, p_ref[i + skip, h, e * BS : (e + 1) * BS, :], ((1,), (0,)))
        acc = acc * scale_ref[i + skip, h : h + 1, :]
        out_ref[:, rows, :] = acc.astype(BF).reshape(comps, head_chan, BS)


def mix_call(part, lists, place, v, p, scale, halo, prev, heads, head_dim):
    comps, chans, atoms = v.shape
    blocks = atoms // BS
    half = blocks // 2 - REACH
    steps = REACH if halo else half
    skip = {"low": 0, "high": half, "far": 0, "near": REACH}[part]

    def at(i, lists, place):
        if part in ("low", "high"):
            return i + REACH + skip
        return edge_block(i + skip, place, blocks)

    whole = lambda shape: pl.BlockSpec(shape, lambda g, *_: (0,) * len(shape), pipeline_mode=pl.Buffered(1))
    extra = list(halo) + ([] if prev is None else [prev])
    return pl.pallas_call(
        functools.partial(mix_kernel, heads, head_dim, chans // heads, blocks, part, skip),
        grid_spec=pltpu.PrefetchScalarGridSpec(
            num_scalar_prefetch=2,
            grid=(steps,),
            in_specs=[
                whole(v.shape),
                whole(p.shape),
                whole(scale.shape),
            ]
            + [whole(x.shape) for x in halo]
            + ([] if prev is None else [pl.BlockSpec(memory_space=pl.ANY)]),
            out_specs=pl.BlockSpec((comps, chans, BS), lambda i, *s: (0, 0, at(i, *s))),
            scratch_shapes=[pltpu.VMEM((3 * REACH, comps, chans, BS), BF)] if halo else [],
        ),
        out_shape=jax.ShapeDtypeStruct(v.shape, BF),
        input_output_aliases={} if prev is None else {4 + len(extra): 0},
        compiler_params=params(16),
        cost_estimate=pl.CostEstimate(
            flops=steps * chans * comps * NNB * BS * BS * 2, transcendentals=0,
            bytes_accessed=steps * chans * comps * BS * 8,
        ),
    )(lists, place, v, p, scale, *extra)


SPREAD = 2 * KMAX + 1
WIDE = 16


def wave(turns):
    r = turns - jnp.round(turns)
    u = r * r
    return horner(COS, u), horner(SIN, u) * r


def grid_points(base, planes):
    rows = planes * SPREAD * WIDE
    place = lax.broadcasted_iota(jnp.int32, (1, rows), 1).astype(F32)
    pair = jnp.floor((place + 0.5) * (1.0 / WIDE))
    n3 = place - pair * WIDE - KMAX
    plane = jnp.floor((pair + 0.5) * (1.0 / SPREAD))
    return plane + base.astype(F32), pair - plane * SPREAD - KMAX, n3


def grid_weights(n, base, planes):
    pairs = planes * SPREAD
    high = -(-pairs // 16) * 16
    flip = jnp.where(n[0:1] < 0, -1, 1)
    pair = (n[0:1] * flip - base) * SPREAD + n[1:2] * flip + KMAX
    mine = (n[0:1] * flip >= base) & (n[0:1] * flip < base + planes)
    third = n[2:3] * flip + KMAX
    count = n.shape[1]
    is_pair = (lax.broadcasted_iota(jnp.int32, (high, count), 0) == pair) & mine
    is_third = lax.broadcasted_iota(jnp.int32, (WIDE, count), 0) == third
    one_hot = lambda x: jnp.where(x, 1.0, 0.0).astype(BF)
    found = dot(one_hot(is_pair), one_hot(is_third), ((1,), (1,)))
    rows = pairs * WIDE
    row = lax.broadcasted_iota(jnp.int32, (WIDE, rows), 0)
    spread = one_hot((lax.broadcasted_iota(jnp.int32, (WIDE, rows), 1) & (WIDE - 1)) == row)
    wide = sum(dot(part, spread, ((1,), (0,))) for part in thirds(found))
    own = lax.broadcasted_iota(jnp.int32, (high, rows), 1) >> (WIDE.bit_length() - 1)
    times = jnp.sum(jnp.where(own == lax.broadcasted_iota(jnp.int32, (high, rows), 0), wide, 0.0), axis=0, keepdims=True)
    n1, n2, n3 = grid_points(base, planes)
    norm = n1 * n1 + n2 * n2 + n3 * n3
    safe = jnp.maximum(norm, 1.0)
    return jnp.where(norm > 0, times * (ewald_scale * jnp.exp(-ewald_damp * safe) / safe), 0.0)


def table_kernel(planes, step, place, n_ref, f_ref, out_ref, weight_ref, pairs):
    base = place[1] * planes
    weight_ref[...] = grid_weights(n_ref[...], base, planes)
    steps = (lax.broadcasted_iota(jnp.int32, (WIDE, step), 0) - KMAX).astype(F32)
    for start in range(0, f_ref.shape[1], step):
        cols = slice(start, start + step)
        second = wave(steps * f_ref[1:2, cols])
        third = wave(steps * f_ref[2:3, cols])
        for plane in range(planes):
            first = wave((base + plane).astype(F32) * f_ref[0:1, cols])
            pairs[0, plane] = first[0] * second[0] - first[1] * second[1]
            pairs[1, plane] = first[1] * second[0] + first[0] * second[1]
            for m in range(SPREAD):
                real, imag = pairs[0, plane, m : m + 1, :], pairs[1, plane, m : m + 1, :]
                at = slice((plane * SPREAD + m) * WIDE, (plane * SPREAD + m + 1) * WIDE)
                out_ref[0, at, cols] = (real * third[0] - imag * third[1]).astype(BF)
                out_ref[1, at, cols] = (imag * third[0] + real * third[1]).astype(BF)


def table_call(place, n, f, planes):
    rows = planes * SPREAD * WIDE
    atoms = f.shape[1]
    step = 256
    whole = lambda shape: pl.BlockSpec(shape, lambda g, *_: (0,) * len(shape), pipeline_mode=pl.Buffered(1))
    return pl.pallas_call(
        functools.partial(table_kernel, planes, step),
        grid_spec=pltpu.PrefetchScalarGridSpec(
            num_scalar_prefetch=1,
            grid=(1,),
            in_specs=[whole(n.shape), whole(f.shape)],
            out_specs=[whole((2, rows, atoms)), whole((1, rows))],
            scratch_shapes=[pltpu.VMEM((2, planes, WIDE, step), F32)],
        ),
        out_shape=[jax.ShapeDtypeStruct((2, rows, atoms), BF), jax.ShapeDtypeStruct((1, rows), F32)],
        compiler_params=params(12),
        cost_estimate=pl.CostEstimate(flops=rows * atoms * 40, transcendentals=0, bytes_accessed=rows * atoms * 4),
        name="table",
    )(place, n, f)


def structure_kernel(inv_root, c_ref, t_ref, out_ref):
    high, low = halves(c_ref[...])
    both = jnp.concatenate([high, low], axis=0)
    s = dot(t_ref[...], both, ((1,), (1,)))
    nq = c_ref.shape[0]
    out_ref[...] = (s[:, :nq] + s[:, nq:]).T * inv_root


def structure_call(c, table, inv_root):
    rows, atoms = table.shape
    step = rows
    nq = c.shape[0]
    return pl.pallas_call(
        functools.partial(structure_kernel, inv_root),
        grid=(rows // step,),
        in_specs=[pl.BlockSpec((nq, atoms), lambda i: (0, 0)), pl.BlockSpec((step, atoms), lambda i: (i, 0))],
        out_specs=pl.BlockSpec((nq, step), lambda i: (0, i)),
        out_shape=jax.ShapeDtypeStruct((nq, rows), F32),
        compiler_params=params(12),
        cost_estimate=pl.CostEstimate(flops=rows * atoms * 512, transcendentals=0, bytes_accessed=rows * atoms * 2),
        name="structure",
    )(c, table)


def field_kernel(planes, step, place, s_ref, weight_ref, c_ref, t_ref, out_ref):
    nq = c_ref.shape[0]
    waves = weight_ref.shape[1]
    n = grid_points(place[1] * planes, planes)
    real = s_ref[:, :waves] * weight_ref[...]
    imag = s_ref[:, waves:] * weight_ref[...]
    with_cos = jnp.concatenate([real] + [-imag * n[d] for d in range(3)], axis=0)
    with_sin = jnp.concatenate([imag] + [real * n[d] for d in range(3)], axis=0)
    with_cos, with_sin = [jnp.concatenate(halves(x), axis=0) for x in (with_cos, with_sin)]
    for start in range(0, c_ref.shape[1], step):
        cols = slice(start, start + step)
        both = dot(with_cos, t_ref[0, :, cols], ((1,), (0,))) + dot(with_sin, t_ref[1, :, cols], ((1,), (0,)))
        sums = both[: 4 * nq] + both[4 * nq :]
        c = c_ref[:, cols]
        out_ref[0:nq, cols] = sums[:nq]
        forces = [
            jnp.sum(c * sums[(d + 1) * nq : (d + 2) * nq], axis=0, keepdims=True) for d in range(3)
        ]
        out_ref[nq : nq + 8, cols] = jnp.concatenate(forces + [jnp.zeros((5, step), F32)], axis=0)


def field_call(place, s, weight, c, table, planes):
    _, rows, atoms = table.shape
    nq = c.shape[0]
    whole = lambda shape: pl.BlockSpec(shape, lambda g, *_: (0,) * len(shape), pipeline_mode=pl.Buffered(1))
    return pl.pallas_call(
        functools.partial(field_kernel, planes, 512),
        grid_spec=pltpu.PrefetchScalarGridSpec(
            num_scalar_prefetch=1,
            grid=(1,),
            in_specs=[whole(x.shape) for x in (s, weight, c, table)],
            out_specs=whole((nq + 8, atoms)),
        ),
        out_shape=jax.ShapeDtypeStruct((nq + 8, atoms), F32),
        compiler_params=params(12),
        cost_estimate=pl.CostEstimate(flops=rows * atoms * 512, transcendentals=0, bytes_accessed=rows * atoms * 2),
        name="fields",
    )(place, s, weight, c, table)


def finish_kernel(mine_ref, theirs_ref, potential_ref, force_ref):
    nq = potential_ref.shape[0]
    total = mine_ref[...].astype(F32) + theirs_ref[...].astype(F32)
    potential_ref[...] = total[:nq]
    force_ref[...] = total[nq : nq + 3]


def finish_call(mine, theirs, nq):
    atoms = mine.shape[1]
    return pl.pallas_call(
        finish_kernel,
        out_shape=[jax.ShapeDtypeStruct((nq, atoms), F32), jax.ShapeDtypeStruct((3, atoms), F32)],
        compiler_params=pltpu.CompilerParams(vmem_limit_bytes=4 << 20),
        name="finish",
    )(mine, theirs)


def exchanged(x, axis, step):
    size = lax.axis_size(axis)
    if step >= size:
        return x
    return x + lax.ppermute(x, axis, [(i, i ^ step) for i in range(size)])


def summed(x, axis, step=1, stop=None):
    size = lax.axis_size(axis)
    assert size & (size - 1) == 0
    while step < (stop or size):
        x = exchanged(x, axis, step)
        step *= 2
    return x


def whole_step(
    queries,
    key_states,
    value_states,
    fractional,
    block_counts,
    neighbors,
    integer_wave_vectors,
    charge_weight,
):
    heads, head_dim, atoms = queries.shape
    nq = charge_weight.shape[1]
    planes = (KMAX + 1) // lax.axis_size("inner")
    assert planes * lax.axis_size("inner") == KMAX + 1
    inv_root = 1.0 / math.sqrt(atoms * lax.axis_size("seq"))
    place = jnp.stack([lax.axis_index("seq"), lax.axis_index("inner")]).astype(jnp.int32)
    width = REACH * BS
    count = lax.axis_size("seq")
    near_pairs = [(i, i ^ 1) for i in range(count)]
    far_pairs = [(i, i + 1 if i % 2 else i - 1) for i in range(1, count - 1)]

    def swap(x, pairs):
        return lax.ppermute(x, "seq", pairs)

    values = value_states.transpose(1, 0, 2)
    keys = key_states.reshape(heads * head_dim, atoms)
    asked = queries.reshape(heads * head_dim, atoms)
    near, far, far_big, v0, keys, asked, weight, counts, lists = load_call(
        place, keys, values, (asked, charge_weight.T, block_counts, neighbors.T), width
    )
    vectors = integer_wave_vectors
    far = swap(far, far_pairs)
    near = swap(near, near_pairs)
    far_big = swap(far_big, far_pairs)

    p_in, scale_in, part, near_big = scores_call(
        "interior", lists, counts, place, asked, keys, v0, weight, (values,), heads, head_dim
    )
    near_big = swap(near_big, near_pairs)
    p_out, scale_out, part = scores_call(
        "edges", lists, counts, place, asked, keys, v0, weight, (far, near, part), heads, head_dim
    )
    table, wave_weight = table_call(place, vectors, fractional, planes)
    last = lax.axis_size("inner") // 2

    def halfway(x):
        x = summed(x, "inner", stop=last).astype(BF)
        return x, lax.ppermute(x, "inner", [(i, i ^ last) for i in range(2 * last)])

    mine, theirs = halfway(part)
    charges = mine.astype(F32) + theirs.astype(F32)
    structure = structure_call(charges, table.reshape(-1, atoms), inv_root)
    structure = summed(structure, "seq")
    fields = field_call(place, structure, wave_weight, charges, table, planes)
    fields, others = halfway(fields)
    potential, forces = finish_call(fields, others, nq)

    mix = functools.partial(mix_call, heads=heads, head_dim=head_dim)
    attention = mix("low", lists, place, values, p_in, scale_in, (), None)
    attention = mix("far", lists, place, values, p_out, scale_out, (far, far_big), attention)
    attention = mix("high", lists, place, values, p_in, scale_in, (), attention)
    attention = mix("near", lists, place, values, p_out, scale_out, (near, near_big), attention)
    return (attention.transpose(1, 0, 2), potential, forces)


def solution(mesh):
    placed = (
        P("inner", None, "seq"),
        P("inner", None, "seq"),
        P("inner", None, "seq"),
        P(None, "seq"),
        P(),
        P("seq", None),
        P(),
        P("inner", None),
    )
    return jax.shard_map(
        whole_step,
        mesh=mesh,
        in_specs=placed,
        out_specs=(P("inner", None, "seq"), P(None, "seq"), P(None, "seq")),
        check_vma=False,
    )
```

```python
import functools
import math

import jax
import jax.numpy as jnp
from jax import lax
from jax.experimental import pallas as pl
from jax.experimental.pallas import tpu as pltpu
from jax.sharding import PartitionSpec as P


BS = 256
NNB = 3
REACH = 2
KMAX = 7
LOG2E = 1.4426950408889634

ewald_scale = 40.0
ewald_damp = 0.02

BF = jnp.bfloat16
F32 = jnp.float32

SIN = (6.283185302511499, -41.34170040531678, 81.60513138577247, -76.70301535353673,
       42.02592698394968, -14.899846662448152, 3.2381375038938693)
COS = (0.9999999890590217, -19.73920449945376, 64.93911745989128, -85.45013953083522,
       60.167630950695504, -25.967599247822193, 6.5286581606558824)


def params(mib):
    return pltpu.CompilerParams(vmem_limit_bytes=mib << 20, dimension_semantics=("arbitrary",))


def dot(a, b, dims):
    return lax.dot_general(a, b, (dims, ((), ())), preferred_element_type=F32)


def horner(coeffs, u):
    total = coeffs[-1]
    for c in coeffs[-2::-1]:
        total = total * u + c
    return total


def halves(x):
    high = x.astype(BF)
    return high, (x - high.astype(F32)).astype(BF)


def thirds(x):
    high, low = halves(x)
    return high, low, ((x - high.astype(F32)) - low.astype(F32)).astype(BF)


def columns_of(place, width, atoms, far):
    first = on_left(place, far)
    return pl.ds(pl.multiple_of(jnp.where(first, 0, atoms - width), 128), width)


def run(moves, sems):
    started = [pltpu.make_async_copy(src, dst, sems.at[i]) for i, (src, dst) in enumerate(moves)]
    for copy in started:
        copy.start()
    for copy in started:
        copy.wait()


def load_kernel(place, k, v, *refs):
    others, (near, far, far_big, v0, *copies), sems = refs[: (len(refs) - 6) // 2], refs[(len(refs) - 6) // 2 : -1], refs[-1]
    rows, atoms = k.shape
    chans, width = v.shape[1], near.shape[1]
    moves = []
    for piece, is_far in ((far, True), (near, False)):
        cols = columns_of(place, width, atoms, is_far)
        moves.append((k.at[:, cols], piece.at[pl.ds(0, rows)]))
        moves.append((v.at[0, :, cols], piece.at[pl.ds(rows, chans)]))
    moves += list(zip((k, *others), copies)) + [(v.at[0], v0)]
    moves.append((v.at[pl.ds(1, far_big.shape[0]), :, columns_of(place, width, atoms, True)], far_big))
    run(moves, sems)


def load_call(place, k, v, others, width):
    comps, chans, atoms = v.shape
    shape = jax.ShapeDtypeStruct
    outs = [shape((k.shape[0] + chans, width), BF)] * 2 + [shape((comps - 1, chans, width), BF)]
    outs += [shape((chans, atoms), BF)] + [shape(x.shape, x.dtype) for x in (k, *others)]
    operands = (k, v, *others)
    return pl.pallas_call(
        load_kernel,
        grid_spec=pltpu.PrefetchScalarGridSpec(
            num_scalar_prefetch=1,
            grid=(1,),
            in_specs=[pl.BlockSpec(memory_space=pltpu.HBM)] * len(operands),
            out_specs=[pl.BlockSpec(memory_space=pl.ANY)] * len(outs),
            scratch_shapes=[pltpu.SemaphoreType.DMA((7 + len(others),))],
        ),
        out_shape=outs,
        compiler_params=params(2),
        cost_estimate=pl.CostEstimate(flops=0, transcendentals=0, bytes_accessed=1 << 20),
        name="load",
    )(place, *[pltpu.with_memory_space_constraint(x, pltpu.HBM) for x in operands])


def on_left(place, far):
    even = place[0] % 2 == 0
    return even if far else jnp.logical_not(even)


def edge_block(step, place, blocks):
    left = (step < REACH) == (place[0] % 2 == 0)
    return step % REACH + jnp.where(left, 0, blocks - REACH)


def score_kernel(heads, head_dim, head_chan, blocks, part, lists, counts, place, *refs):
    q_ref, k_ref, v_ref, cw_ref = refs[:4]
    if part == "interior":
        sides = ()
        values, p_ref, scale_ref, charge_ref, near_big, kaug, v0, sems = refs[4:]
        atoms, width = values.shape[2], near_big.shape[2]
        cut = values.at[pl.ds(1, near_big.shape[0]), :, columns_of(place, width, atoms, False)]
        cutting = pltpu.make_async_copy(cut, near_big, sems.at[0])
        cutting.start()
    else:
        sides, (p_ref, scale_ref, charge_ref, kaug, v0) = refs[4:7], refs[7:]
    first = place[0] * blocks
    total = counts.shape[0]
    lane = lax.broadcasted_iota(jnp.int32, (16, BS), 1)
    row = lax.broadcasted_iota(jnp.int32, (16, BS), 0)
    top_row = jnp.where(row == 0, 1.0, 0.0).astype(BF)

    def fill(b, keys, values):
        index = first + b - REACH
        inside = (index >= 0) & (index < total)
        live = jnp.where(inside, counts[jnp.clip(index, 0, total - 1)], 0)
        bias = jnp.where((row == 0) & (lane >= live), -1e30, 0.0).astype(BF)
        for h in range(heads):
            for copy in range(3):
                kaug[b, h, copy * head_dim : (copy + 1) * head_dim, :] = keys[h * head_dim : (h + 1) * head_dim]
            kaug[b, h, 3 * head_dim : 3 * head_dim + 16, :] = bias
            v0[b, h, 0:head_chan] = values[h * head_chan : (h + 1) * head_chan]
            v0[b, h, head_chan : head_chan + 16] = top_row

    for b in range(blocks):
        cols = slice(b * BS, (b + 1) * BS)
        fill(b + REACH, k_ref[:, cols], v_ref[:, cols])
    if sides:
        for far, side in zip((True, False), sides[:2]):
            base = jnp.where(on_left(place, far), 0, blocks + REACH)
            for b in range(REACH):
                cols = slice(b * BS, (b + 1) * BS)
                fill(base + b, side[0 : heads * head_dim, cols], side[heads * head_dim :, cols])
        inner = slice(REACH * BS, (blocks - REACH) * BS)
        charge_ref[:, inner] = sides[2][:, inner]
    else:
        charge_ref[...] = jnp.zeros_like(charge_ref)

    def block_of(i):
        return i + REACH if part == "interior" else edge_block(i, place, blocks)

    def columns(g):
        return pl.ds(pl.multiple_of(g * BS, BS), BS)

    def scores_of(i, h):
        g = block_of(i)
        listed = [lists[e, g] - (first - REACH) for e in range(NNB)]
        q = q_ref[h * head_dim : (h + 1) * head_dim, columns(g)].astype(F32) * (head_dim ** (-0.5) * LOG2E)
        qa = jnp.concatenate([*thirds(q), top_row], axis=0)
        return listed, [dot(kaug[b, h], qa, ((0,), (0,))) for b in listed]

    steps = p_ref.shape[0]
    pairs = [(i, h) for i in range(steps) for h in range(heads)]
    coming = scores_of(*pairs[0])
    charge = None
    for at, (i, h) in enumerate(pairs):
        listed, scores = coming
        if at + 1 < len(pairs):
            coming = scores_of(*pairs[at + 1])
        g = block_of(i)
        top = functools.reduce(jnp.maximum, [jnp.max(s, axis=0, keepdims=True) for s in scores])
        mixed = 0.0
        for e, b in enumerate(listed):
            w16 = jnp.exp2(scores[e] - top).astype(BF)
            p_ref[i, h, e * BS : (e + 1) * BS, :] = w16
            mixed = mixed + dot(v0[b, h], w16, ((1,), (0,)))
        live_q = lane[0:1] < counts[first + g]
        scale = jnp.where(live_q, 1.0 / mixed[head_chan : head_chan + 1], 0.0)
        scale_ref[i, h : h + 1, :] = scale
        att0 = (mixed[:head_chan] * scale).astype(BF)
        term = dot(cw_ref[:, h * head_chan : (h + 1) * head_chan], att0, ((1,), (0,)))
        charge = term if h == 0 else charge + term
        if h == heads - 1:
            charge_ref[:, columns(g)] = charge
    if part == "interior":
        cutting.wait()


def scores_call(part, lists, counts, place, q, k, v0, cw, sides, heads, head_dim):
    chans, atoms = v0.shape
    blocks = atoms // BS
    nq = cw.shape[0]
    head_chan = chans // heads
    band = blocks + 2 * REACH
    steps = blocks - 2 * REACH if part == "interior" else 2 * REACH
    whole = lambda shape: pl.BlockSpec(shape, lambda g, *_: (0,) * len(shape), pipeline_mode=pl.Buffered(1))
    shapes = [((steps, heads, NNB * BS, BS), BF), ((steps, heads, BS), F32), ((nq, atoms), F32)]
    interior = part == "interior"
    cuts = [((sides[0].shape[0] - 1, chans, REACH * BS), BF)] if interior else []
    if interior:
        sides = [pltpu.with_memory_space_constraint(x, pltpu.HBM) for x in sides]
    return pl.pallas_call(
        functools.partial(score_kernel, heads, head_dim, head_chan, blocks, part),
        grid_spec=pltpu.PrefetchScalarGridSpec(
            num_scalar_prefetch=3,
            grid=(1,),
            in_specs=[whole(x.shape) for x in (q, k, v0, cw)]
            + [pl.BlockSpec(memory_space=pltpu.HBM) if interior else whole(x.shape) for x in sides],
            out_specs=[whole(shape) for shape, _ in shapes] + [pl.BlockSpec(memory_space=pl.ANY)] * len(cuts),
            scratch_shapes=[
                pltpu.VMEM((band, heads, 3 * head_dim + 16, BS), BF),
                pltpu.VMEM((band, heads, head_chan + 16, BS), BF),
            ]
            + [pltpu.SemaphoreType.DMA((1,))] * len(cuts),
        ),
        out_shape=[jax.ShapeDtypeStruct(*x) for x in shapes + cuts],
        compiler_params=params(16),
        cost_estimate=pl.CostEstimate(
            flops=steps * heads * NNB * BS * BS * 200, transcendentals=steps * heads * NNB * BS * BS,
            bytes_accessed=steps * heads * NNB * BS * BS * 2,
        ),
    )(lists, counts, place, q, k, v0, cw, *sides)


def mix_kernel(heads, head_dim, head_chan, blocks, part, skip, lists, place, v_ref, p_ref, scale_ref, *refs):
    halo, out_ref = refs[: 2 if part in ("far", "near") else 0], refs[-2 if part in ("far", "near") else -1]
    comps = v_ref.shape[0]
    i = pl.program_id(0)
    offset = place[0] * blocks
    if halo:
        small, big = halo
        band = refs[-1]
        span = 3 * REACH
        left = on_left(place, part == "far")
        begin = jnp.where(left, 0, blocks + 2 * REACH - span)

        @pl.when(i == 0)
        def _():
            own = jnp.where(left, REACH, 0)
            first = jnp.where(left, 0, blocks - 2 * REACH)
            for b in range(2 * REACH):
                band[own + b] = v_ref[:, :, pl.ds(pl.multiple_of((first + b) * BS, BS), BS)]
            other = jnp.where(left, 0, 2 * REACH)
            for b in range(REACH):
                cols = slice(b * BS, (b + 1) * BS)
                band[other + b, 0] = small[heads * head_dim :, cols]
                band[other + b, 1:] = big[:, :, cols]

        g = edge_block(i if part == "far" else i + REACH, place, blocks)
        listed = [lists[e, g] - offset + REACH - begin for e in range(NNB)]
        pick = lambda b, rows: band[b, :, rows, :]
    else:
        g = i + (REACH if part == "low" else blocks // 2)
        listed = [lists[e, g] - offset for e in range(NNB)]
        pick = lambda b, rows: v_ref[:, rows, pl.ds(pl.multiple_of(b * BS, BS), BS)]
    for h in range(heads):
        rows = slice(h * head_chan, (h + 1) * head_chan)
        acc = 0.0
        for e in range(NNB):
            v = pick(listed[e], rows).reshape(comps * head_chan, BS)
            acc = acc + dot(v, p_ref[i + skip, h, e * BS : (e + 1) * BS, :], ((1,), (0,)))
        acc = acc * scale_ref[i + skip, h : h + 1, :]
        out_ref[:, rows, :] = acc.astype(BF).reshape(comps, head_chan, BS)


def mix_call(part, lists, place, v, p, scale, halo, prev, heads, head_dim):
    comps, chans, atoms = v.shape
    blocks = atoms // BS
    half = blocks // 2 - REACH
    steps = REACH if halo else half
    skip = {"low": 0, "high": half, "far": 0, "near": REACH}[part]

    def at(i, lists, place):
        if part in ("low", "high"):
            return i + REACH + skip
        return edge_block(i + skip, place, blocks)

    whole = lambda shape: pl.BlockSpec(shape, lambda g, *_: (0,) * len(shape), pipeline_mode=pl.Buffered(1))
    extra = list(halo) + ([] if prev is None else [prev])
    return pl.pallas_call(
        functools.partial(mix_kernel, heads, head_dim, chans // heads, blocks, part, skip),
        grid_spec=pltpu.PrefetchScalarGridSpec(
            num_scalar_prefetch=2,
            grid=(steps,),
            in_specs=[
                whole(v.shape),
                whole(p.shape),
                whole(scale.shape),
            ]
            + [whole(x.shape) for x in halo]
            + ([] if prev is None else [pl.BlockSpec(memory_space=pl.ANY)]),
            out_specs=pl.BlockSpec((comps, chans, BS), lambda i, *s: (0, 0, at(i, *s))),
            scratch_shapes=[pltpu.VMEM((3 * REACH, comps, chans, BS), BF)] if halo else [],
        ),
        out_shape=jax.ShapeDtypeStruct(v.shape, BF),
        input_output_aliases={} if prev is None else {4 + len(extra): 0},
        compiler_params=params(16),
        cost_estimate=pl.CostEstimate(
            flops=steps * chans * comps * NNB * BS * BS * 2, transcendentals=0,
            bytes_accessed=steps * chans * comps * BS * 8,
        ),
    )(lists, place, v, p, scale, *extra)


def own_kernel(heads, head_chan, blocks, lists, place, v_ref, p_ref, sum_ref):
    comps = v_ref.shape[0]
    for i in range(REACH):
        g = edge_block(i + REACH, place, blocks)
        for h in range(heads):
            rows = slice(h * head_chan, (h + 1) * head_chan)
            acc = 0.0
            for e in range(NNB):
                b = lists[e, g] - place[0] * blocks
                own = jnp.where((b >= 0) & (b < blocks), 1.0, 0.0)
                cols = pl.ds(pl.multiple_of(jnp.clip(b, 0, blocks - 1) * BS, BS), BS)
                v = v_ref[:, rows, cols].reshape(comps * head_chan, BS)
                acc = acc + own * dot(v, p_ref[i + REACH, h, e * BS : (e + 1) * BS, :], ((1,), (0,)))
            sum_ref[i, h] = acc


def own_call(lists, place, v, p, heads):
    comps, chans, atoms = v.shape
    blocks = atoms // BS
    whole = lambda shape: pl.BlockSpec(shape, lambda g, *_: (0,) * len(shape), pipeline_mode=pl.Buffered(1))
    shape = (REACH, heads, comps * chans // heads, BS)
    return pl.pallas_call(
        functools.partial(own_kernel, heads, chans // heads, blocks),
        grid_spec=pltpu.PrefetchScalarGridSpec(
            num_scalar_prefetch=2,
            grid=(1,),
            in_specs=[whole(v.shape), whole(p.shape)],
            out_specs=whole(shape),
        ),
        out_shape=jax.ShapeDtypeStruct(shape, F32),
        compiler_params=params(16),
        cost_estimate=pl.CostEstimate(
            flops=REACH * chans * comps * NNB * BS * BS * 2, transcendentals=0,
            bytes_accessed=REACH * chans * comps * BS * 8,
        ),
        name="near_own",
    )(lists, place, v, p)


def near_kernel(heads, head_dim, head_chan, blocks, lists, place, sum_ref, p_ref, scale_ref, small, big, prev, out_ref, acc):
    i = pl.program_id(0)
    g = edge_block(i + REACH, place, blocks)
    comps = big.shape[0] + 1
    for h in range(heads):
        rows = slice(h * head_chan, (h + 1) * head_chan)
        first = heads * head_dim + h * head_chan
        acc[h] = sum_ref[i, h]
        for e in range(NNB):
            b = lists[e, g] - place[0] * blocks

            @pl.when((b < 0) | (b >= blocks))
            def _():
                at = jnp.clip(jnp.where(b < 0, b + REACH, b - blocks), 0, REACH - 1)
                cols = pl.ds(pl.multiple_of(at * BS, BS), BS)
                v = jnp.concatenate([small[first : first + head_chan, cols][None], big[:, rows, cols]], axis=0)
                v = v.reshape(comps * head_chan, BS)
                acc[h] += dot(v, p_ref[i + REACH, h, e * BS : (e + 1) * BS, :], ((1,), (0,)))

    for h in range(heads):
        rows = slice(h * head_chan, (h + 1) * head_chan)
        total = acc[h] * scale_ref[i + REACH, h : h + 1, :]
        out_ref[:, rows, :] = total.astype(BF).reshape(comps, head_chan, BS)


def near_call(lists, place, v_shape, sums, p, scale, halo, prev, heads, head_dim):
    comps, chans, atoms = v_shape
    blocks = atoms // BS
    whole = lambda shape: pl.BlockSpec(shape, lambda g, *_: (0,) * len(shape), pipeline_mode=pl.Buffered(1))
    return pl.pallas_call(
        functools.partial(near_kernel, heads, head_dim, chans // heads, blocks),
        grid_spec=pltpu.PrefetchScalarGridSpec(
            num_scalar_prefetch=2,
            grid=(REACH,),
            in_specs=[whole(x.shape) for x in (sums, p, scale, *halo)] + [pl.BlockSpec(memory_space=pl.ANY)],
            out_specs=pl.BlockSpec(
                (comps, chans, BS), lambda i, lists, place: (0, 0, edge_block(i + REACH, place, blocks))
            ),
            scratch_shapes=[pltpu.VMEM(sums.shape[1:], F32)],
        ),
        out_shape=jax.ShapeDtypeStruct(v_shape, BF),
        input_output_aliases={7: 0},
        compiler_params=params(16),
        cost_estimate=pl.CostEstimate(
            flops=REACH * chans * comps * NNB * BS * BS, transcendentals=0,
            bytes_accessed=REACH * chans * comps * BS * 8,
        ),
        name="mix_near",
    )(lists, place, sums, p, scale, *halo, prev)


SPREAD = 2 * KMAX + 1
WIDE = 16


def wave(turns):
    r = turns - jnp.round(turns)
    u = r * r
    return horner(COS, u), horner(SIN, u) * r


def grid_points(base, planes):
    rows = planes * SPREAD * WIDE
    place = lax.broadcasted_iota(jnp.int32, (1, rows), 1).astype(F32)
    pair = jnp.floor((place + 0.5) * (1.0 / WIDE))
    n3 = place - pair * WIDE - KMAX
    plane = jnp.floor((pair + 0.5) * (1.0 / SPREAD))
    return plane + base.astype(F32), pair - plane * SPREAD - KMAX, n3


def grid_weights(n, base, planes):
    pairs = planes * SPREAD
    high = -(-pairs // 16) * 16
    flip = jnp.where(n[0:1] < 0, -1, 1)
    pair = (n[0:1] * flip - base) * SPREAD + n[1:2] * flip + KMAX
    mine = (n[0:1] * flip >= base) & (n[0:1] * flip < base + planes)
    third = n[2:3] * flip + KMAX
    count = n.shape[1]
    is_pair = (lax.broadcasted_iota(jnp.int32, (high, count), 0) == pair) & mine
    is_third = lax.broadcasted_iota(jnp.int32, (WIDE, count), 0) == third
    one_hot = lambda x: jnp.where(x, 1.0, 0.0).astype(BF)
    found = dot(one_hot(is_pair), one_hot(is_third), ((1,), (1,)))
    rows = pairs * WIDE
    row = lax.broadcasted_iota(jnp.int32, (WIDE, rows), 0)
    spread = one_hot((lax.broadcasted_iota(jnp.int32, (WIDE, rows), 1) & (WIDE - 1)) == row)
    wide = sum(dot(part, spread, ((1,), (0,))) for part in thirds(found))
    own = lax.broadcasted_iota(jnp.int32, (high, rows), 1) >> (WIDE.bit_length() - 1)
    times = jnp.sum(jnp.where(own == lax.broadcasted_iota(jnp.int32, (high, rows), 0), wide, 0.0), axis=0, keepdims=True)
    n1, n2, n3 = grid_points(base, planes)
    norm = n1 * n1 + n2 * n2 + n3 * n3
    safe = jnp.maximum(norm, 1.0)
    return jnp.where(norm > 0, times * (ewald_scale * jnp.exp(-ewald_damp * safe) / safe), 0.0)


def table_kernel(planes, step, place, n_ref, f_ref, out_ref, weight_ref, pairs):
    base = place[1] * planes
    weight_ref[...] = grid_weights(n_ref[...], base, planes)
    steps = (lax.broadcasted_iota(jnp.int32, (WIDE, step), 0) - KMAX).astype(F32)
    for start in range(0, f_ref.shape[1], step):
        cols = slice(start, start + step)
        second = wave(steps * f_ref[1:2, cols])
        third = wave(steps * f_ref[2:3, cols])
        for plane in range(planes):
            first = wave((base + plane).astype(F32) * f_ref[0:1, cols])
            pairs[0, plane] = first[0] * second[0] - first[1] * second[1]
            pairs[1, plane] = first[1] * second[0] + first[0] * second[1]
            for m in range(SPREAD):
                real, imag = pairs[0, plane, m : m + 1, :], pairs[1, plane, m : m + 1, :]
                at = slice((plane * SPREAD + m) * WIDE, (plane * SPREAD + m + 1) * WIDE)
                out_ref[0, at, cols] = (real * third[0] - imag * third[1]).astype(BF)
                out_ref[1, at, cols] = (imag * third[0] + real * third[1]).astype(BF)


def table_call(place, n, f, planes):
    rows = planes * SPREAD * WIDE
    atoms = f.shape[1]
    step = 256
    whole = lambda shape: pl.BlockSpec(shape, lambda g, *_: (0,) * len(shape), pipeline_mode=pl.Buffered(1))
    return pl.pallas_call(
        functools.partial(table_kernel, planes, step),
        grid_spec=pltpu.PrefetchScalarGridSpec(
            num_scalar_prefetch=1,
            grid=(1,),
            in_specs=[whole(n.shape), whole(f.shape)],
            out_specs=[whole((2, rows, atoms)), whole((1, rows))],
            scratch_shapes=[pltpu.VMEM((2, planes, WIDE, step), F32)],
        ),
        out_shape=[jax.ShapeDtypeStruct((2, rows, atoms), BF), jax.ShapeDtypeStruct((1, rows), F32)],
        compiler_params=params(12),
        cost_estimate=pl.CostEstimate(flops=rows * atoms * 40, transcendentals=0, bytes_accessed=rows * atoms * 4),
        name="table",
    )(place, n, f)


def structure_kernel(inv_root, c_ref, t_ref, out_ref):
    high, low = halves(c_ref[...])
    both = jnp.concatenate([high, low], axis=0)
    s = dot(t_ref[...], both, ((1,), (1,)))
    nq = c_ref.shape[0]
    out_ref[...] = (s[:, :nq] + s[:, nq:]).T * inv_root


def structure_call(c, table, inv_root):
    rows, atoms = table.shape
    step = rows
    nq = c.shape[0]
    return pl.pallas_call(
        functools.partial(structure_kernel, inv_root),
        grid=(rows // step,),
        in_specs=[pl.BlockSpec((nq, atoms), lambda i: (0, 0)), pl.BlockSpec((step, atoms), lambda i: (i, 0))],
        out_specs=pl.BlockSpec((nq, step), lambda i: (0, i)),
        out_shape=jax.ShapeDtypeStruct((nq, rows), F32),
        compiler_params=params(12),
        cost_estimate=pl.CostEstimate(flops=rows * atoms * 512, transcendentals=0, bytes_accessed=rows * atoms * 2),
        name="structure",
    )(c, table)


def field_kernel(planes, step, place, s_ref, weight_ref, c_ref, t_ref, out_ref):
    nq = c_ref.shape[0]
    waves = weight_ref.shape[1]
    n = grid_points(place[1] * planes, planes)
    real = s_ref[:, :waves] * weight_ref[...]
    imag = s_ref[:, waves:] * weight_ref[...]
    with_cos = jnp.concatenate([real] + [-imag * n[d] for d in range(3)], axis=0)
    with_sin = jnp.concatenate([imag] + [real * n[d] for d in range(3)], axis=0)
    with_cos, with_sin = [jnp.concatenate(halves(x), axis=0) for x in (with_cos, with_sin)]
    for start in range(0, c_ref.shape[1], step):
        cols = slice(start, start + step)
        both = dot(with_cos, t_ref[0, :, cols], ((1,), (0,))) + dot(with_sin, t_ref[1, :, cols], ((1,), (0,)))
        sums = both[: 4 * nq] + both[4 * nq :]
        c = c_ref[:, cols]
        out_ref[0:nq, cols] = sums[:nq]
        forces = [
            jnp.sum(c * sums[(d + 1) * nq : (d + 2) * nq], axis=0, keepdims=True) for d in range(3)
        ]
        out_ref[nq : nq + 8, cols] = jnp.concatenate(forces + [jnp.zeros((5, step), F32)], axis=0)


def field_call(place, s, weight, c, table, planes):
    _, rows, atoms = table.shape
    nq = c.shape[0]
    whole = lambda shape: pl.BlockSpec(shape, lambda g, *_: (0,) * len(shape), pipeline_mode=pl.Buffered(1))
    return pl.pallas_call(
        functools.partial(field_kernel, planes, 512),
        grid_spec=pltpu.PrefetchScalarGridSpec(
            num_scalar_prefetch=1,
            grid=(1,),
            in_specs=[whole(x.shape) for x in (s, weight, c, table)],
            out_specs=whole((nq + 8, atoms)),
        ),
        out_shape=jax.ShapeDtypeStruct((nq + 8, atoms), F32),
        compiler_params=params(12),
        cost_estimate=pl.CostEstimate(flops=rows * atoms * 512, transcendentals=0, bytes_accessed=rows * atoms * 2),
        name="fields",
    )(place, s, weight, c, table)


def finish_kernel(mine_ref, theirs_ref, potential_ref, force_ref):
    nq = potential_ref.shape[0]
    total = mine_ref[...].astype(F32) + theirs_ref[...].astype(F32)
    potential_ref[...] = total[:nq]
    force_ref[...] = total[nq : nq + 3]


def finish_call(mine, theirs, nq):
    atoms = mine.shape[1]
    return pl.pallas_call(
        finish_kernel,
        out_shape=[jax.ShapeDtypeStruct((nq, atoms), F32), jax.ShapeDtypeStruct((3, atoms), F32)],
        compiler_params=pltpu.CompilerParams(vmem_limit_bytes=4 << 20),
        name="finish",
    )(mine, theirs)


def exchanged(x, axis, step):
    size = lax.axis_size(axis)
    if step >= size:
        return x
    return x + lax.ppermute(x, axis, [(i, i ^ step) for i in range(size)])


def summed(x, axis, step=1, stop=None):
    size = lax.axis_size(axis)
    assert size & (size - 1) == 0
    while step < (stop or size):
        x = exchanged(x, axis, step)
        step *= 2
    return x


def whole_step(
    queries,
    key_states,
    value_states,
    fractional,
    block_counts,
    neighbors,
    integer_wave_vectors,
    charge_weight,
):
    heads, head_dim, atoms = queries.shape
    nq = charge_weight.shape[1]
    planes = (KMAX + 1) // lax.axis_size("inner")
    assert planes * lax.axis_size("inner") == KMAX + 1
    inv_root = 1.0 / math.sqrt(atoms * lax.axis_size("seq"))
    place = jnp.stack([lax.axis_index("seq"), lax.axis_index("inner")]).astype(jnp.int32)
    width = REACH * BS
    count = lax.axis_size("seq")
    near_pairs = [(i, i ^ 1) for i in range(count)]
    far_pairs = [(i, i + 1 if i % 2 else i - 1) for i in range(1, count - 1)]

    def swap(x, pairs):
        return lax.ppermute(x, "seq", pairs)

    values = value_states.transpose(1, 0, 2)
    keys = key_states.reshape(heads * head_dim, atoms)
    asked = queries.reshape(heads * head_dim, atoms)
    near, far, far_big, v0, keys, asked, weight, counts, lists = load_call(
        place, keys, values, (asked, charge_weight.T, block_counts, neighbors.T), width
    )
    vectors = integer_wave_vectors
    far = swap(far, far_pairs)
    near = swap(near, near_pairs)
    far_big = swap(far_big, far_pairs)

    p_in, scale_in, part, near_big = scores_call(
        "interior", lists, counts, place, asked, keys, v0, weight, (values,), heads, head_dim
    )
    near_big = swap(near_big, near_pairs)
    p_out, scale_out, part = scores_call(
        "edges", lists, counts, place, asked, keys, v0, weight, (far, near, part), heads, head_dim
    )
    table, wave_weight = table_call(place, vectors, fractional, planes)
    last = lax.axis_size("inner") // 2

    def halfway(x):
        x = summed(x, "inner", stop=last).astype(BF)
        return x, lax.ppermute(x, "inner", [(i, i ^ last) for i in range(2 * last)])

    mine, theirs = halfway(part)
    charges = mine.astype(F32) + theirs.astype(F32)
    structure = structure_call(charges, table.reshape(-1, atoms), inv_root)
    structure = summed(structure, "seq")
    fields = field_call(place, structure, wave_weight, charges, table, planes)
    fields, others = halfway(fields)
    potential, forces = finish_call(fields, others, nq)

    mix = functools.partial(mix_call, heads=heads, head_dim=head_dim)
    attention = mix("low", lists, place, values, p_in, scale_in, (), None)
    attention = mix("far", lists, place, values, p_out, scale_out, (far, far_big), attention)
    attention = mix("high", lists, place, values, p_in, scale_in, (), attention)
    sums = own_call(lists, place, values, p_out, heads)
    attention = near_call(
        lists, place, values.shape, sums, p_out, scale_out, (near, near_big), attention, heads, head_dim
    )
    return (attention.transpose(1, 0, 2), potential, forces)


def solution(mesh):
    placed = (
        P("inner", None, "seq"),
        P("inner", None, "seq"),
        P("inner", None, "seq"),
        P(None, "seq"),
        P(),
        P("seq", None),
        P(),
        P("inner", None),
    )
    return jax.shard_map(
        whole_step,
        mesh=mesh,
        in_specs=placed,
        out_specs=(P("inner", None, "seq"), P(None, "seq"), P(None, "seq")),
        check_vma=False,
    )
```

```python
import functools
import math

import jax
import jax.numpy as jnp
from jax import lax
from jax.experimental import pallas as pl
from jax.experimental.pallas import tpu as pltpu
from jax.sharding import PartitionSpec as P


BS = 256
NNB = 3
REACH = 2
KMAX = 7
LOG2E = 1.4426950408889634

ewald_scale = 40.0
ewald_damp = 0.02

BF = jnp.bfloat16
F32 = jnp.float32

SIN = (6.283185302511499, -41.34170040531678, 81.60513138577247, -76.70301535353673,
       42.02592698394968, -14.899846662448152, 3.2381375038938693)
COS = (0.9999999890590217, -19.73920449945376, 64.93911745989128, -85.45013953083522,
       60.167630950695504, -25.967599247822193, 6.5286581606558824)


def params(mib):
    return pltpu.CompilerParams(vmem_limit_bytes=mib << 20, dimension_semantics=("arbitrary",))


def dot(a, b, dims):
    return lax.dot_general(a, b, (dims, ((), ())), preferred_element_type=F32)


def horner(coeffs, u):
    total = coeffs[-1]
    for c in coeffs[-2::-1]:
        total = total * u + c
    return total


def halves(x):
    high = x.astype(BF)
    return high, (x - high.astype(F32)).astype(BF)


def thirds(x):
    high, low = halves(x)
    return high, low, ((x - high.astype(F32)) - low.astype(F32)).astype(BF)


def columns_of(place, width, atoms, far):
    first = on_left(place, far)
    return pl.ds(pl.multiple_of(jnp.where(first, 0, atoms - width), 128), width)


def run(moves, sems):
    started = [pltpu.make_async_copy(src, dst, sems.at[i]) for i, (src, dst) in enumerate(moves)]
    for copy in started:
        copy.start()
    for copy in started:
        copy.wait()


def load_kernel(place, k, v, *refs):
    others, (near, far, far_big, v0, *copies), sems = refs[: (len(refs) - 6) // 2], refs[(len(refs) - 6) // 2 : -1], refs[-1]
    rows, atoms = k.shape
    chans, width = v.shape[1], near.shape[1]
    moves = []
    for piece, is_far in ((far, True), (near, False)):
        cols = columns_of(place, width, atoms, is_far)
        moves.append((k.at[:, cols], piece.at[pl.ds(0, rows)]))
        moves.append((v.at[0, :, cols], piece.at[pl.ds(rows, chans)]))
    moves += list(zip((k, *others), copies)) + [(v.at[0], v0)]
    moves.append((v.at[pl.ds(1, far_big.shape[0]), :, columns_of(place, width, atoms, True)], far_big))
    run(moves, sems)


def load_call(place, k, v, others, width):
    comps, chans, atoms = v.shape
    shape = jax.ShapeDtypeStruct
    outs = [shape((k.shape[0] + chans, width), BF)] * 2 + [shape((comps - 1, chans, width), BF)]
    outs += [shape((chans, atoms), BF)] + [shape(x.shape, x.dtype) for x in (k, *others)]
    operands = (k, v, *others)
    return pl.pallas_call(
        load_kernel,
        grid_spec=pltpu.PrefetchScalarGridSpec(
            num_scalar_prefetch=1,
            grid=(1,),
            in_specs=[pl.BlockSpec(memory_space=pltpu.HBM)] * len(operands),
            out_specs=[pl.BlockSpec(memory_space=pl.ANY)] * len(outs),
            scratch_shapes=[pltpu.SemaphoreType.DMA((7 + len(others),))],
        ),
        out_shape=outs,
        compiler_params=params(2),
        cost_estimate=pl.CostEstimate(flops=0, transcendentals=0, bytes_accessed=1 << 20),
        name="load",
    )(place, *[pltpu.with_memory_space_constraint(x, pltpu.HBM) for x in operands])


def on_left(place, far):
    even = place[0] % 2 == 0
    return even if far else jnp.logical_not(even)


def edge_block(step, place, blocks):
    left = (step < REACH) == (place[0] % 2 == 0)
    return step % REACH + jnp.where(left, 0, blocks - REACH)


def score_kernel(heads, head_dim, head_chan, blocks, part, lists, counts, place, *refs):
    q_ref, k_ref, v_ref, cw_ref = refs[:4]
    if part == "interior":
        sides = ()
        values, p_ref, scale_ref, charge_ref, near_big, kaug, v0, sems = refs[4:]
        atoms, width = values.shape[2], near_big.shape[2]
        cut = values.at[pl.ds(1, near_big.shape[0]), :, columns_of(place, width, atoms, False)]
        cutting = pltpu.make_async_copy(cut, near_big, sems.at[0])
        cutting.start()
    else:
        sides, (p_ref, scale_ref, charge_ref, kaug, v0) = refs[4:7], refs[7:]
    first = place[0] * blocks
    total = counts.shape[0]
    lane = lax.broadcasted_iota(jnp.int32, (16, BS), 1)
    row = lax.broadcasted_iota(jnp.int32, (16, BS), 0)
    top_row = jnp.where(row == 0, 1.0, 0.0).astype(BF)

    def fill(b, keys, values):
        index = first + b - REACH
        inside = (index >= 0) & (index < total)
        live = jnp.where(inside, counts[jnp.clip(index, 0, total - 1)], 0)
        bias = jnp.where((row == 0) & (lane >= live), -1e30, 0.0).astype(BF)
        for h in range(heads):
            for copy in range(3):
                kaug[b, h, copy * head_dim : (copy + 1) * head_dim, :] = keys[h * head_dim : (h + 1) * head_dim]
            kaug[b, h, 3 * head_dim : 3 * head_dim + 16, :] = bias
            v0[b, h, 0:head_chan] = values[h * head_chan : (h + 1) * head_chan]
            v0[b, h, head_chan : head_chan + 16] = top_row

    for b in range(blocks):
        cols = slice(b * BS, (b + 1) * BS)
        fill(b + REACH, k_ref[:, cols], v_ref[:, cols])
    if sides:
        for far, side in zip((True, False), sides[:2]):
            base = jnp.where(on_left(place, far), 0, blocks + REACH)
            for b in range(REACH):
                cols = slice(b * BS, (b + 1) * BS)
                fill(base + b, side[0 : heads * head_dim, cols], side[heads * head_dim :, cols])
        inner = slice(REACH * BS, (blocks - REACH) * BS)
        charge_ref[:, inner] = sides[2][:, inner]
    else:
        charge_ref[...] = jnp.zeros_like(charge_ref)

    def block_of(i):
        return i + REACH if part == "interior" else edge_block(i, place, blocks)

    def columns(g):
        return pl.ds(pl.multiple_of(g * BS, BS), BS)

    def scores_of(i, h):
        g = block_of(i)
        listed = [lists[e, g] - (first - REACH) for e in range(NNB)]
        q = q_ref[h * head_dim : (h + 1) * head_dim, columns(g)].astype(F32) * (head_dim ** (-0.5) * LOG2E)
        qa = jnp.concatenate([*thirds(q), top_row], axis=0)
        return listed, [dot(kaug[b, h], qa, ((0,), (0,))) for b in listed]

    steps = p_ref.shape[0]
    pairs = [(i, h) for i in range(steps) for h in range(heads)]
    coming = scores_of(*pairs[0])
    charge = None
    for at, (i, h) in enumerate(pairs):
        listed, scores = coming
        if at + 1 < len(pairs):
            coming = scores_of(*pairs[at + 1])
        g = block_of(i)
        top = functools.reduce(jnp.maximum, [jnp.max(s, axis=0, keepdims=True) for s in scores])
        mixed = 0.0
        for e, b in enumerate(listed):
            w16 = jnp.exp2(scores[e] - top).astype(BF)
            p_ref[i, h, e * BS : (e + 1) * BS, :] = w16
            mixed = mixed + dot(v0[b, h], w16, ((1,), (0,)))
        live_q = lane[0:1] < counts[first + g]
        scale = jnp.where(live_q, 1.0 / mixed[head_chan : head_chan + 1], 0.0)
        scale_ref[i, h : h + 1, :] = scale
        att0 = (mixed[:head_chan] * scale).astype(BF)
        term = dot(cw_ref[:, h * head_chan : (h + 1) * head_chan], att0, ((1,), (0,)))
        charge = term if h == 0 else charge + term
        if h == heads - 1:
            charge_ref[:, columns(g)] = charge
    if part == "interior":
        cutting.wait()


def scores_call(part, lists, counts, place, q, k, v0, cw, sides, heads, head_dim):
    chans, atoms = v0.shape
    blocks = atoms // BS
    nq = cw.shape[0]
    head_chan = chans // heads
    band = blocks + 2 * REACH
    steps = blocks - 2 * REACH if part == "interior" else 2 * REACH
    whole = lambda shape: pl.BlockSpec(shape, lambda g, *_: (0,) * len(shape), pipeline_mode=pl.Buffered(1))
    shapes = [((steps, heads, NNB * BS, BS), BF), ((steps, heads, BS), F32), ((nq, atoms), F32)]
    interior = part == "interior"
    cuts = [((sides[0].shape[0] - 1, chans, REACH * BS), BF)] if interior else []
    if interior:
        sides = [pltpu.with_memory_space_constraint(x, pltpu.HBM) for x in sides]
    return pl.pallas_call(
        functools.partial(score_kernel, heads, head_dim, head_chan, blocks, part),
        grid_spec=pltpu.PrefetchScalarGridSpec(
            num_scalar_prefetch=3,
            grid=(1,),
            in_specs=[whole(x.shape) for x in (q, k, v0, cw)]
            + [pl.BlockSpec(memory_space=pltpu.HBM) if interior else whole(x.shape) for x in sides],
            out_specs=[whole(shape) for shape, _ in shapes] + [pl.BlockSpec(memory_space=pl.ANY)] * len(cuts),
            scratch_shapes=[
                pltpu.VMEM((band, heads, 3 * head_dim + 16, BS), BF),
                pltpu.VMEM((band, heads, head_chan + 16, BS), BF),
            ]
            + [pltpu.SemaphoreType.DMA((1,))] * len(cuts),
        ),
        out_shape=[jax.ShapeDtypeStruct(*x) for x in shapes + cuts],
        compiler_params=params(16),
        cost_estimate=pl.CostEstimate(
            flops=steps * heads * NNB * BS * BS * 200, transcendentals=steps * heads * NNB * BS * BS,
            bytes_accessed=steps * heads * NNB * BS * BS * 2,
        ),
    )(lists, counts, place, q, k, v0, cw, *sides)


def mix_kernel(heads, head_dim, head_chan, blocks, part, skip, lists, place, v_ref, p_ref, scale_ref, *refs):
    halo, out_ref = refs[: 2 if part in ("far", "near") else 0], refs[-2 if part in ("far", "near") else -1]
    comps = v_ref.shape[0]
    i = pl.program_id(0)
    offset = place[0] * blocks
    if halo:
        small, big = halo
        band = refs[-1]
        span = 3 * REACH
        left = on_left(place, part == "far")
        begin = jnp.where(left, 0, blocks + 2 * REACH - span)

        @pl.when(i == 0)
        def _():
            own = jnp.where(left, REACH, 0)
            first = jnp.where(left, 0, blocks - 2 * REACH)
            for b in range(2 * REACH):
                band[own + b] = v_ref[:, :, pl.ds(pl.multiple_of((first + b) * BS, BS), BS)]
            other = jnp.where(left, 0, 2 * REACH)
            for b in range(REACH):
                cols = slice(b * BS, (b + 1) * BS)
                band[other + b, 0] = small[heads * head_dim :, cols]
                band[other + b, 1:] = big[:, :, cols]

        g = edge_block(i if part == "far" else i + REACH, place, blocks)
        listed = [lists[e, g] - offset + REACH - begin for e in range(NNB)]
        pick = lambda b, rows: band[b, :, rows, :]
    else:
        g = i + (REACH if part == "low" else blocks // 2)
        listed = [lists[e, g] - offset for e in range(NNB)]
        pick = lambda b, rows: v_ref[:, rows, pl.ds(pl.multiple_of(b * BS, BS), BS)]
    for h in range(heads):
        rows = slice(h * head_chan, (h + 1) * head_chan)
        acc = 0.0
        for e in range(NNB):
            v = pick(listed[e], rows).reshape(comps * head_chan, BS)
            acc = acc + dot(v, p_ref[i + skip, h, e * BS : (e + 1) * BS, :], ((1,), (0,)))
        acc = acc * scale_ref[i + skip, h : h + 1, :]
        out_ref[:, rows, :] = acc.astype(BF).reshape(comps, head_chan, BS)


def mix_call(part, lists, place, v, p, scale, halo, prev, heads, head_dim):
    comps, chans, atoms = v.shape
    blocks = atoms // BS
    half = blocks // 2 - REACH
    steps = REACH if halo else half
    skip = {"low": 0, "high": half, "far": 0, "near": REACH}[part]

    def at(i, lists, place):
        if part in ("low", "high"):
            return i + REACH + skip
        return edge_block(i + skip, place, blocks)

    whole = lambda shape: pl.BlockSpec(shape, lambda g, *_: (0,) * len(shape), pipeline_mode=pl.Buffered(1))
    extra = list(halo) + ([] if prev is None else [prev])
    return pl.pallas_call(
        functools.partial(mix_kernel, heads, head_dim, chans // heads, blocks, part, skip),
        grid_spec=pltpu.PrefetchScalarGridSpec(
            num_scalar_prefetch=2,
            grid=(steps,),
            in_specs=[
                whole(v.shape),
                whole(p.shape),
                whole(scale.shape),
            ]
            + [whole(x.shape) for x in halo]
            + ([] if prev is None else [pl.BlockSpec(memory_space=pl.ANY)]),
            out_specs=pl.BlockSpec((comps, chans, BS), lambda i, *s: (0, 0, at(i, *s))),
            scratch_shapes=[pltpu.VMEM((3 * REACH, comps, chans, BS), BF)] if halo else [],
        ),
        out_shape=jax.ShapeDtypeStruct(v.shape, BF),
        input_output_aliases={} if prev is None else {4 + len(extra): 0},
        compiler_params=params(16),
        cost_estimate=pl.CostEstimate(
            flops=steps * chans * comps * NNB * BS * BS * 2, transcendentals=0,
            bytes_accessed=steps * chans * comps * BS * 8,
        ),
    )(lists, place, v, p, scale, *extra)


def own_kernel(heads, head_chan, blocks, lists, place, v_ref, p_ref, sum_ref):
    comps = v_ref.shape[0]
    for i in range(REACH):
        g = edge_block(i + REACH, place, blocks)
        for h in range(heads):
            rows = slice(h * head_chan, (h + 1) * head_chan)
            acc = 0.0
            for e in range(NNB):
                b = lists[e, g] - place[0] * blocks
                own = jnp.where((b >= 0) & (b < blocks), 1.0, 0.0)
                cols = pl.ds(pl.multiple_of(jnp.clip(b, 0, blocks - 1) * BS, BS), BS)
                v = v_ref[:, rows, cols].reshape(comps * head_chan, BS)
                acc = acc + own * dot(v, p_ref[i + REACH, h, e * BS : (e + 1) * BS, :], ((1,), (0,)))
            sum_ref[i, h] = acc


def own_call(lists, place, v, p, heads):
    comps, chans, atoms = v.shape
    blocks = atoms // BS
    whole = lambda shape: pl.BlockSpec(shape, lambda g, *_: (0,) * len(shape), pipeline_mode=pl.Buffered(1))
    shape = (REACH, heads, comps * chans // heads, BS)
    return pl.pallas_call(
        functools.partial(own_kernel, heads, chans // heads, blocks),
        grid_spec=pltpu.PrefetchScalarGridSpec(
            num_scalar_prefetch=2,
            grid=(1,),
            in_specs=[whole(v.shape), whole(p.shape)],
            out_specs=whole(shape),
        ),
        out_shape=jax.ShapeDtypeStruct(shape, F32),
        compiler_params=params(16),
        cost_estimate=pl.CostEstimate(
            flops=REACH * chans * comps * NNB * BS * BS * 2, transcendentals=0,
            bytes_accessed=REACH * chans * comps * BS * 8,
        ),
        name="near_own",
    )(lists, place, v, p)


def near_kernel(heads, head_dim, head_chan, blocks, lists, place, sum_ref, p_ref, scale_ref, small, big, prev, out_ref, acc):
    i = pl.program_id(0)
    g = edge_block(i + REACH, place, blocks)
    comps = big.shape[0] + 1
    for h in range(heads):
        rows = slice(h * head_chan, (h + 1) * head_chan)
        first = heads * head_dim + h * head_chan
        acc[h] = sum_ref[i, h]
        for e in range(NNB):
            b = lists[e, g] - place[0] * blocks

            @pl.when((b < 0) | (b >= blocks))
            def _():
                at = jnp.clip(jnp.where(b < 0, b + REACH, b - blocks), 0, REACH - 1)
                cols = pl.ds(pl.multiple_of(at * BS, BS), BS)
                v = jnp.concatenate([small[first : first + head_chan, cols][None], big[:, rows, cols]], axis=0)
                v = v.reshape(comps * head_chan, BS)
                acc[h] += dot(v, p_ref[i + REACH, h, e * BS : (e + 1) * BS, :], ((1,), (0,)))

    for h in range(heads):
        rows = slice(h * head_chan, (h + 1) * head_chan)
        total = acc[h] * scale_ref[i + REACH, h : h + 1, :]
        out_ref[:, rows, :] = total.astype(BF).reshape(comps, head_chan, BS)


def near_call(lists, place, v_shape, sums, p, scale, halo, prev, heads, head_dim):
    comps, chans, atoms = v_shape
    blocks = atoms // BS
    whole = lambda shape: pl.BlockSpec(shape, lambda g, *_: (0,) * len(shape), pipeline_mode=pl.Buffered(1))
    return pl.pallas_call(
        functools.partial(near_kernel, heads, head_dim, chans // heads, blocks),
        grid_spec=pltpu.PrefetchScalarGridSpec(
            num_scalar_prefetch=2,
            grid=(REACH,),
            in_specs=[whole(x.shape) for x in (sums, p, scale, *halo)] + [pl.BlockSpec(memory_space=pl.ANY)],
            out_specs=pl.BlockSpec(
                (comps, chans, BS), lambda i, lists, place: (0, 0, edge_block(i + REACH, place, blocks))
            ),
            scratch_shapes=[pltpu.VMEM(sums.shape[1:], F32)],
        ),
        out_shape=jax.ShapeDtypeStruct(v_shape, BF),
        input_output_aliases={7: 0},
        compiler_params=params(16),
        cost_estimate=pl.CostEstimate(
            flops=REACH * chans * comps * NNB * BS * BS, transcendentals=0,
            bytes_accessed=REACH * chans * comps * BS * 8,
        ),
        name="mix_near",
    )(lists, place, sums, p, scale, *halo, prev)


SPREAD = 2 * KMAX + 1
WIDE = 16


def wave(turns):
    r = turns - jnp.round(turns)
    u = r * r
    return horner(COS, u), horner(SIN, u) * r


def grid_points(base, planes):
    rows = planes * SPREAD * WIDE
    place = lax.broadcasted_iota(jnp.int32, (1, rows), 1).astype(F32)
    pair = jnp.floor((place + 0.5) * (1.0 / WIDE))
    n3 = place - pair * WIDE - KMAX
    plane = jnp.floor((pair + 0.5) * (1.0 / SPREAD))
    return plane + base.astype(F32), pair - plane * SPREAD - KMAX, n3


def grid_weights(n, base, planes):
    pairs = planes * SPREAD
    high = -(-pairs // 16) * 16
    flip = jnp.where(n[0:1] < 0, -1, 1)
    pair = (n[0:1] * flip - base) * SPREAD + n[1:2] * flip + KMAX
    mine = (n[0:1] * flip >= base) & (n[0:1] * flip < base + planes)
    third = n[2:3] * flip + KMAX
    count = n.shape[1]
    is_pair = (lax.broadcasted_iota(jnp.int32, (high, count), 0) == pair) & mine
    is_third = lax.broadcasted_iota(jnp.int32, (WIDE, count), 0) == third
    one_hot = lambda x: jnp.where(x, 1.0, 0.0).astype(BF)
    found = dot(one_hot(is_pair), one_hot(is_third), ((1,), (1,)))
    rows = pairs * WIDE
    row = lax.broadcasted_iota(jnp.int32, (WIDE, rows), 0)
    spread = one_hot((lax.broadcasted_iota(jnp.int32, (WIDE, rows), 1) & (WIDE - 1)) == row)
    wide = sum(dot(part, spread, ((1,), (0,))) for part in thirds(found))
    own = lax.broadcasted_iota(jnp.int32, (high, rows), 1) >> (WIDE.bit_length() - 1)
    times = jnp.sum(jnp.where(own == lax.broadcasted_iota(jnp.int32, (high, rows), 0), wide, 0.0), axis=0, keepdims=True)
    n1, n2, n3 = grid_points(base, planes)
    norm = n1 * n1 + n2 * n2 + n3 * n3
    safe = jnp.maximum(norm, 1.0)
    return jnp.where(norm > 0, times * (ewald_scale * jnp.exp(-ewald_damp * safe) / safe), 0.0)


def table_kernel(planes, step, place, n_ref, f_ref, out_ref, weight_ref, pairs):
    base = place[1] * planes
    weight_ref[...] = grid_weights(n_ref[...], base, planes)
    steps = (lax.broadcasted_iota(jnp.int32, (WIDE, step), 0) - KMAX).astype(F32)
    for start in range(0, f_ref.shape[1], step):
        cols = slice(start, start + step)
        second = wave(steps * f_ref[1:2, cols])
        third = wave(steps * f_ref[2:3, cols])
        for plane in range(planes):
            first = wave((base + plane).astype(F32) * f_ref[0:1, cols])
            pairs[0, plane] = first[0] * second[0] - first[1] * second[1]
            pairs[1, plane] = first[1] * second[0] + first[0] * second[1]
            for m in range(SPREAD):
                real, imag = pairs[0, plane, m : m + 1, :], pairs[1, plane, m : m + 1, :]
                at = slice((plane * SPREAD + m) * WIDE, (plane * SPREAD + m + 1) * WIDE)
                out_ref[0, at, cols] = (real * third[0] - imag * third[1]).astype(BF)
                out_ref[1, at, cols] = (imag * third[0] + real * third[1]).astype(BF)


def table_call(place, n, f, planes):
    rows = planes * SPREAD * WIDE
    atoms = f.shape[1]
    step = 256
    whole = lambda shape: pl.BlockSpec(shape, lambda g, *_: (0,) * len(shape), pipeline_mode=pl.Buffered(1))
    return pl.pallas_call(
        functools.partial(table_kernel, planes, step),
        grid_spec=pltpu.PrefetchScalarGridSpec(
            num_scalar_prefetch=1,
            grid=(1,),
            in_specs=[whole(n.shape), whole(f.shape)],
            out_specs=[whole((2, rows, atoms)), whole((1, rows))],
            scratch_shapes=[pltpu.VMEM((2, planes, WIDE, step), F32)],
        ),
        out_shape=[jax.ShapeDtypeStruct((2, rows, atoms), BF), jax.ShapeDtypeStruct((1, rows), F32)],
        compiler_params=params(12),
        cost_estimate=pl.CostEstimate(flops=rows * atoms * 40, transcendentals=0, bytes_accessed=rows * atoms * 4),
        name="table",
    )(place, n, f)


def structure_kernel(inv_root, c_ref, t_ref, out_ref):
    high, low = halves(c_ref[...])
    both = jnp.concatenate([high, low], axis=0)
    s = dot(t_ref[...], both, ((1,), (1,)))
    nq = c_ref.shape[0]
    out_ref[...] = (s[:, :nq] + s[:, nq:]).T * inv_root


def structure_call(c, table, inv_root):
    rows, atoms = table.shape
    step = rows
    nq = c.shape[0]
    return pl.pallas_call(
        functools.partial(structure_kernel, inv_root),
        grid=(rows // step,),
        in_specs=[pl.BlockSpec((nq, atoms), lambda i: (0, 0)), pl.BlockSpec((step, atoms), lambda i: (i, 0))],
        out_specs=pl.BlockSpec((nq, step), lambda i: (0, i)),
        out_shape=jax.ShapeDtypeStruct((nq, rows), F32),
        compiler_params=params(12),
        cost_estimate=pl.CostEstimate(flops=rows * atoms * 512, transcendentals=0, bytes_accessed=rows * atoms * 2),
        name="structure",
    )(c, table)


def field_kernel(planes, step, place, s_ref, weight_ref, c_ref, t_ref, out_ref):
    nq = c_ref.shape[0]
    waves = weight_ref.shape[1]
    n = grid_points(place[1] * planes, planes)
    real = s_ref[:, :waves] * weight_ref[...]
    imag = s_ref[:, waves:] * weight_ref[...]
    with_cos = jnp.concatenate([real] + [-imag * n[d] for d in range(3)], axis=0)
    with_sin = jnp.concatenate([imag] + [real * n[d] for d in range(3)], axis=0)
    with_cos, with_sin = [jnp.concatenate(halves(x), axis=0) for x in (with_cos, with_sin)]
    for start in range(0, c_ref.shape[1], step):
        cols = slice(start, start + step)
        both = dot(with_cos, t_ref[0, :, cols], ((1,), (0,))) + dot(with_sin, t_ref[1, :, cols], ((1,), (0,)))
        sums = both[: 4 * nq] + both[4 * nq :]
        c = c_ref[:, cols]
        out_ref[0:nq, cols] = sums[:nq]
        forces = [
            jnp.sum(c * sums[(d + 1) * nq : (d + 2) * nq], axis=0, keepdims=True) for d in range(3)
        ]
        out_ref[nq : nq + 8, cols] = jnp.concatenate(forces + [jnp.zeros((5, step), F32)], axis=0)


def field_call(place, s, weight, c, table, planes):
    _, rows, atoms = table.shape
    nq = c.shape[0]
    whole = lambda shape: pl.BlockSpec(shape, lambda g, *_: (0,) * len(shape), pipeline_mode=pl.Buffered(1))
    return pl.pallas_call(
        functools.partial(field_kernel, planes, 512),
        grid_spec=pltpu.PrefetchScalarGridSpec(
            num_scalar_prefetch=1,
            grid=(1,),
            in_specs=[whole(x.shape) for x in (s, weight, c, table)],
            out_specs=whole((nq + 8, atoms)),
        ),
        out_shape=jax.ShapeDtypeStruct((nq + 8, atoms), F32),
        compiler_params=params(12),
        cost_estimate=pl.CostEstimate(flops=rows * atoms * 512, transcendentals=0, bytes_accessed=rows * atoms * 2),
        name="fields",
    )(place, s, weight, c, table)


def finish_kernel(mine_ref, theirs_ref, potential_ref, force_ref):
    nq = potential_ref.shape[0]
    total = mine_ref[...].astype(F32) + theirs_ref[...].astype(F32)
    potential_ref[...] = total[:nq]
    force_ref[...] = total[nq : nq + 3]


def finish_call(mine, theirs, nq):
    atoms = mine.shape[1]
    return pl.pallas_call(
        finish_kernel,
        out_shape=[jax.ShapeDtypeStruct((nq, atoms), F32), jax.ShapeDtypeStruct((3, atoms), F32)],
        compiler_params=pltpu.CompilerParams(vmem_limit_bytes=4 << 20),
        name="finish",
    )(mine, theirs)


def exchanged(x, axis, step):
    size = lax.axis_size(axis)
    if step >= size:
        return x
    return x + lax.ppermute(x, axis, [(i, i ^ step) for i in range(size)])


def summed(x, axis, step=1, stop=None):
    size = lax.axis_size(axis)
    assert size & (size - 1) == 0
    while step < (stop or size):
        x = exchanged(x, axis, step)
        step *= 2
    return x


def whole_step(
    queries,
    key_states,
    value_states,
    fractional,
    block_counts,
    neighbors,
    integer_wave_vectors,
    charge_weight,
):
    heads, head_dim, atoms = queries.shape
    nq = charge_weight.shape[1]
    planes = (KMAX + 1) // lax.axis_size("inner")
    assert planes * lax.axis_size("inner") == KMAX + 1
    inv_root = 1.0 / math.sqrt(atoms * lax.axis_size("seq"))
    place = jnp.stack([lax.axis_index("seq"), lax.axis_index("inner")]).astype(jnp.int32)
    width = REACH * BS
    count = lax.axis_size("seq")
    near_pairs = [(i, i ^ 1) for i in range(count)]
    far_pairs = [(i, i + 1 if i % 2 else i - 1) for i in range(1, count - 1)]

    def swap(x, pairs):
        return lax.ppermute(x, "seq", pairs)

    values = value_states.transpose(1, 0, 2)
    keys = key_states.reshape(heads * head_dim, atoms)
    asked = queries.reshape(heads * head_dim, atoms)
    near, far, far_big, v0, keys, asked, weight, counts, lists = load_call(
        place, keys, values, (asked, charge_weight.T, block_counts, neighbors.T), width
    )
    vectors = integer_wave_vectors
    far = swap(far, far_pairs)
    near = swap(near, near_pairs)
    far_big = swap(far_big, far_pairs)

    p_in, scale_in, part, near_big = scores_call(
        "interior", lists, counts, place, asked, keys, v0, weight, (values,), heads, head_dim
    )
    near_big = swap(near_big, near_pairs)
    p_out, scale_out, part = scores_call(
        "edges", lists, counts, place, asked, keys, v0, weight, (far, near, part), heads, head_dim
    )
    table, wave_weight = table_call(place, vectors, fractional, planes)
    last = lax.axis_size("inner") // 2

    def halfway(x):
        x = summed(x, "inner", stop=last)
        low = x.astype(BF)
        return x, low, lax.ppermute(low, "inner", [(i, i ^ last) for i in range(2 * last)])

    mine, _, theirs = halfway(part)
    charges = mine + theirs.astype(F32)
    structure = structure_call(charges, table.reshape(-1, atoms), inv_root)
    structure = structure + lax.ppermute(structure.astype(BF), "seq", near_pairs).astype(F32)
    structure = summed(structure, "seq", 2)
    fields = field_call(place, structure, wave_weight, charges, table, planes)
    _, fields, others = halfway(fields)
    potential, forces = finish_call(fields, others, nq)

    mix = functools.partial(mix_call, heads=heads, head_dim=head_dim)
    attention = mix("low", lists, place, values, p_in, scale_in, (), None)
    attention = mix("far", lists, place, values, p_out, scale_out, (far, far_big), attention)
    attention = mix("high", lists, place, values, p_in, scale_in, (), attention)
    sums = own_call(lists, place, values, p_out, heads)
    attention = near_call(
        lists, place, values.shape, sums, p_out, scale_out, (near, near_big), attention, heads, head_dim
    )
    return (attention.transpose(1, 0, 2), potential, forces)


def solution(mesh):
    placed = (
        P("inner", None, "seq"),
        P("inner", None, "seq"),
        P("inner", None, "seq"),
        P(None, "seq"),
        P(),
        P("seq", None),
        P(),
        P("inner", None),
    )
    return jax.shard_map(
        whole_step,
        mesh=mesh,
        in_specs=placed,
        out_specs=(P("inner", None, "seq"), P(None, "seq"), P(None, "seq")),
        check_vma=False,
    )
```

```python
import functools
import math

import jax
import jax.numpy as jnp
from jax import lax
from jax.experimental import pallas as pl
from jax.experimental.pallas import tpu as pltpu
from jax.sharding import PartitionSpec as P


BS = 256
NNB = 3
REACH = 2
KMAX = 7
LOG2E = 1.4426950408889634

ewald_scale = 40.0
ewald_damp = 0.02

BF = jnp.bfloat16
F32 = jnp.float32

SIN = (6.283185302511499, -41.34170040531678, 81.60513138577247, -76.70301535353673,
       42.02592698394968, -14.899846662448152, 3.2381375038938693)
COS = (0.9999999890590217, -19.73920449945376, 64.93911745989128, -85.45013953083522,
       60.167630950695504, -25.967599247822193, 6.5286581606558824)


def params(mib):
    return pltpu.CompilerParams(vmem_limit_bytes=mib << 20, dimension_semantics=("arbitrary",))


def dot(a, b, dims):
    return lax.dot_general(a, b, (dims, ((), ())), preferred_element_type=F32)


def horner(coeffs, u):
    total = coeffs[-1]
    for c in coeffs[-2::-1]:
        total = total * u + c
    return total


def halves(x):
    high = x.astype(BF)
    return high, (x - high.astype(F32)).astype(BF)


def thirds(x):
    high, low = halves(x)
    return high, low, ((x - high.astype(F32)) - low.astype(F32)).astype(BF)


def columns_of(place, width, atoms, far):
    first = on_left(place, far)
    return pl.ds(pl.multiple_of(jnp.where(first, 0, atoms - width), 128), width)


def run(moves, sems):
    started = [pltpu.make_async_copy(src, dst, sems.at[i]) for i, (src, dst) in enumerate(moves)]
    for copy in started:
        copy.start()
    for copy in started:
        copy.wait()


def load_kernel(place, k, v, *refs):
    others, (near, far, far_big, v0, *copies), sems = refs[: (len(refs) - 6) // 2], refs[(len(refs) - 6) // 2 : -1], refs[-1]
    rows, atoms = k.shape
    chans, width = v.shape[1], near.shape[1]
    moves = []
    for piece, is_far in ((far, True), (near, False)):
        cols = columns_of(place, width, atoms, is_far)
        moves.append((k.at[:, cols], piece.at[pl.ds(0, rows)]))
        moves.append((v.at[0, :, cols], piece.at[pl.ds(rows, chans)]))
    moves += list(zip((k, *others), copies)) + [(v.at[0], v0)]
    moves.insert(0, (v.at[pl.ds(1, far_big.shape[0]), :, columns_of(place, width, atoms, True)], far_big))
    run(moves, sems)


def load_call(place, k, v, others, width):
    comps, chans, atoms = v.shape
    shape = jax.ShapeDtypeStruct
    outs = [shape((k.shape[0] + chans, width), BF)] * 2 + [shape((comps - 1, chans, width), BF)]
    outs += [shape((chans, atoms), BF)] + [shape(x.shape, x.dtype) for x in (k, *others)]
    operands = (k, v, *others)
    return pl.pallas_call(
        load_kernel,
        grid_spec=pltpu.PrefetchScalarGridSpec(
            num_scalar_prefetch=1,
            grid=(1,),
            in_specs=[pl.BlockSpec(memory_space=pltpu.HBM)] * len(operands),
            out_specs=[pl.BlockSpec(memory_space=pl.ANY)] * len(outs),
            scratch_shapes=[pltpu.SemaphoreType.DMA((7 + len(others),))],
        ),
        out_shape=outs,
        compiler_params=params(2),
        cost_estimate=pl.CostEstimate(flops=0, transcendentals=0, bytes_accessed=1 << 20),
        name="load",
    )(place, *[pltpu.with_memory_space_constraint(x, pltpu.HBM) for x in operands])


def cut_kernel(place, v, piece, sem):
    cols = columns_of(place, piece.shape[2], v.shape[2], False)
    copy = pltpu.make_async_copy(v.at[pl.ds(1, piece.shape[0]), :, cols], piece, sem)
    copy.start()
    copy.wait()


def cut_call(place, v, width):
    comps, chans, _ = v.shape
    return pl.pallas_call(
        cut_kernel,
        grid_spec=pltpu.PrefetchScalarGridSpec(
            num_scalar_prefetch=1,
            grid=(1,),
            in_specs=[pl.BlockSpec(memory_space=pltpu.HBM)],
            out_specs=pl.BlockSpec(memory_space=pl.ANY),
            scratch_shapes=[pltpu.SemaphoreType.DMA],
        ),
        out_shape=jax.ShapeDtypeStruct((comps - 1, chans, width), BF),
        compiler_params=params(2),
        cost_estimate=pl.CostEstimate(flops=0, transcendentals=0, bytes_accessed=1 << 20),
        name="cut",
    )(place, pltpu.with_memory_space_constraint(v, pltpu.HBM))


def on_left(place, far):
    even = place[0] % 2 == 0
    return even if far else jnp.logical_not(even)


def edge_block(step, place, blocks):
    left = (step < REACH) == (place[0] % 2 == 0)
    return step % REACH + jnp.where(left, 0, blocks - REACH)


def score_kernel(heads, head_dim, head_chan, blocks, part, lists, counts, place, *refs):
    q_ref, k_ref, v_ref, cw_ref = refs[:4]
    sides, (p_ref, scale_ref, charge_ref, kaug, v0) = refs[4:-5], refs[-5:]
    first = place[0] * blocks
    total = counts.shape[0]
    lane = lax.broadcasted_iota(jnp.int32, (16, BS), 1)
    row = lax.broadcasted_iota(jnp.int32, (16, BS), 0)
    top_row = jnp.where(row == 0, 1.0, 0.0).astype(BF)

    def fill(b, keys, values):
        index = first + b - REACH
        inside = (index >= 0) & (index < total)
        live = jnp.where(inside, counts[jnp.clip(index, 0, total - 1)], 0)
        bias = jnp.where((row == 0) & (lane >= live), -1e30, 0.0).astype(BF)
        for h in range(heads):
            for copy in range(3):
                kaug[b, h, copy * head_dim : (copy + 1) * head_dim, :] = keys[h * head_dim : (h + 1) * head_dim]
            kaug[b, h, 3 * head_dim : 3 * head_dim + 16, :] = bias
            v0[b, h, 0:head_chan] = values[h * head_chan : (h + 1) * head_chan]
            v0[b, h, head_chan : head_chan + 16] = top_row

    for b in range(blocks):
        cols = slice(b * BS, (b + 1) * BS)
        fill(b + REACH, k_ref[:, cols], v_ref[:, cols])
    if sides:
        for far, side in zip((True, False), sides[:2]):
            base = jnp.where(on_left(place, far), 0, blocks + REACH)
            for b in range(REACH):
                cols = slice(b * BS, (b + 1) * BS)
                fill(base + b, side[0 : heads * head_dim, cols], side[heads * head_dim :, cols])
        inner = slice(REACH * BS, (blocks - REACH) * BS)
        charge_ref[:, inner] = sides[2][:, inner]
    else:
        charge_ref[...] = jnp.zeros_like(charge_ref)

    def block_of(i):
        return i + REACH if part == "interior" else edge_block(i, place, blocks)

    def columns(g):
        return pl.ds(pl.multiple_of(g * BS, BS), BS)

    def scores_of(i, h):
        g = block_of(i)
        listed = [lists[e, g] - (first - REACH) for e in range(NNB)]
        q = q_ref[h * head_dim : (h + 1) * head_dim, columns(g)].astype(F32) * (head_dim ** (-0.5) * LOG2E)
        qa = jnp.concatenate([*thirds(q), top_row], axis=0)
        return listed, [dot(kaug[b, h], qa, ((0,), (0,))) for b in listed]

    steps = p_ref.shape[0]
    pairs = [(i, h) for i in range(steps) for h in range(heads)]
    coming = scores_of(*pairs[0])
    charge = None
    for at, (i, h) in enumerate(pairs):
        listed, scores = coming
        if at + 1 < len(pairs):
            coming = scores_of(*pairs[at + 1])
        g = block_of(i)
        top = functools.reduce(jnp.maximum, [jnp.max(s, axis=0, keepdims=True) for s in scores])
        mixed = 0.0
        for e, b in enumerate(listed):
            w16 = jnp.exp2(scores[e] - top).astype(BF)
            p_ref[i, h, e * BS : (e + 1) * BS, :] = w16
            mixed = mixed + dot(v0[b, h], w16, ((1,), (0,)))
        live_q = lane[0:1] < counts[first + g]
        scale = jnp.where(live_q, 1.0 / mixed[head_chan : head_chan + 1], 0.0)
        scale_ref[i, h : h + 1, :] = scale
        att0 = (mixed[:head_chan] * scale).astype(BF)
        term = dot(cw_ref[:, h * head_chan : (h + 1) * head_chan], att0, ((1,), (0,)))
        charge = term if h == 0 else charge + term
        if h == heads - 1:
            charge_ref[:, columns(g)] = charge


def scores_call(part, lists, counts, place, q, k, v0, cw, sides, heads, head_dim):
    chans, atoms = v0.shape
    blocks = atoms // BS
    nq = cw.shape[0]
    head_chan = chans // heads
    band = blocks + 2 * REACH
    steps = blocks - 2 * REACH if part == "interior" else 2 * REACH
    whole = lambda shape: pl.BlockSpec(shape, lambda g, *_: (0,) * len(shape), pipeline_mode=pl.Buffered(1))
    shapes = [((steps, heads, NNB * BS, BS), BF), ((steps, heads, BS), F32), ((nq, atoms), F32)]
    return pl.pallas_call(
        functools.partial(score_kernel, heads, head_dim, head_chan, blocks, part),
        grid_spec=pltpu.PrefetchScalarGridSpec(
            num_scalar_prefetch=3,
            grid=(1,),
            in_specs=[whole(x.shape) for x in (q, k, v0, cw, *sides)],
            out_specs=[whole(shape) for shape, _ in shapes],
            scratch_shapes=[
                pltpu.VMEM((band, heads, 3 * head_dim + 16, BS), BF),
                pltpu.VMEM((band, heads, head_chan + 16, BS), BF),
            ],
        ),
        out_shape=[jax.ShapeDtypeStruct(*x) for x in shapes],
        compiler_params=params(16),
        cost_estimate=pl.CostEstimate(
            flops=steps * heads * NNB * BS * BS * 200, transcendentals=steps * heads * NNB * BS * BS,
            bytes_accessed=steps * heads * NNB * BS * BS * 2,
        ),
    )(lists, counts, place, q, k, v0, cw, *sides)


def mix_kernel(heads, head_dim, head_chan, blocks, part, skip, lists, place, v_ref, p_ref, scale_ref, *refs):
    halo, out_ref = refs[: 2 if part in ("far", "near") else 0], refs[-2 if part in ("far", "near") else -1]
    comps = v_ref.shape[0]
    i = pl.program_id(0)
    offset = place[0] * blocks
    if halo:
        small, big = halo
        band = refs[-1]
        span = 3 * REACH
        left = on_left(place, part == "far")
        begin = jnp.where(left, 0, blocks + 2 * REACH - span)

        @pl.when(i == 0)
        def _():
            own = jnp.where(left, REACH, 0)
            first = jnp.where(left, 0, blocks - 2 * REACH)
            for b in range(2 * REACH):
                band[own + b] = v_ref[:, :, pl.ds(pl.multiple_of((first + b) * BS, BS), BS)]
            other = jnp.where(left, 0, 2 * REACH)
            for b in range(REACH):
                cols = slice(b * BS, (b + 1) * BS)
                band[other + b, 0] = small[heads * head_dim :, cols]
                band[other + b, 1:] = big[:, :, cols]

        g = edge_block(i if part == "far" else i + REACH, place, blocks)
        listed = [lists[e, g] - offset + REACH - begin for e in range(NNB)]
        pick = lambda b, rows: band[b, :, rows, :]
    else:
        g = i + (REACH if part == "low" else blocks // 2)
        listed = [lists[e, g] - offset for e in range(NNB)]
        pick = lambda b, rows: v_ref[:, rows, pl.ds(pl.multiple_of(b * BS, BS), BS)]
    for h in range(heads):
        rows = slice(h * head_chan, (h + 1) * head_chan)
        acc = 0.0
        for e in range(NNB):
            v = pick(listed[e], rows).reshape(comps * head_chan, BS)
            acc = acc + dot(v, p_ref[i + skip, h, e * BS : (e + 1) * BS, :], ((1,), (0,)))
        acc = acc * scale_ref[i + skip, h : h + 1, :]
        out_ref[:, rows, :] = acc.astype(BF).reshape(comps, head_chan, BS)


def mix_call(part, lists, place, v, p, scale, halo, prev, heads, head_dim):
    comps, chans, atoms = v.shape
    blocks = atoms // BS
    half = blocks // 2 - REACH
    steps = REACH if halo else half
    skip = {"low": 0, "high": half, "far": 0, "near": REACH}[part]

    def at(i, lists, place):
        if part in ("low", "high"):
            return i + REACH + skip
        return edge_block(i + skip, place, blocks)

    whole = lambda shape: pl.BlockSpec(shape, lambda g, *_: (0,) * len(shape), pipeline_mode=pl.Buffered(1))
    extra = list(halo) + ([] if prev is None else [prev])
    return pl.pallas_call(
        functools.partial(mix_kernel, heads, head_dim, chans // heads, blocks, part, skip),
        grid_spec=pltpu.PrefetchScalarGridSpec(
            num_scalar_prefetch=2,
            grid=(steps,),
            in_specs=[
                whole(v.shape),
                whole(p.shape),
                whole(scale.shape),
            ]
            + [whole(x.shape) for x in halo]
            + ([] if prev is None else [pl.BlockSpec(memory_space=pl.ANY)]),
            out_specs=pl.BlockSpec((comps, chans, BS), lambda i, *s: (0, 0, at(i, *s))),
            scratch_shapes=[pltpu.VMEM((3 * REACH, comps, chans, BS), BF)] if halo else [],
        ),
        out_shape=jax.ShapeDtypeStruct(v.shape, BF),
        input_output_aliases={} if prev is None else {4 + len(extra): 0},
        compiler_params=params(16),
        cost_estimate=pl.CostEstimate(
            flops=steps * chans * comps * NNB * BS * BS * 2, transcendentals=0,
            bytes_accessed=steps * chans * comps * BS * 8,
        ),
    )(lists, place, v, p, scale, *extra)


def own_kernel(heads, head_chan, blocks, lists, place, v_ref, p_ref, sum_ref):
    comps = v_ref.shape[0]
    for i in range(REACH):
        g = edge_block(i + REACH, place, blocks)
        for h in range(heads):
            rows = slice(h * head_chan, (h + 1) * head_chan)
            acc = 0.0
            for e in range(NNB):
                b = lists[e, g] - place[0] * blocks
                own = jnp.where((b >= 0) & (b < blocks), 1.0, 0.0)
                cols = pl.ds(pl.multiple_of(jnp.clip(b, 0, blocks - 1) * BS, BS), BS)
                v = v_ref[:, rows, cols].reshape(comps * head_chan, BS)
                acc = acc + own * dot(v, p_ref[i + REACH, h, e * BS : (e + 1) * BS, :], ((1,), (0,)))
            sum_ref[i, h] = acc


def own_call(lists, place, v, p, heads):
    comps, chans, atoms = v.shape
    blocks = atoms // BS
    whole = lambda shape: pl.BlockSpec(shape, lambda g, *_: (0,) * len(shape), pipeline_mode=pl.Buffered(1))
    shape = (REACH, heads, comps * chans // heads, BS)
    return pl.pallas_call(
        functools.partial(own_kernel, heads, chans // heads, blocks),
        grid_spec=pltpu.PrefetchScalarGridSpec(
            num_scalar_prefetch=2,
            grid=(1,),
            in_specs=[whole(v.shape), whole(p.shape)],
            out_specs=whole(shape),
        ),
        out_shape=jax.ShapeDtypeStruct(shape, F32),
        compiler_params=params(16),
        cost_estimate=pl.CostEstimate(
            flops=REACH * chans * comps * NNB * BS * BS * 2, transcendentals=0,
            bytes_accessed=REACH * chans * comps * BS * 8,
        ),
        name="near_own",
    )(lists, place, v, p)


def near_kernel(heads, head_dim, head_chan, blocks, lists, place, sum_ref, p_ref, scale_ref, small, big, prev, out_ref, acc):
    i = pl.program_id(0)
    g = edge_block(i + REACH, place, blocks)
    comps = big.shape[0] + 1
    for h in range(heads):
        rows = slice(h * head_chan, (h + 1) * head_chan)
        first = heads * head_dim + h * head_chan
        acc[h] = sum_ref[i, h]
        for e in range(NNB):
            b = lists[e, g] - place[0] * blocks

            @pl.when((b < 0) | (b >= blocks))
            def _():
                at = jnp.clip(jnp.where(b < 0, b + REACH, b - blocks), 0, REACH - 1)
                cols = pl.ds(pl.multiple_of(at * BS, BS), BS)
                v = jnp.concatenate([small[first : first + head_chan, cols][None], big[:, rows, cols]], axis=0)
                v = v.reshape(comps * head_chan, BS)
                acc[h] += dot(v, p_ref[i + REACH, h, e * BS : (e + 1) * BS, :], ((1,), (0,)))

    for h in range(heads):
        rows = slice(h * head_chan, (h + 1) * head_chan)
        total = acc[h] * scale_ref[i + REACH, h : h + 1, :]
        out_ref[:, rows, :] = total.astype(BF).reshape(comps, head_chan, BS)


def near_call(lists, place, v_shape, sums, p, scale, halo, prev, heads, head_dim):
    comps, chans, atoms = v_shape
    blocks = atoms // BS
    whole = lambda shape: pl.BlockSpec(shape, lambda g, *_: (0,) * len(shape), pipeline_mode=pl.Buffered(1))
    return pl.pallas_call(
        functools.partial(near_kernel, heads, head_dim, chans // heads, blocks),
        grid_spec=pltpu.PrefetchScalarGridSpec(
            num_scalar_prefetch=2,
            grid=(REACH,),
            in_specs=[whole(x.shape) for x in (sums, p, scale, *halo)] + [pl.BlockSpec(memory_space=pl.ANY)],
            out_specs=pl.BlockSpec(
                (comps, chans, BS), lambda i, lists, place: (0, 0, edge_block(i + REACH, place, blocks))
            ),
            scratch_shapes=[pltpu.VMEM(sums.shape[1:], F32)],
        ),
        out_shape=jax.ShapeDtypeStruct(v_shape, BF),
        input_output_aliases={7: 0},
        compiler_params=params(16),
        cost_estimate=pl.CostEstimate(
            flops=REACH * chans * comps * NNB * BS * BS, transcendentals=0,
            bytes_accessed=REACH * chans * comps * BS * 8,
        ),
        name="mix_near",
    )(lists, place, sums, p, scale, *halo, prev)


SPREAD = 2 * KMAX + 1
WIDE = 16


def wave(turns):
    r = turns - jnp.round(turns)
    u = r * r
    return horner(COS, u), horner(SIN, u) * r


def grid_points(base, planes):
    rows = planes * SPREAD * WIDE
    place = lax.broadcasted_iota(jnp.int32, (1, rows), 1).astype(F32)
    pair = jnp.floor((place + 0.5) * (1.0 / WIDE))
    n3 = place - pair * WIDE - KMAX
    plane = jnp.floor((pair + 0.5) * (1.0 / SPREAD))
    return plane + base.astype(F32), pair - plane * SPREAD - KMAX, n3


def grid_weights(n, base, planes):
    pairs = planes * SPREAD
    high = -(-pairs // 16) * 16
    flip = jnp.where(n[0:1] < 0, -1, 1)
    pair = (n[0:1] * flip - base) * SPREAD + n[1:2] * flip + KMAX
    mine = (n[0:1] * flip >= base) & (n[0:1] * flip < base + planes)
    third = n[2:3] * flip + KMAX
    count = n.shape[1]
    is_pair = (lax.broadcasted_iota(jnp.int32, (high, count), 0) == pair) & mine
    is_third = lax.broadcasted_iota(jnp.int32, (WIDE, count), 0) == third
    one_hot = lambda x: jnp.where(x, 1.0, 0.0).astype(BF)
    found = dot(one_hot(is_pair), one_hot(is_third), ((1,), (1,)))
    rows = pairs * WIDE
    row = lax.broadcasted_iota(jnp.int32, (WIDE, rows), 0)
    spread = one_hot((lax.broadcasted_iota(jnp.int32, (WIDE, rows), 1) & (WIDE - 1)) == row)
    wide = sum(dot(part, spread, ((1,), (0,))) for part in thirds(found))
    own = lax.broadcasted_iota(jnp.int32, (high, rows), 1) >> (WIDE.bit_length() - 1)
    times = jnp.sum(jnp.where(own == lax.broadcasted_iota(jnp.int32, (high, rows), 0), wide, 0.0), axis=0, keepdims=True)
    n1, n2, n3 = grid_points(base, planes)
    norm = n1 * n1 + n2 * n2 + n3 * n3
    safe = jnp.maximum(norm, 1.0)
    return jnp.where(norm > 0, times * (ewald_scale * jnp.exp(-ewald_damp * safe) / safe), 0.0)


def table_kernel(planes, step, place, n_ref, f_ref, out_ref, weight_ref, pairs):
    base = place[1] * planes
    weight_ref[...] = grid_weights(n_ref[...], base, planes)
    steps = (lax.broadcasted_iota(jnp.int32, (WIDE, step), 0) - KMAX).astype(F32)
    for start in range(0, f_ref.shape[1], step):
        cols = slice(start, start + step)
        second = wave(steps * f_ref[1:2, cols])
        third = wave(steps * f_ref[2:3, cols])
        for plane in range(planes):
            first = wave((base + plane).astype(F32) * f_ref[0:1, cols])
            pairs[0, plane] = first[0] * second[0] - first[1] * second[1]
            pairs[1, plane] = first[1] * second[0] + first[0] * second[1]
            for m in range(SPREAD):
                real, imag = pairs[0, plane, m : m + 1, :], pairs[1, plane, m : m + 1, :]
                at = slice((plane * SPREAD + m) * WIDE, (plane * SPREAD + m + 1) * WIDE)
                out_ref[0, at, cols] = (real * third[0] - imag * third[1]).astype(BF)
                out_ref[1, at, cols] = (imag * third[0] + real * third[1]).astype(BF)


def table_call(place, n, f, planes):
    rows = planes * SPREAD * WIDE
    atoms = f.shape[1]
    step = 256
    whole = lambda shape: pl.BlockSpec(shape, lambda g, *_: (0,) * len(shape), pipeline_mode=pl.Buffered(1))
    return pl.pallas_call(
        functools.partial(table_kernel, planes, step),
        grid_spec=pltpu.PrefetchScalarGridSpec(
            num_scalar_prefetch=1,
            grid=(1,),
            in_specs=[whole(n.shape), whole(f.shape)],
            out_specs=[whole((2, rows, atoms)), whole((1, rows))],
            scratch_shapes=[pltpu.VMEM((2, planes, WIDE, step), F32)],
        ),
        out_shape=[jax.ShapeDtypeStruct((2, rows, atoms), BF), jax.ShapeDtypeStruct((1, rows), F32)],
        compiler_params=params(12),
        cost_estimate=pl.CostEstimate(flops=rows * atoms * 40, transcendentals=0, bytes_accessed=rows * atoms * 4),
        name="table",
    )(place, n, f)


def structure_kernel(inv_root, c_ref, t_ref, out_ref):
    high, low = halves(c_ref[...])
    both = jnp.concatenate([high, low], axis=0)
    s = dot(t_ref[...], both, ((1,), (1,)))
    nq = c_ref.shape[0]
    out_ref[...] = (s[:, :nq] + s[:, nq:]).T * inv_root


def structure_call(c, table, inv_root):
    rows, atoms = table.shape
    step = rows
    nq = c.shape[0]
    return pl.pallas_call(
        functools.partial(structure_kernel, inv_root),
        grid=(rows // step,),
        in_specs=[pl.BlockSpec((nq, atoms), lambda i: (0, 0)), pl.BlockSpec((step, atoms), lambda i: (i, 0))],
        out_specs=pl.BlockSpec((nq, step), lambda i: (0, i)),
        out_shape=jax.ShapeDtypeStruct((nq, rows), F32),
        compiler_params=params(12),
        cost_estimate=pl.CostEstimate(flops=rows * atoms * 512, transcendentals=0, bytes_accessed=rows * atoms * 2),
        name="structure",
    )(c, table)


def field_kernel(planes, step, place, s_ref, weight_ref, c_ref, t_ref, out_ref):
    nq = c_ref.shape[0]
    waves = weight_ref.shape[1]
    n = grid_points(place[1] * planes, planes)
    real = s_ref[:, :waves] * weight_ref[...]
    imag = s_ref[:, waves:] * weight_ref[...]
    with_cos = jnp.concatenate([real] + [-imag * n[d] for d in range(3)], axis=0)
    with_sin = jnp.concatenate([imag] + [real * n[d] for d in range(3)], axis=0)
    with_cos, with_sin = [jnp.concatenate(halves(x), axis=0) for x in (with_cos, with_sin)]
    for start in range(0, c_ref.shape[1], step):
        cols = slice(start, start + step)
        both = dot(with_cos, t_ref[0, :, cols], ((1,), (0,))) + dot(with_sin, t_ref[1, :, cols], ((1,), (0,)))
        sums = both[: 4 * nq] + both[4 * nq :]
        c = c_ref[:, cols]
        out_ref[0:nq, cols] = sums[:nq]
        forces = [
            jnp.sum(c * sums[(d + 1) * nq : (d + 2) * nq], axis=0, keepdims=True) for d in range(3)
        ]
        out_ref[nq : nq + 8, cols] = jnp.concatenate(forces + [jnp.zeros((5, step), F32)], axis=0)


def field_call(place, s, weight, c, table, planes):
    _, rows, atoms = table.shape
    nq = c.shape[0]
    whole = lambda shape: pl.BlockSpec(shape, lambda g, *_: (0,) * len(shape), pipeline_mode=pl.Buffered(1))
    return pl.pallas_call(
        functools.partial(field_kernel, planes, 512),
        grid_spec=pltpu.PrefetchScalarGridSpec(
            num_scalar_prefetch=1,
            grid=(1,),
            in_specs=[whole(x.shape) for x in (s, weight, c, table)],
            out_specs=whole((nq + 8, atoms)),
        ),
        out_shape=jax.ShapeDtypeStruct((nq + 8, atoms), F32),
        compiler_params=params(12),
        cost_estimate=pl.CostEstimate(flops=rows * atoms * 512, transcendentals=0, bytes_accessed=rows * atoms * 2),
        name="fields",
    )(place, s, weight, c, table)


def finish_kernel(mine_ref, theirs_ref, potential_ref, force_ref):
    nq = potential_ref.shape[0]
    total = mine_ref[...].astype(F32) + theirs_ref[...].astype(F32)
    potential_ref[...] = total[:nq]
    force_ref[...] = total[nq : nq + 3]


def finish_call(mine, theirs, nq):
    atoms = mine.shape[1]
    return pl.pallas_call(
        finish_kernel,
        out_shape=[jax.ShapeDtypeStruct((nq, atoms), F32), jax.ShapeDtypeStruct((3, atoms), F32)],
        compiler_params=pltpu.CompilerParams(vmem_limit_bytes=4 << 20),
        name="finish",
    )(mine, theirs)


def exchanged(x, axis, step):
    size = lax.axis_size(axis)
    if step >= size:
        return x
    return x + lax.ppermute(x, axis, [(i, i ^ step) for i in range(size)])


def summed(x, axis, step=1, stop=None):
    size = lax.axis_size(axis)
    assert size & (size - 1) == 0
    while step < (stop or size):
        x = exchanged(x, axis, step)
        step *= 2
    return x


def whole_step(
    queries,
    key_states,
    value_states,
    fractional,
    block_counts,
    neighbors,
    integer_wave_vectors,
    charge_weight,
):
    heads, head_dim, atoms = queries.shape
    nq = charge_weight.shape[1]
    planes = (KMAX + 1) // lax.axis_size("inner")
    assert planes * lax.axis_size("inner") == KMAX + 1
    inv_root = 1.0 / math.sqrt(atoms * lax.axis_size("seq"))
    place = jnp.stack([lax.axis_index("seq"), lax.axis_index("inner")]).astype(jnp.int32)
    width = REACH * BS
    count = lax.axis_size("seq")
    near_pairs = [(i, i ^ 1) for i in range(count)]
    far_pairs = [(i, i + 1 if i % 2 else i - 1) for i in range(1, count - 1)]

    def swap(x, pairs):
        return lax.ppermute(x, "seq", pairs)

    values = value_states.transpose(1, 0, 2)
    keys = key_states.reshape(heads * head_dim, atoms)
    asked = queries.reshape(heads * head_dim, atoms)
    near, far, far_big, v0, keys, asked, weight, counts, lists = load_call(
        place, keys, values, (asked, charge_weight.T, block_counts, neighbors.T), width
    )
    vectors = integer_wave_vectors
    far = swap(far, far_pairs)
    near = swap(near, near_pairs)
    far_big = swap(far_big, far_pairs)

    p_in, scale_in, part = scores_call(
        "interior", lists, counts, place, asked, keys, v0, weight, (), heads, head_dim
    )
    near_big = swap(cut_call(place, values, width), near_pairs)
    p_out, scale_out, part = scores_call(
        "edges", lists, counts, place, asked, keys, v0, weight, (far, near, part), heads, head_dim
    )
    table, wave_weight = table_call(place, vectors, fractional, planes)
    last = lax.axis_size("inner") // 2

    def halfway(x):
        x = summed(x, "inner", stop=last)
        low = x.astype(BF)
        return x, low, lax.ppermute(low, "inner", [(i, i ^ last) for i in range(2 * last)])

    mine, _, theirs = halfway(part)
    charges = mine + theirs.astype(F32)
    structure = structure_call(charges, table.reshape(-1, atoms), inv_root)
    structure = structure + lax.ppermute(structure.astype(BF), "seq", near_pairs).astype(F32)
    structure = summed(structure, "seq", 2)
    fields = field_call(place, structure, wave_weight, charges, table, planes)
    _, fields, others = halfway(fields)
    potential, forces = finish_call(fields, others, nq)

    mix = functools.partial(mix_call, heads=heads, head_dim=head_dim)
    attention = mix("low", lists, place, values, p_in, scale_in, (), None)
    attention = mix("far", lists, place, values, p_out, scale_out, (far, far_big), attention)
    attention = mix("high", lists, place, values, p_in, scale_in, (), attention)
    sums = own_call(lists, place, values, p_out, heads)
    attention = near_call(
        lists, place, values.shape, sums, p_out, scale_out, (near, near_big), attention, heads, head_dim
    )
    return (attention.transpose(1, 0, 2), potential, forces)


def solution(mesh):
    placed = (
        P("inner", None, "seq"),
        P("inner", None, "seq"),
        P("inner", None, "seq"),
        P(None, "seq"),
        P(),
        P("seq", None),
        P(),
        P("inner", None),
    )
    return jax.shard_map(
        whole_step,
        mesh=mesh,
        in_specs=placed,
        out_specs=(P("inner", None, "seq"), P(None, "seq"), P(None, "seq")),
        check_vma=False,
    )
```
